32 devices in a mesh: lat: 8 (over y, x, core), lon: 4 (over z).
Axes of the slice: x: 2, y: 2, z: 4, core: 2. Of those that a mesh axis runs over, the one named last changes fastest.
Arguments:
- ocean_state: bfloat16 [1, 96, 640, 768], P(None, 'lat', None, 'lon'), may hold values from -6 to 6
- zonal_kernel: bfloat16 [2, 5, 256, 640], replicated, may hold values from -0.15625 to 0.15625
- norm_gain: bfloat16 [2, 640], replicated, may hold values from 0.099609375 to 1.8984375
- input_weight: bfloat16 [2, 640, 1280], replicated, may hold values from -0.25 to 0.25
- output_weight: bfloat16 [2, 1280, 640], replicated, may hold values from -0.15625 to 0.15625
Outputs:
- state_out: bfloat16 [1, 96, 640, 768], P(None, 'lat', None, 'lon')
The draws below stay inside these ranges and needn't reach their ends.
All inputs are finite; a program needn't handle non-finite values.
Results may differ from the reference program's by a relative error of at most 0.009.
Values may be sent and summed in bfloat16 or wider, within the bound.
No kernel may reach another device: no remote copies, remote signals or barrier semaphores. Data moves between devices by JAX's collectives and lax.ppermute only.
A program may use at most 128 MiB of HBM per device.

```python
import math
import jax
import jax.numpy as jnp
from jax import lax

C = 640
FF = 1280
W = 768
TAPS = 256
KROWS = 5
BLOCKS = 2
BATCH = 1
H = 96


def levels(stream_key, extent, pieces, low, largest):
    factor_of = 1.0
    for axis_at, parts in pieces:
        steps = jax.random.uniform(jax.random.fold_in(jax.random.fold_in(stream_key, 6), axis_at), (parts,), jnp.float32, low / len(pieces), largest / len(pieces))
        factor_of = factor_of * jnp.repeat(jnp.exp(steps), extent[axis_at] // parts).reshape((-1,) + (1,) * (len(extent) - 1 - axis_at))
    return factor_of


def gaussian(own_key, shape, spread, most, cuts=(), kind=jnp.bfloat16):
    result = spread * jax.random.normal(own_key, shape, jnp.float32)
    if cuts:
        result = result * levels(own_key, shape, cuts, -0.22, 0.18)
    return jnp.clip(result, -most, most).astype(kind)


def setup_inputs(seed: int = 0) -> dict:
    seeds = jax.random.split(jax.random.key(seed), 6)
    ocean_state = gaussian(seeds[0], (BATCH, H, C, W), 1.0, 6.0, ((1, 8), (3, 4)))
    zonal_kernel = gaussian(seeds[1], (BLOCKS, KROWS, TAPS, C), (KROWS * TAPS) ** -0.5, 0.15625)
    norm_gain = jnp.clip(1.0 + 0.18 * jax.random.normal(seeds[2], (BLOCKS, C), jnp.float32), 0.099609375, 1.8984375).astype(jnp.bfloat16)
    input_weight = gaussian(seeds[3], (BLOCKS, C, FF), C ** -0.5, 0.25)
    output_weight = gaussian(seeds[4], (BLOCKS, FF, C), FF ** -0.5, 0.15625)
    return dict(ocean_state=ocean_state, zonal_kernel=zonal_kernel, norm_gain=norm_gain, input_weight=input_weight, output_weight=output_weight)


def latitude_weights(row_start, row_count, total_rows):
    row_index = row_start + jnp.arange(row_count, dtype=jnp.int32)
    return jnp.sin(jnp.pi * (row_index.astype(jnp.float32) + 0.5) / total_rows)

def zonal_mix(current, kernel_layer):
    weights = latitude_weights(0, H, H)
    group_size = math.gcd(C, 64)
    group_count = C // group_size
    weighted = current.astype(jnp.float32) * weights[None, :, None, None]
    weighted = weighted.reshape(BATCH, H, group_count, group_size, W).transpose(2, 0, 1, 3, 4)
    tap_values = kernel_layer.astype(jnp.float32).reshape(KROWS, TAPS, group_count, group_size).transpose(2, 0, 3, 1)
    rim_rows = KROWS // 2

    def per_group(group_pair):
        signal_rows, filters = group_pair
        filters = jnp.pad(filters, ((0, 0), (0, 0), (0, W - TAPS)))
        filters = jnp.roll(filters, -(TAPS // 2), axis=2)
        spectra = jnp.fft.rfft(filters, axis=2)
        signal = jnp.fft.rfft(signal_rows, axis=3)
        padded = jnp.pad(signal, ((0, 0), (rim_rows, rim_rows), (0, 0), (0, 0)))
        summed = padded[:, 0:H] * spectra[0]
        for offset in range(1, KROWS):
            summed = summed + padded[:, offset:offset + H] * spectra[offset]
        return jnp.fft.irfft(summed, n=W, axis=3)
    mapped = lax.map(per_group, (weighted, tap_values))
    return mapped.transpose(1, 2, 0, 3, 4).reshape(BATCH, H, C, W)

def feed_forward(mixed_in, gain_layer, input_layer, output_layer):
    gain_values = gain_layer.astype(jnp.float32)
    lifting = input_layer.astype(jnp.float32)
    lowered = output_layer.astype(jnp.float32)

    def per_row(lat_slab):
        values = lat_slab.astype(jnp.float32)
        average = lax.optimization_barrier(jnp.mean(values, axis=1, keepdims=True))
        variance = lax.optimization_barrier(jnp.mean(jnp.square(values - average), axis=1, keepdims=True))
        normed = ((values - average) * lax.rsqrt(variance + 1e-05) * gain_values[None, :, None]).astype(jnp.bfloat16)
        hidden = jnp.einsum('bcw,cf->bwf', normed.astype(jnp.float32), lifting)
        hidden = jax.nn.gelu(hidden, approximate=False).astype(jnp.bfloat16)
        projected = jnp.einsum('bwf,fc->bcw', hidden.astype(jnp.float32), lowered)
        return (values + projected).astype(jnp.bfloat16)
    rows_first = mixed_in.transpose(1, 0, 2, 3)
    return lax.map(per_row, rows_first).transpose(1, 0, 2, 3)

def reference(ocean_state, zonal_kernel, norm_gain, input_weight, output_weight):
    current = ocean_state
    for layer_index in range(BLOCKS):
        convolved = zonal_mix(current, zonal_kernel[layer_index])
        mixed_out = (current.astype(jnp.float32) + jax.nn.gelu(convolved, approximate=False)).astype(jnp.bfloat16)
        current = feed_forward(mixed_out, norm_gain[layer_index], input_weight[layer_index], output_weight[layer_index])
    return current
```

```python
import functools
import math

import jax
import jax.numpy as jnp
import numpy as np
from jax import lax
from jax.experimental import pallas as pl
from jax.experimental.pallas import tpu as pltpu
from jax.sharding import PartitionSpec as P

LANES = 128


def round_up(value, step):
    return -(-value // step) * step


def plan(width, taps):
    half = taps // 2
    padded = round_up(width, LANES)
    length = round_up(width + taps, 2 * LANES)
    return half, padded, length


def bases(width, taps):
    half, padded, length = plan(width, taps)
    places = np.full(2 * half + padded, -1)
    places[:half] = np.arange(half)
    places[half : half + width] = half + np.arange(width)
    places[half + padded :] = half + width + np.arange(half)
    odd = 2 * np.arange(length // 2) + 1

    def wave(points):
        angle = np.pi / length * (points[:, None] * odd[None, :] % (2 * length))
        return np.concatenate([np.cos(angle), -np.sin(angle)], axis=1)

    forward = np.where(places[:, None] >= 0, wave(places), 0.0)
    inverse = 2.0 / length * wave(2 * half + np.arange(width)).T
    tap_basis = wave(np.arange(taps))
    return tuple(jnp.asarray(a, jnp.bfloat16) for a in (forward, inverse, tap_basis))


def gelu(values):
    return 0.5 * values * (1.0 + lax.erf(values * math.sqrt(0.5)))


def conv_kernel(
    quad, left, mid, right, low, high, factors, forward, inverse, out, ext, spectra, mixed, *, half, padded, rim
):
    rows, channels, width = mid.shape
    freqs = forward.shape[1] // 2
    every = rows + 2 * rim
    taps_r = 2 * rim + 1
    inner = slice(rim, rim + rows)
    ext[:rim] = low[...]
    ext[rim + rows :] = high[...]
    ext[inner, :, :half] = left[...]
    ext[inner, :, half : half + width] = mid[...]
    if padded > width:
        ext[inner, :, half + width : half + padded] = jnp.zeros((rows, channels, padded - width), ext.dtype)
    ext[inner, :, half + padded :] = right[...]
    group = 8 if every % 8 == 0 else 1
    for g in range(0, every, group):
        flat = ext[g : g + group].reshape(group * channels, ext.shape[2])
        result = jnp.dot(flat, forward[...], preferred_element_type=jnp.float32)
        for j in range(group):
            spectra[g + j] = result[j * channels : (j + 1) * channels] * quad[g + j]

    def block(c, carry):
        c = pl.ds(pl.multiple_of(c * 16, 16), 16)
        for f in range(0, freqs, LANES):
            re = slice(f, f + LANES)
            im = slice(freqs + f, freqs + f + LANES)
            fr = [factors[r, c, re] for r in range(taps_r)]
            fi = [factors[r, c, im] for r in range(taps_r)]
            xr = [spectra[g, c, re] for g in range(taps_r - 1)]
            xi = [spectra[g, c, im] for g in range(taps_r - 1)]
            for h in range(rows):
                xr.append(spectra[h + taps_r - 1, c, re])
                xi.append(spectra[h + taps_r - 1, c, im])
                yr = xr[0] * fr[0] - xi[0] * fi[0]
                yi = xr[0] * fi[0] + xi[0] * fr[0]
                for r in range(1, taps_r):
                    yr = yr + (xr[r] * fr[r] - xi[r] * fi[r])
                    yi = yi + (xr[r] * fi[r] + xi[r] * fr[r])
                mixed[h, c, re] = yr.astype(mixed.dtype)
                mixed[h, c, im] = yi.astype(mixed.dtype)
                xr.pop(0)
                xi.pop(0)
        return carry

    lax.fori_loop(0, channels // 16, block, 0)
    group = 4 if rows % 4 == 0 else 1
    for h in range(0, rows, group):
        flat = mixed[h : h + group].reshape(group * channels, mixed.shape[2])
        conv = jnp.dot(flat, inverse[...], preferred_element_type=jnp.float32)
        conv = conv.reshape(group, channels, width)
        out[h : h + group] = (mid[h : h + group].astype(jnp.float32) + gelu(conv)).astype(out.dtype)


def convolve(quad, left, mid, right, low, high, factors, forward, inverse, half, padded, rim):
    rows, channels, width = mid.shape
    every = rows + 2 * rim
    block = math.gcd(channels, 64)
    length = forward.shape[1]
    wide = forward.shape[0]

    def rows_of(count, last):
        return pl.BlockSpec((count, block, last), lambda i: (0, i, 0))

    def whole(array):
        return pl.BlockSpec(array.shape, lambda i: (0,) * array.ndim)

    kernel = functools.partial(conv_kernel, half=half, padded=padded, rim=rim)
    return pl.pallas_call(
        kernel,
        grid=(channels // block,),
        out_shape=jax.ShapeDtypeStruct(mid.shape, jnp.bfloat16),
        in_specs=[
            pl.BlockSpec(memory_space=pltpu.SMEM),
            rows_of(rows, half),
            rows_of(rows, width),
            rows_of(rows, half),
            rows_of(rim, wide),
            rows_of(rim, wide),
            rows_of(factors.shape[0], length),
            whole(forward),
            whole(inverse),
        ],
        out_specs=rows_of(rows, width),
        scratch_shapes=[
            pltpu.VMEM((every, block, wide), jnp.bfloat16),
            pltpu.VMEM((every, block, length), jnp.float32),
            pltpu.VMEM((rows, block, length), jnp.bfloat16),
        ],
        compiler_params=pltpu.CompilerParams(vmem_limit_bytes=56 << 20),
        cost_estimate=pl.CostEstimate(
            flops=2 * channels * length * (every * wide + rows * width),
            bytes_accessed=4 * channels * (every * wide + factors.shape[0] * length),
            transcendentals=rows * channels * width,
        ),
        name="zonal_conv",
    )(quad, left, mid, right, low, high, factors, forward, inverse)


def mlp_kernel(gain, w_in, w_out, mixed, out, *edges, half):
    values = mixed[0].astype(jnp.float32)
    average = jnp.mean(values, axis=0, keepdims=True)
    centred = values - average
    variance = jnp.mean(jnp.square(centred), axis=0, keepdims=True)
    normed = (centred * lax.rsqrt(variance + 1e-05) * gain[...]).astype(jnp.bfloat16)
    total = values
    hidden_units = w_in.shape[0]
    step = math.gcd(hidden_units, 256)
    for f in range(0, hidden_units, step):
        hidden = jnp.dot(w_in[f : f + step], normed, preferred_element_type=jnp.float32)
        hidden = gelu(hidden).astype(jnp.bfloat16)
        total = total + jnp.dot(w_out[:, f : f + step], hidden, preferred_element_type=jnp.float32)
    result = total.astype(jnp.bfloat16)
    out[0] = result
    if edges:
        edges[0][0] = result[:, :half]
        edges[1][0] = result[:, result.shape[1] - half :]


def mlp(gain, w_in, w_out, mixed, edge):
    rows, channels, width = mixed.shape
    hidden_units = w_in.shape[0]

    def whole(array):
        return pl.BlockSpec(array.shape, lambda i: (0,) * array.ndim)

    def row(last):
        return pl.BlockSpec((1, channels, last), lambda i: (i, 0, 0))

    lasts = [width] + ([edge, edge] if edge else [])
    return pl.pallas_call(
        functools.partial(mlp_kernel, half=edge),
        grid=(rows,),
        out_shape=[jax.ShapeDtypeStruct((rows, channels, last), jnp.bfloat16) for last in lasts],
        in_specs=[whole(gain), whole(w_in), whole(w_out), row(width)],
        out_specs=[row(last) for last in lasts],
        compiler_params=pltpu.CompilerParams(vmem_limit_bytes=56 << 20),
        cost_estimate=pl.CostEstimate(
            flops=4 * rows * width * channels * hidden_units,
            bytes_accessed=4 * rows * width * channels,
            transcendentals=rows * width * hidden_units,
        ),
        name="channel_mlp",
    )(gain, w_in, w_out, mixed)


def rotate(block, axis, hops):
    count = lax.axis_size(axis)
    return lax.ppermute(block, axis, [(i, (i + hops) % count) for i in range(count)])


def zonal_halos(first, last, width, half):
    if half <= width:
        return rotate(last, "lon", 1), rotate(first, "lon", -1)
    lefts, rights, hops, missing = [], [], 1, half
    while missing > 0:
        take = min(width, missing)
        lefts.insert(0, rotate(last[..., last.shape[2] - take :], "lon", hops))
        rights.append(rotate(first[..., :take], "lon", -hops))
        missing -= take
        hops += 1
    return jnp.concatenate(lefts, axis=2), jnp.concatenate(rights, axis=2)


def step_rows(block, hops):
    count = lax.axis_size("lat")
    pairs = [(i, i + hops) for i in range(count) if 0 <= i + hops < count]
    return lax.ppermute(block, "lat", pairs)


def body(ocean_state, zonal_kernel, norm_gain, input_weight, output_weight):
    blocks, kernel_rows, taps, channels = zonal_kernel.shape
    _, rows, _, width = ocean_state.shape
    rim = kernel_rows // 2
    half, padded, length = plan(width, taps)
    edge = min(half, width)
    forward, inverse, tap_basis = bases(width, taps)
    total_rows = rows * lax.axis_size("lat")
    index = lax.axis_index("lat") * rows - rim + jnp.arange(rows + 2 * rim, dtype=jnp.int32)
    quad = jnp.sin(jnp.pi * (index.astype(jnp.float32) + 0.5) / total_rows)
    quad = jnp.where((index >= 0) & (index < total_rows), quad, 0.0)
    factors = jnp.einsum("lrtc,tk->lrck", zonal_kernel, tap_basis, preferred_element_type=jnp.float32)
    w_in = jnp.swapaxes(input_weight, 1, 2)
    w_out = jnp.swapaxes(output_weight, 1, 2)
    gains = norm_gain.astype(jnp.float32)[:, :, None]

    current = ocean_state[0]
    first, last = current[..., :edge], current[..., width - edge :]
    for layer in range(blocks):
        left, right = zonal_halos(first, last, width, half)

        def extended(rows_slice):
            pieces = [left[rows_slice], current[rows_slice]]
            if padded > width:
                pieces.append(jnp.zeros((rim, channels, padded - width), current.dtype))
            return jnp.concatenate(pieces + [right[rows_slice]], axis=2)

        low = step_rows(extended(slice(rows - rim, rows)), 1)
        high = step_rows(extended(slice(0, rim)), -1)
        mixed = convolve(
            quad, left, current, right, low, high, factors[layer], forward, inverse, half, padded, rim
        )
        outs = mlp(gains[layer], w_in[layer], w_out[layer], mixed, edge if layer + 1 < blocks else 0)
        current = outs[0]
        if layer + 1 < blocks:
            first, last = outs[1], outs[2]
    return current[None]


def solution(mesh):
    in_specs = (P(None, "lat", None, "lon"), P(), P(), P(), P())
    out_specs = P(None, "lat", None, "lon")
    return jax.shard_map(body, mesh=mesh, in_specs=in_specs, out_specs=out_specs, check_vma=False)
```

```python
import functools
import math

import jax
import jax.numpy as jnp
import numpy as np
from jax import lax
from jax.experimental import pallas as pl
from jax.experimental.pallas import tpu as pltpu
from jax.sharding import PartitionSpec as P

LANES = 128
PACK = 16


def bases(width, taps):
    length = -(-(width + taps) // (2 * PACK)) * 2 * PACK
    odd = 2 * np.arange(length // 2) + 1

    def wave(points):
        angle = np.pi / length * (points[:, None] * odd[None, :] % (2 * length))
        return np.concatenate([np.cos(angle), -np.sin(angle)], axis=1)

    forward = wave(np.arange(width + taps)).T
    inverse = 2.0 / length * wave(taps + np.arange(width))
    tap_basis = wave(np.arange(taps)).T
    return tuple(jnp.asarray(a, jnp.bfloat16) for a in (forward, inverse, tap_basis))


def gelu(values):
    return 0.5 * values * (1.0 + lax.erf(values * math.sqrt(0.5)))


def conv_kernel(*refs, windows, row_refs, counts):
    quad, forward, inverse, factors = refs[:4]
    sources = refs[4 : 4 + counts]
    out, ext, spectra, product = refs[4 + counts :]
    lanes = out.shape[2]
    width = out.shape[1]
    freqs = forward.shape[0] // 2
    every = len(row_refs)
    taps_r = factors.shape[0]
    for g, (_, pieces) in enumerate(row_refs):
        start = 0
        for source, at in pieces:
            size = sources[source].shape[1]
            ext[start : start + size, g * lanes : (g + 1) * lanes] = sources[source][at]
            start += size
    for g in range(0, every, 2):
        two = slice(g * lanes, (g + 2) * lanes)
        result = jnp.dot(forward[...], ext[:, two], preferred_element_type=jnp.float32)
        for j in range(2):
            spectra[g + j] = result[:, j * lanes : (j + 1) * lanes] * quad[row_refs[g + j][0]]

    def block(f, carry):
        start = pl.multiple_of(f * PACK, PACK)
        re = pl.ds(start, PACK)
        im = pl.ds(pl.multiple_of(freqs + start, PACK), PACK)
        fr = [factors[r, re] for r in range(taps_r)]
        fi = [factors[r, im] for r in range(taps_r)]
        h = 0
        for first, count in windows:
            xr = [spectra[first + g, re] for g in range(taps_r - 1)]
            xi = [spectra[first + g, im] for g in range(taps_r - 1)]
            for k in range(count):
                xr.append(spectra[first + k + taps_r - 1, re])
                xi.append(spectra[first + k + taps_r - 1, im])
                yr = xr[0] * fr[0] - xi[0] * fi[0]
                yi = xr[0] * fi[0] + xi[0] * fr[0]
                for r in range(1, taps_r):
                    yr = yr + (xr[r] * fr[r] - xi[r] * fi[r])
                    yi = yi + (xr[r] * fi[r] + xi[r] * fr[r])
                here = slice(h * lanes, (h + 1) * lanes)
                product[re, here] = yr.astype(product.dtype)
                product[im, here] = yi.astype(product.dtype)
                xr.pop(0)
                xi.pop(0)
                h += 1
        return carry

    lax.fori_loop(0, freqs // PACK, block, 0)
    own = [row_refs[first + taps_r // 2 + k][1] for first, count in windows for k in range(count)]
    for h in range(0, len(own), 2):
        two = slice(h * lanes, (h + 2) * lanes)
        conv = jnp.dot(inverse[...], product[:, two], preferred_element_type=jnp.float32)
        for j in range(2):
            source, at = own[h + j][1]
            value = sources[source][at].astype(jnp.float32)
            out[h + j] = (value + gelu(conv[:, j * lanes : (j + 1) * lanes])).astype(out.dtype)


def convolve(quad, tables, factors, sources, rows, windows):
    forward, inverse = tables
    taps_r, length, channels = factors.shape
    out_rows = sum(count for _, count in windows)
    width = inverse.shape[0]

    def block(array):
        return pl.BlockSpec((array.shape[0], array.shape[1], LANES), lambda i: (0, 0, i))

    def whole(array):
        return pl.BlockSpec(array.shape, lambda i: (0,) * array.ndim)

    out = jax.ShapeDtypeStruct((out_rows, width, channels), jnp.bfloat16)
    kernel = functools.partial(conv_kernel, windows=windows, row_refs=rows, counts=len(sources))
    return pl.pallas_call(
        kernel,
        grid=(channels // LANES,),
        out_shape=out,
        in_specs=[pl.BlockSpec(memory_space=pltpu.SMEM), whole(forward), whole(inverse), block(factors)]
        + [block(a) for a in sources],
        out_specs=block(out),
        scratch_shapes=[
            pltpu.VMEM((forward.shape[1], len(rows) * LANES), jnp.bfloat16),
            pltpu.VMEM((len(rows), length, LANES), jnp.float32),
            pltpu.VMEM((length, out_rows * LANES), jnp.bfloat16),
        ],
        compiler_params=pltpu.CompilerParams(vmem_limit_bytes=48 << 20),
        cost_estimate=pl.CostEstimate(
            flops=2 * channels * length * (len(rows) * forward.shape[1] + out_rows * width),
            bytes_accessed=2 * channels * (len(rows) * forward.shape[1] + 2 * taps_r * length),
            transcendentals=out_rows * channels * width,
        ),
        name="zonal_conv",
    )(quad, forward, inverse, factors, *sources)


def mlp_kernel(gain, w_in, w_out, mixed, *refs, half, kept):
    refs = refs[kept:]
    count, width, channels = mixed.shape
    values = mixed[...].reshape(count * width, channels).astype(jnp.float32)
    average = jnp.mean(values, axis=1, keepdims=True)
    centred = values - average
    variance = jnp.mean(jnp.square(centred), axis=1, keepdims=True)
    normed = (centred * lax.rsqrt(variance + 1e-05) * gain[...]).astype(jnp.bfloat16)
    total = values
    hidden_units = w_in.shape[1]
    step = math.gcd(hidden_units, 256)
    for f in range(0, hidden_units, step):
        hidden = jnp.dot(normed, w_in[:, f : f + step], preferred_element_type=jnp.float32)
        hidden = gelu(hidden).astype(jnp.bfloat16)
        total = total + jnp.dot(hidden, w_out[f : f + step], preferred_element_type=jnp.float32)
    result = total.astype(jnp.bfloat16).reshape(count, width, channels)
    refs[0][...] = result
    if half:
        refs[1][...] = result[:, :half]
        refs[2][...] = result[:, width - half :]


def mlp(gain, w_in, w_out, mixed, places, out_rows, edge, kept=None):
    _, width, channels = mixed.shape
    hidden_units = w_in.shape[1]
    steps = len(places)

    def place(kind):
        def index(i):
            at = places[0][kind]
            for k in range(1, steps):
                at = at + (places[k][kind] - places[k - 1][kind]) * (i >= k).astype(jnp.int32)
            return (at, 0, 0)

        return index

    def whole(array):
        return pl.BlockSpec(array.shape, lambda i: (0,) * array.ndim)

    def pair(lon, kind):
        return pl.BlockSpec((2, lon, channels), place(kind))

    lasts = [width] + ([edge, edge] if edge else [])
    extra = [] if kept is None else [kept]
    return pl.pallas_call(
        functools.partial(mlp_kernel, half=edge, kept=len(extra)),
        grid=(steps,),
        out_shape=[jax.ShapeDtypeStruct((out_rows, last, channels), jnp.bfloat16) for last in lasts],
        in_specs=[whole(gain), whole(w_in), whole(w_out), pair(width, 0)]
        + [pl.BlockSpec(memory_space=pl.ANY) for _ in extra],
        out_specs=[pair(last, 1) for last in lasts],
        input_output_aliases={4: 0} if extra else {},
        compiler_params=pltpu.CompilerParams(vmem_limit_bytes=48 << 20),
        cost_estimate=pl.CostEstimate(
            flops=8 * steps * width * channels * hidden_units,
            bytes_accessed=8 * steps * width * channels + 4 * channels * hidden_units,
            transcendentals=2 * steps * width * hidden_units,
        ),
        name="channel_mlp",
    )(gain, w_in, w_out, mixed, *extra)


def rotate(block, axis, hops):
    count = lax.axis_size(axis)
    return lax.ppermute(block, axis, [(i, (i + hops) % count) for i in range(count)])


def zonal_halos(first, last, half):
    width = first.shape[1]
    if half <= width:
        return rotate(last, "lon", 1), rotate(first, "lon", -1)
    lefts, rights, hops, missing = [], [], 1, half
    while missing > 0:
        take = min(width, missing)
        lefts.insert(0, rotate(last[:, width - take :], "lon", hops))
        rights.append(rotate(first[:, :take], "lon", -hops))
        missing -= take
        hops += 1
    return jnp.concatenate(lefts, axis=1), jnp.concatenate(rights, axis=1)


def step_rows(block, hops):
    count = lax.axis_size("lat")
    pairs = [(i, i + hops) for i in range(count) if 0 <= i + hops < count]
    return lax.ppermute(block, "lat", pairs)


def body(ocean_state, zonal_kernel, norm_gain, input_weight, output_weight):
    blocks, kernel_rows, taps, channels = zonal_kernel.shape
    _, rows, _, width = ocean_state.shape
    rim = kernel_rows // 2
    half = taps // 2
    edge = min(half, width)
    forward, inverse, tap_basis = bases(width, taps)
    total_rows = rows * lax.axis_size("lat")
    index = lax.axis_index("lat") * rows - rim + jnp.arange(rows + 2 * rim, dtype=jnp.int32)
    quad = jnp.sin(jnp.pi * (index.astype(jnp.float32) + 0.5) / total_rows)
    quad = jnp.where((index >= 0) & (index < total_rows), quad, 0.0)
    factors = [
        jnp.einsum("kt,rtc->rkc", tap_basis, zonal_kernel[layer], preferred_element_type=jnp.float32)
        for layer in range(blocks)
    ]
    gains = norm_gain.astype(jnp.float32)[:, None, :]

    groups = [
        list(range(rim)) + list(range(rows - rim, rows)),
        list(range(rim, 2 * rim)) + list(range(rows - 2 * rim, rows - rim)),
        list(range(2 * rim, rows - 2 * rim)),
    ]
    group_of = {row: (k, at) for k, members in enumerate(groups) for at, row in enumerate(members)}
    state = jnp.swapaxes(ocean_state[0], 1, 2)
    mids = [state]
    mid_of = {row: (0, row) for row in range(rows)}

    def pick(members):
        low = members[: len(members) // 2]
        high = members[len(members) // 2 :]
        return jnp.concatenate([state[low[0] : low[-1] + 1], state[high[0] : high[-1] + 1]], axis=0)

    firsts = [pick(members)[:, :edge] for members in groups]
    lasts = [pick(members)[:, width - edge :] for members in groups]
    out = None
    for layer in range(blocks):
        final = layer + 1 == blocks
        halos = [zonal_halos(firsts[k], lasts[k], half) for k in range(3)]
        left = [pair[0] for pair in halos]
        right = [pair[1] for pair in halos]

        def extended(start, stop):
            at = group_of[start][1]
            source, row = mid_of[start]
            count = stop - start
            return jnp.concatenate(
                [left[0][at : at + count], mids[source][row : row + count], right[0][at : at + count]], axis=1
            )

        low = step_rows(extended(rows - rim, rows), 1)
        high = step_rows(extended(0, rim), -1)

        def own(row, used_mids, used):
            k, at = group_of[row]
            source, mid_row = mid_of[row]
            n = len(used_mids)
            j = used.index(k)
            return (row + rim, [(n + j, at), (used_mids.index(source), mid_row), (n + len(used) + j, at)])

        def lat(number, at, place):
            return (place, [(number, at)])

        used = [0, 1]
        used_mids = sorted({mid_of[row][0] for k in used for row in groups[k]})
        sources = [mids[s] for s in used_mids] + [left[k] for k in used] + [right[k] for k in used] + [low, high]
        n = len(sources)
        outer = (
            [lat(n - 2, r, r) for r in range(rim)]
            + [own(row, used_mids, used) for row in range(2 * rim)]
            + [own(row, used_mids, used) for row in range(rows - 2 * rim, rows)]
            + [lat(n - 1, r, rows + rim + r) for r in range(rim)]
        )
        windows = [(0, rim), (3 * rim, rim)]
        mixed_outer = convolve(quad, (forward, inverse), factors[layer], sources, outer, windows)
        used = [0, 1, 2]
        used_mids = sorted({source for source, _ in mid_of.values()})
        sources = [mids[s] for s in used_mids] + left + right
        inner = [own(row, used_mids, used) for row in range(rows)]
        weights = (gains[layer], input_weight[layer], output_weight[layer])
        pairs = rows // 2
        if final:
            places = [(0, 0), (1, pairs - 1)]
            (out,) = mlp(*weights, mixed_outer, places, rows, 0)
            mixed_inner = convolve(quad, (forward, inverse), factors[layer], sources, inner, [(0, rows - 2 * rim)])
            places = [(p, p + 1) for p in range(pairs - 2)]
            (out,) = mlp(*weights, mixed_inner, places, rows, 0, kept=out)
        else:
            outs = [mlp(*weights, mixed_outer, [(0, 0), (1, 1)], 2 * rim, edge)]
            mixed_inner = convolve(quad, (forward, inverse), factors[layer], sources, inner, [(0, rows - 2 * rim)])
            outs.append(mlp(*weights, mixed_inner, [(0, 0), (pairs - 3, 1)], 2 * rim, edge))
            places = [(p + 1, p) for p in range(pairs - 4)]
            outs.append(mlp(*weights, mixed_inner, places, rows - 4 * rim, edge))
            mids = [o[0] for o in outs]
            mid_of = group_of
            firsts = [o[1] for o in outs]
            lasts = [o[2] for o in outs]
    return jnp.swapaxes(out, 1, 2)[None]


def solution(mesh):
    in_specs = (P(None, "lat", None, "lon"), P(), P(), P(), P())
    out_specs = P(None, "lat", None, "lon")
    return jax.shard_map(body, mesh=mesh, in_specs=in_specs, out_specs=out_specs, check_vma=False)
```

```python
import functools
import math

import jax
import jax.numpy as jnp
import numpy as np
from jax import lax
from jax.experimental import pallas as pl
from jax.experimental.pallas import tpu as pltpu
from jax.sharding import PartitionSpec as P


LANES = 128
PACK = 16


def bases(width, taps):
    length = -(-(width + taps) // (2 * PACK)) * 2 * PACK
    odd = 2 * np.arange(length // 2) + 1

    def wave(points):
        angle = np.pi / length * (points[:, None] * odd[None, :] % (2 * length))
        return np.concatenate([np.cos(angle), -np.sin(angle)], axis=1)

    forward = wave(np.arange(width + taps)).T
    inverse = 2.0 / length * wave(taps + np.arange(width))
    tap_basis = wave(np.arange(taps)).T
    return tuple(jnp.asarray(a, jnp.bfloat16) for a in (forward, inverse, tap_basis))


def gelu(values):
    return 0.5 * values * (1.0 + lax.erf(values * math.sqrt(0.5)))


def conv_kernel(*refs, windows, row_refs, counts):
    quad, forward, inverse, factors = refs[:4]
    sources = refs[4 : 4 + counts]
    out, ext, spectra, product = refs[4 + counts :]
    lanes = out.shape[2]
    freqs = forward.shape[0] // 2
    every = len(row_refs)
    taps_r = factors.shape[0]
    for g, (_, pieces) in enumerate(row_refs):
        start = 0
        for source, at in pieces:
            size = sources[source].shape[1]
            ext[start : start + size, g * lanes : (g + 1) * lanes] = sources[source][at]
            start += size
    for g in range(0, every, 2):
        two = slice(g * lanes, (g + 2) * lanes)
        result = jnp.dot(forward[...], ext[:, two], preferred_element_type=jnp.float32)
        for j in range(2):
            spectra[g + j] = result[:, j * lanes : (j + 1) * lanes] * quad[row_refs[g + j][0]]

    def block(f, carry):
        start = pl.multiple_of(f * PACK, PACK)
        re = pl.ds(start, PACK)
        im = pl.ds(pl.multiple_of(freqs + start, PACK), PACK)
        fr = [factors[r, re] for r in range(taps_r)]
        fi = [factors[r, im] for r in range(taps_r)]
        h = 0
        for first, count in windows:
            xr = [spectra[first + g, re] for g in range(taps_r - 1)]
            xi = [spectra[first + g, im] for g in range(taps_r - 1)]
            for k in range(count):
                xr.append(spectra[first + k + taps_r - 1, re])
                xi.append(spectra[first + k + taps_r - 1, im])
                yr = xr[0] * fr[0] - xi[0] * fi[0]
                yi = xr[0] * fi[0] + xi[0] * fr[0]
                for r in range(1, taps_r):
                    yr = yr + (xr[r] * fr[r] - xi[r] * fi[r])
                    yi = yi + (xr[r] * fi[r] + xi[r] * fr[r])
                here = slice(h * lanes, (h + 1) * lanes)
                product[re, here] = yr.astype(product.dtype)
                product[im, here] = yi.astype(product.dtype)
                xr.pop(0)
                xi.pop(0)
                h += 1
        return carry

    lax.fori_loop(0, freqs // PACK, block, 0)
    own = [row_refs[first + taps_r // 2 + k][1] for first, count in windows for k in range(count)]
    for h in range(0, len(own), 2):
        two = slice(h * lanes, (h + 2) * lanes)
        conv = jnp.dot(inverse[...], product[:, two], preferred_element_type=jnp.float32)
        for j in range(2):
            source, at = own[h + j][1]
            value = sources[source][at].astype(jnp.float32)
            out[h + j] = (value + gelu(conv[:, j * lanes : (j + 1) * lanes])).astype(out.dtype)


def convolve(quad, tables, factors, sources, rows, windows):
    forward, inverse = tables
    taps_r, length, channels = factors.shape
    out_rows = sum(count for _, count in windows)
    width = inverse.shape[0]

    def block(array):
        return pl.BlockSpec((array.shape[0], array.shape[1], LANES), lambda i: (0, 0, i))

    def whole(array):
        return pl.BlockSpec(array.shape, lambda i: (0,) * array.ndim)

    out = jax.ShapeDtypeStruct((out_rows, width, channels), jnp.bfloat16)
    kernel = functools.partial(conv_kernel, windows=windows, row_refs=rows, counts=len(sources))
    return pl.pallas_call(
        kernel,
        grid=(channels // LANES,),
        out_shape=out,
        in_specs=[pl.BlockSpec(memory_space=pltpu.SMEM), whole(forward), whole(inverse), block(factors)]
        + [block(a) for a in sources],
        out_specs=block(out),
        scratch_shapes=[
            pltpu.VMEM((forward.shape[1], len(rows) * LANES), jnp.bfloat16),
            pltpu.VMEM((len(rows), length, LANES), jnp.float32),
            pltpu.VMEM((length, out_rows * LANES), jnp.bfloat16),
        ],
        compiler_params=pltpu.CompilerParams(vmem_limit_bytes=48 << 20),
        cost_estimate=pl.CostEstimate(
            flops=2 * channels * length * (len(rows) * forward.shape[1] + out_rows * width),
            bytes_accessed=2 * channels * (len(rows) * forward.shape[1] + 2 * taps_r * length),
            transcendentals=out_rows * channels * width,
        ),
        name="zonal_conv",
    )(quad, forward, inverse, factors, *sources)


def mlp_kernel(gain, w_in, w_out, mixed, *refs, half, kept):
    refs = refs[kept:]
    count, width, channels = mixed.shape
    values = mixed[...].reshape(count * width, channels).astype(jnp.float32)
    average = jnp.mean(values, axis=1, keepdims=True)
    centred = values - average
    variance = jnp.mean(jnp.square(centred), axis=1, keepdims=True)
    normed = (centred * lax.rsqrt(variance + 1e-05) * gain[...]).astype(jnp.bfloat16)
    total = values
    hidden_units = w_in.shape[1]
    step = math.gcd(hidden_units, 256)
    for f in range(0, hidden_units, step):
        hidden = jnp.dot(normed, w_in[:, f : f + step], preferred_element_type=jnp.float32)
        hidden = gelu(hidden).astype(jnp.bfloat16)
        total = total + jnp.dot(hidden, w_out[f : f + step], preferred_element_type=jnp.float32)
    result = total.astype(jnp.bfloat16).reshape(count, width, channels)
    refs[0][...] = result
    if half:
        refs[1][...] = result[:, :half]
        refs[2][...] = result[:, width - half :]


def mlp(gain, w_in, w_out, mixed, places, out_rows, edge, kept=None):
    _, width, channels = mixed.shape
    hidden_units = w_in.shape[1]
    steps = len(places)

    def place(kind):
        def index(i):
            at = places[0][kind]
            for k in range(1, steps):
                at = at + (places[k][kind] - places[k - 1][kind]) * (i >= k).astype(jnp.int32)
            return (at, 0, 0)

        return index

    def whole(array):
        return pl.BlockSpec(array.shape, lambda i: (0,) * array.ndim)

    def pair(lon, kind):
        return pl.BlockSpec((2, lon, channels), place(kind))

    lasts = [width] + ([edge, edge] if edge else [])
    extra = [] if kept is None else [kept]
    return pl.pallas_call(
        functools.partial(mlp_kernel, half=edge, kept=len(extra)),
        grid=(steps,),
        out_shape=[jax.ShapeDtypeStruct((out_rows, last, channels), jnp.bfloat16) for last in lasts],
        in_specs=[whole(gain), whole(w_in), whole(w_out), pair(width, 0)]
        + [pl.BlockSpec(memory_space=pl.ANY) for _ in extra],
        out_specs=[pair(last, 1) for last in lasts],
        input_output_aliases={4: 0} if extra else {},
        compiler_params=pltpu.CompilerParams(vmem_limit_bytes=48 << 20),
        cost_estimate=pl.CostEstimate(
            flops=8 * steps * width * channels * hidden_units,
            bytes_accessed=8 * steps * width * channels + 4 * channels * hidden_units,
            transcendentals=2 * steps * width * hidden_units,
        ),
        name="channel_mlp",
    )(gain, w_in, w_out, mixed, *extra)


def rotate(block, axis, hops):
    count = lax.axis_size(axis)
    return lax.ppermute(block, axis, [(i, (i + hops) % count) for i in range(count)])


def zonal_halos(first, last, half):
    width = first.shape[1]
    lefts, rights, hops, missing = [], [], 1, half
    while missing > 0:
        take = min(width, missing)
        lefts.insert(0, rotate(last[:, width - take :], "lon", hops))
        rights.append(rotate(first[:, :take], "lon", -hops))
        missing -= take
        hops += 1
    if len(lefts) == 1:
        return lefts[0], rights[0]
    return jnp.concatenate(lefts, axis=1), jnp.concatenate(rights, axis=1)


def step_rows(block, hops):
    count = lax.axis_size("lat")
    pairs = [(i, i + hops) for i in range(count) if 0 <= i + hops < count]
    return lax.ppermute(block, "lat", pairs)


def body(ocean_state, zonal_kernel, norm_gain, input_weight, output_weight):
    blocks, kernel_rows, taps, _ = zonal_kernel.shape
    _, rows, _, width = ocean_state.shape
    rim = kernel_rows // 2
    half = taps // 2
    edge = min(half, width)
    forward, inverse, tap_basis = bases(width, taps)
    total_rows = rows * lax.axis_size("lat")
    index = lax.axis_index("lat") * rows - rim + jnp.arange(rows + 2 * rim, dtype=jnp.int32)
    quad = jnp.sin(jnp.pi * (index.astype(jnp.float32) + 0.5) / total_rows)
    quad = jnp.where((index >= 0) & (index < total_rows), quad, 0.0)
    factors = [
        jnp.einsum("kt,rtc->rkc", tap_basis, zonal_kernel[layer], preferred_element_type=jnp.float32)
        for layer in range(blocks)
    ]
    gains = norm_gain.astype(jnp.float32)[:, None, :]

    groups = [
        list(range(rim)) + list(range(rows - rim, rows)),
        list(range(rim, 2 * rim)) + list(range(rows - 2 * rim, rows - rim)),
        list(range(2 * rim, rows - 2 * rim)),
    ]
    group_of = {row: (k, at) for k, members in enumerate(groups) for at, row in enumerate(members)}
    state = jnp.swapaxes(ocean_state[0], 1, 2)
    mids = [state]
    mid_of = {row: (0, row) for row in range(rows)}

    def pick(members):
        low = members[: len(members) // 2]
        high = members[len(members) // 2 :]
        return jnp.concatenate([state[low[0] : low[-1] + 1], state[high[0] : high[-1] + 1]], axis=0)

    firsts = [pick(members)[:, :edge] for members in groups]
    lasts = [pick(members)[:, width - edge :] for members in groups]
    out = None
    for layer in range(blocks):
        final = layer + 1 == blocks
        halos = [zonal_halos(firsts[k], lasts[k], half) for k in range(3)]
        left = [pair[0] for pair in halos]
        right = [pair[1] for pair in halos]

        def extended(start, stop):
            at = group_of[start][1]
            source, row = mid_of[start]
            count = stop - start
            return jnp.concatenate(
                [left[0][at : at + count], mids[source][row : row + count], right[0][at : at + count]], axis=1
            )

        low = step_rows(extended(rows - rim, rows), 1)
        high = step_rows(extended(0, rim), -1)

        def own(row, used_mids, used):
            k, at = group_of[row]
            source, mid_row = mid_of[row]
            n = len(used_mids)
            j = used.index(k)
            return (row + rim, [(n + j, at), (used_mids.index(source), mid_row), (n + len(used) + j, at)])

        def lat(number, at, place):
            return (place, [(number, at)])

        used = [0, 1]
        used_mids = sorted({mid_of[row][0] for k in used for row in groups[k]})
        sources = [mids[s] for s in used_mids] + [left[k] for k in used] + [right[k] for k in used] + [low, high]
        n = len(sources)
        outer = (
            [lat(n - 2, r, r) for r in range(rim)]
            + [own(row, used_mids, used) for row in range(2 * rim)]
            + [own(row, used_mids, used) for row in range(rows - 2 * rim, rows)]
            + [lat(n - 1, r, rows + rim + r) for r in range(rim)]
        )
        windows = [(0, rim), (3 * rim, rim)]
        tables = (forward, inverse)
        mixed_outer = convolve(quad, tables, factors[layer], sources, outer, windows)
        used = [0, 1, 2]
        used_mids = sorted({source for source, _ in mid_of.values()})
        sources = [mids[s] for s in used_mids] + left + right
        inner = [own(row, used_mids, used) for row in range(rows)]
        weights = (gains[layer], input_weight[layer], output_weight[layer])
        pairs = rows // 2
        mixed_inner = convolve(quad, tables, factors[layer], sources, inner, [(0, rows - 2 * rim)])
        if final:
            places = [(0, 0), (1, pairs - 1)]
            (out,) = mlp(*weights, mixed_outer, places, rows, 0)
            places = [(p, p + 1) for p in range(pairs - 2)]
            (out,) = mlp(*weights, mixed_inner, places, rows, 0, kept=out)
        else:
            outs = [mlp(*weights, mixed_outer, [(0, 0), (1, 1)], 2 * rim, edge)]
            outs.append(mlp(*weights, mixed_inner, [(0, 0), (pairs - 3, 1)], 2 * rim, edge))
            places = [(p + 1, p) for p in range(pairs - 4)]
            outs.append(mlp(*weights, mixed_inner, places, rows - 4 * rim, edge))
            mids = [o[0] for o in outs]
            mid_of = group_of
            firsts = [o[1] for o in outs]
            lasts = [o[2] for o in outs]
    return jnp.swapaxes(out, 1, 2)[None]


def solution(mesh):
    in_specs = (P(None, "lat", None, "lon"), P(), P(), P(), P())
    out_specs = P(None, "lat", None, "lon")
    return jax.shard_map(body, mesh=mesh, in_specs=in_specs, out_specs=out_specs, check_vma=False)
```

```python
import functools
import math

import jax
import jax.numpy as jnp
import numpy as np
from jax import lax
from jax.experimental import pallas as pl
from jax.experimental.pallas import tpu as pltpu
from jax.sharding import PartitionSpec as P


LANES = 128
PACK = 16


def bases(width, taps):
    length = -(-(width + taps) // (2 * PACK)) * 2 * PACK
    odd = 2 * np.arange(length // 2) + 1

    def wave(points):
        angle = np.pi / length * (points[:, None] * odd[None, :] % (2 * length))
        return np.concatenate([np.cos(angle), -np.sin(angle)], axis=1)

    forward = wave(np.arange(width + taps)).T
    inverse = 2.0 / length * wave(taps + np.arange(width))
    tap_basis = wave(np.arange(taps)).T
    return tuple(jnp.asarray(a, jnp.bfloat16) for a in (forward, inverse, tap_basis))


def gelu(values):
    return 0.5 * values * (1.0 + lax.erf(values * math.sqrt(0.5)))


def conv_kernel(*refs, windows, row_refs, counts):
    quad, forward, inverse, factors = refs[:4]
    sources = refs[4 : 4 + counts]
    out, ext, spectra, product = refs[4 + counts :]
    lanes = out.shape[2]
    freqs = forward.shape[0] // 2
    every = len(row_refs)
    taps_r = factors.shape[0]
    for g, (_, pieces) in enumerate(row_refs):
        start = 0
        for source, at in pieces:
            size = sources[source].shape[1]
            ext[start : start + size, g * lanes : (g + 1) * lanes] = sources[source][at]
            start += size
    for g in range(0, every, 2):
        two = slice(g * lanes, (g + 2) * lanes)
        result = jnp.dot(forward[...], ext[:, two], preferred_element_type=jnp.float32)
        for j in range(2):
            spectra[g + j] = result[:, j * lanes : (j + 1) * lanes] * quad[row_refs[g + j][0]]

    def block(f, carry):
        start = pl.multiple_of(f * PACK, PACK)
        re = pl.ds(start, PACK)
        im = pl.ds(pl.multiple_of(freqs + start, PACK), PACK)
        fr = [factors[r, re] for r in range(taps_r)]
        fi = [factors[r, im] for r in range(taps_r)]
        h = 0
        for first, count in windows:
            xr = [spectra[first + g, re] for g in range(taps_r - 1)]
            xi = [spectra[first + g, im] for g in range(taps_r - 1)]
            for k in range(count):
                xr.append(spectra[first + k + taps_r - 1, re])
                xi.append(spectra[first + k + taps_r - 1, im])
                yr = xr[0] * fr[0] - xi[0] * fi[0]
                yi = xr[0] * fi[0] + xi[0] * fr[0]
                for r in range(1, taps_r):
                    yr = yr + (xr[r] * fr[r] - xi[r] * fi[r])
                    yi = yi + (xr[r] * fi[r] + xi[r] * fr[r])
                here = slice(h * lanes, (h + 1) * lanes)
                product[re, here] = yr.astype(product.dtype)
                product[im, here] = yi.astype(product.dtype)
                xr.pop(0)
                xi.pop(0)
                h += 1
        return carry

    lax.fori_loop(0, freqs // PACK, block, 0)
    own = [row_refs[first + taps_r // 2 + k][1] for first, count in windows for k in range(count)]
    for h in range(0, len(own), 2):
        two = slice(h * lanes, (h + 2) * lanes)
        conv = jnp.dot(inverse[...], product[:, two], preferred_element_type=jnp.float32)
        for j in range(2):
            source, at = own[h + j][1]
            value = sources[source][at].astype(jnp.float32)
            out[h + j] = (value + gelu(conv[:, j * lanes : (j + 1) * lanes])).astype(out.dtype)


def convolve(quad, tables, factors, sources, rows, windows, part):
    forward, inverse = tables
    taps_r, length, _ = factors.shape
    start, blocks = part
    out_rows = sum(count for _, count in windows)
    width = inverse.shape[0]
    lanes = blocks * LANES

    def block(array):
        offset = 0 if array.shape[2] == lanes else start
        return pl.BlockSpec((array.shape[0], array.shape[1], LANES), lambda i: (0, 0, i + offset))

    def whole(array):
        return pl.BlockSpec(array.shape, lambda i: (0,) * array.ndim)

    out = jax.ShapeDtypeStruct((out_rows, width, lanes), jnp.bfloat16)
    kernel = functools.partial(conv_kernel, windows=windows, row_refs=rows, counts=len(sources))
    return pl.pallas_call(
        kernel,
        grid=(blocks,),
        out_shape=out,
        in_specs=[pl.BlockSpec(memory_space=pltpu.SMEM), whole(forward), whole(inverse), block(factors)]
        + [block(a) for a in sources],
        out_specs=block(out),
        scratch_shapes=[
            pltpu.VMEM((forward.shape[1], len(rows) * LANES), jnp.bfloat16),
            pltpu.VMEM((len(rows), length, LANES), jnp.float32),
            pltpu.VMEM((length, out_rows * LANES), jnp.bfloat16),
        ],
        compiler_params=pltpu.CompilerParams(vmem_limit_bytes=48 << 20),
        cost_estimate=pl.CostEstimate(
            flops=2 * lanes * length * (len(rows) * forward.shape[1] + out_rows * width),
            bytes_accessed=2 * lanes * (len(rows) * forward.shape[1] + 2 * taps_r * length),
            transcendentals=out_rows * lanes * width,
        ),
        name="zonal_conv",
    )(quad, forward, inverse, factors, *sources)


def mlp_kernel(gain, w_in, w_out, *refs, half, kept, parts):
    mixed = refs[:parts]
    refs = refs[parts + kept :]
    count, width, _ = mixed[0].shape
    channels = w_in.shape[0]
    values = [m[...].reshape(count * width, m.shape[2]).astype(jnp.float32) for m in mixed]
    values = values[0] if parts == 1 else jnp.concatenate(values, axis=1)
    average = jnp.mean(values, axis=1, keepdims=True)
    centred = values - average
    variance = jnp.mean(jnp.square(centred), axis=1, keepdims=True)
    normed = (centred * lax.rsqrt(variance + 1e-05) * gain[...]).astype(jnp.bfloat16)
    total = values
    hidden_units = w_in.shape[1]
    step = math.gcd(hidden_units, 256)
    for f in range(0, hidden_units, step):
        hidden = jnp.dot(normed, w_in[:, f : f + step], preferred_element_type=jnp.float32)
        hidden = gelu(hidden).astype(jnp.bfloat16)
        total = total + jnp.dot(hidden, w_out[f : f + step], preferred_element_type=jnp.float32)
    result = total.astype(jnp.bfloat16).reshape(count, width, channels)
    refs[0][...] = result
    start = 0
    for first, last in zip(refs[1::2], refs[2::2]):
        here = slice(start, start + first.shape[2])
        first[...] = result[:, :half, here]
        last[...] = result[:, width - half :, here]
        start += first.shape[2]


def mlp(gain, w_in, w_out, mixed, places, out_rows, edge, cuts=(), kept=None):
    width = mixed[0].shape[1]
    channels, hidden_units = w_in.shape
    steps = len(places)

    def place(kind):
        def index(i):
            at = places[0][kind]
            for k in range(1, steps):
                at = at + (places[k][kind] - places[k - 1][kind]) * (i >= k).astype(jnp.int32)
            return (at, 0, 0)

        return index

    def whole(array):
        return pl.BlockSpec(array.shape, lambda i: (0,) * array.ndim)

    def pair(lon, lanes, kind):
        return pl.BlockSpec((2, lon, lanes), place(kind))

    lasts = [(width, channels)] + [(edge, cut) for cut in cuts for _ in range(2)]
    extra = [] if kept is None else [kept]
    return pl.pallas_call(
        functools.partial(mlp_kernel, half=edge, kept=len(extra), parts=len(mixed)),
        grid=(steps,),
        out_shape=[jax.ShapeDtypeStruct((out_rows, *last), jnp.bfloat16) for last in lasts],
        in_specs=[whole(gain), whole(w_in), whole(w_out)]
        + [pair(*m.shape[1:], 0) for m in mixed]
        + [pl.BlockSpec(memory_space=pl.ANY) for _ in extra],
        out_specs=[pair(*last, 1) for last in lasts],
        input_output_aliases={3 + len(mixed): 0} if extra else {},
        compiler_params=pltpu.CompilerParams(vmem_limit_bytes=48 << 20),
        cost_estimate=pl.CostEstimate(
            flops=8 * steps * width * channels * hidden_units,
            bytes_accessed=8 * steps * width * channels + 4 * channels * hidden_units,
            transcendentals=2 * steps * width * hidden_units,
        ),
        name="channel_mlp",
    )(gain, w_in, w_out, *mixed, *extra)


def rotate(block, axis, hops):
    count = lax.axis_size(axis)
    return lax.ppermute(block, axis, [(i, (i + hops) % count) for i in range(count)])


def zonal_halos(first, last, half):
    width = first.shape[1]
    lefts, rights, hops, missing = [], [], 1, half
    while missing > 0:
        take = min(width, missing)
        lefts.insert(0, rotate(last[:, width - take :], "lon", hops))
        rights.append(rotate(first[:, :take], "lon", -hops))
        missing -= take
        hops += 1
    if len(lefts) == 1:
        return lefts[0], rights[0]
    return jnp.concatenate(lefts, axis=1), jnp.concatenate(rights, axis=1)


def step_rows(block, hops):
    count = lax.axis_size("lat")
    pairs = [(i, i + hops) for i in range(count) if 0 <= i + hops < count]
    return lax.ppermute(block, "lat", pairs)


def lane_parts(channels):
    units = channels // LANES
    least = max(1, units // 5)
    sizes = [(units - least + 1) // 2, (units - least) // 2, least]
    return [(sum(sizes[:k]), size) for k, size in enumerate(sizes) if size]


def body(ocean_state, zonal_kernel, norm_gain, input_weight, output_weight):
    blocks, kernel_rows, taps, channels = zonal_kernel.shape
    _, rows, _, width = ocean_state.shape
    rim = kernel_rows // 2
    half = taps // 2
    edge = min(half, width)
    forward, inverse, tap_basis = bases(width, taps)
    total_rows = rows * lax.axis_size("lat")
    index = lax.axis_index("lat") * rows - rim + jnp.arange(rows + 2 * rim, dtype=jnp.int32)
    quad = jnp.sin(jnp.pi * (index.astype(jnp.float32) + 0.5) / total_rows)
    quad = jnp.where((index >= 0) & (index < total_rows), quad, 0.0)
    factors = [
        jnp.einsum("kt,rtc->rkc", tap_basis, zonal_kernel[layer], preferred_element_type=jnp.float32)
        for layer in range(blocks)
    ]
    gains = norm_gain.astype(jnp.float32)[:, None, :]

    groups = [
        list(range(rim)) + list(range(rows - rim, rows)),
        list(range(rim, 2 * rim)) + list(range(rows - 2 * rim, rows - rim)),
        list(range(2 * rim, rows - 2 * rim)),
    ]
    group_of = {row: (k, at) for k, members in enumerate(groups) for at, row in enumerate(members)}
    state = jnp.swapaxes(ocean_state[0], 1, 2)
    mids = [state]
    mid_of = {row: (0, row) for row in range(rows)}

    def pick(members):
        low = members[: len(members) // 2]
        high = members[len(members) // 2 :]
        return jnp.concatenate([state[low[0] : low[-1] + 1], state[high[0] : high[-1] + 1]], axis=0)

    parts = lane_parts(channels)
    pieces = [slice(start * LANES, (start + count) * LANES) for start, count in parts]
    cuts = [count * LANES for _, count in parts]
    lanes = [slice(None), slice(None)] + pieces
    groups_of = [groups[0], groups[1]] + [groups[2]] * len(parts)
    firsts = [pick(members)[:, :edge, cut] for members, cut in zip(groups_of, lanes)]
    lasts = [pick(members)[:, width - edge :, cut] for members, cut in zip(groups_of, lanes)]
    tables = (forward, inverse)
    out = None
    for layer in range(blocks):
        final = layer + 1 == blocks
        halos = [zonal_halos(f, b, half) for f, b in zip(firsts, lasts)]

        def extended(start, stop):
            at = group_of[start][1]
            source, row = mid_of[start]
            count = stop - start
            left, right = halos[0]
            return jnp.concatenate(
                [left[at : at + count], mids[source][row : row + count], right[at : at + count]], axis=1
            )

        low = step_rows(extended(rows - rim, rows), 1)
        high = step_rows(extended(0, rim), -1)

        def own(row, used_mids, used):
            k, at = group_of[row]
            source, mid_row = mid_of[row]
            n = len(used_mids)
            j = used.index(k)
            return (row + rim, [(n + j, at), (used_mids.index(source), mid_row), (n + len(used) + j, at)])

        def lat(number, at, place):
            return (place, [(number, at)])

        used = [0, 1]
        used_mids = sorted({mid_of[row][0] for k in used for row in groups[k]})
        sources = [mids[s] for s in used_mids] + [halos[k][side] for side in (0, 1) for k in used] + [low, high]
        n = len(sources)
        outer = (
            [lat(n - 2, r, r) for r in range(rim)]
            + [own(row, used_mids, used) for row in range(2 * rim)]
            + [own(row, used_mids, used) for row in range(rows - 2 * rim, rows)]
            + [lat(n - 1, r, rows + rim + r) for r in range(rim)]
        )
        windows = [(0, rim), (3 * rim, rim)]
        mixed_outer = [
            convolve(quad, tables, factors[layer], sources, outer, windows, (0, channels // LANES))
        ]
        used = [0, 1, 2]
        used_mids = sorted({source for source, _ in mid_of.values()})
        inner = [own(row, used_mids, used) for row in range(rows)]
        mixed_inner = []
        for k, part in enumerate(parts):
            chosen = [halos[0], halos[1], halos[2 + k]]
            sources = [mids[s] for s in used_mids] + [pair[side] for side in (0, 1) for pair in chosen]
            mixed_inner.append(
                convolve(quad, tables, factors[layer], sources, inner, [(0, rows - 2 * rim)], part)
            )
        weights = (gains[layer], input_weight[layer], output_weight[layer])
        pairs = rows // 2
        if final:
            places = [(0, 0), (1, pairs - 1)]
            (out,) = mlp(*weights, mixed_outer, places, rows, 0)
            places = [(p, p + 1) for p in range(pairs - 2)]
            (out,) = mlp(*weights, mixed_inner, places, rows, 0, kept=out)
        else:
            outs = [mlp(*weights, mixed_outer, [(0, 0), (1, 1)], 2 * rim, edge, [channels])]
            places = [(0, 0), (pairs - 3, 1)]
            outs.append(mlp(*weights, mixed_inner, places, 2 * rim, edge, [channels]))
            places = [(p + 1, p) for p in range(pairs - 4)]
            outs.append(mlp(*weights, mixed_inner, places, rows - 4 * rim, edge, cuts))
            mids = [o[0] for o in outs]
            mid_of = group_of
            firsts = [f for o in outs for f in o[1::2]]
            lasts = [b for o in outs for b in o[2::2]]
    return jnp.swapaxes(out, 1, 2)[None]


def solution(mesh):
    in_specs = (P(None, "lat", None, "lon"), P(), P(), P(), P())
    out_specs = P(None, "lat", None, "lon")
    return jax.shard_map(body, mesh=mesh, in_specs=in_specs, out_specs=out_specs, check_vma=False)
```

```python
import functools
import math

import jax
import jax.numpy as jnp
import numpy as np
from jax import lax
from jax.experimental import pallas as pl
from jax.experimental.pallas import tpu as pltpu
from jax.sharding import PartitionSpec as P


LANES = 128
PACK = 16
SUBLANES = 8


def bases(width, taps):
    length = -(-(width + taps) // (2 * PACK)) * 2 * PACK
    odd = 2 * np.arange(length // 2) + 1

    def wave(points):
        angle = np.pi / length * (points[:, None] * odd[None, :] % (2 * length))
        return np.concatenate([np.cos(angle), -np.sin(angle)], axis=1)

    forward = wave(np.arange(width + taps)).T
    inverse = 2.0 / length * wave(taps + np.arange(width))
    tap_basis = wave(np.arange(taps)).T
    return tuple(jnp.asarray(a, jnp.bfloat16) for a in (forward, inverse, tap_basis))


def gelu(values):
    return 0.5 * values * (1.0 + lax.erf(values * math.sqrt(0.5)))


def conv_kernel(*refs, windows, row_refs, counts):
    quad, forward, inverse, factors = refs[:4]
    sources = refs[4 : 4 + counts]
    out, spectra, product = refs[4 + counts :]
    lanes = out.shape[2]
    freqs = forward.shape[0] // 2
    every = len(row_refs)
    taps_r = factors.shape[0]

    def row(g):
        return jnp.concatenate([sources[source][at, lon] for source, at, lon in row_refs[g][1]], axis=0)

    for g in range(0, every, 2):
        two = jnp.concatenate([row(g), row(g + 1)], axis=1)
        result = jnp.dot(forward[...], two, preferred_element_type=jnp.float32)
        for j in range(2):
            spectra[g + j] = result[:, j * lanes : (j + 1) * lanes] * quad[row_refs[g + j][0]]

    def block(f, carry):
        start = pl.multiple_of(f * SUBLANES, SUBLANES)
        re = pl.ds(start, SUBLANES)
        im = pl.ds(pl.multiple_of(freqs + start, SUBLANES), SUBLANES)
        fr = [factors[r, re] for r in range(taps_r)]
        fi = [factors[r, im] for r in range(taps_r)]
        fd = [b - a for a, b in zip(fr, fi)]
        fs = [b + a for a, b in zip(fr, fi)]
        h = 0
        for first, count in windows:
            xr = [spectra[first + g, re] for g in range(taps_r - 1)]
            xi = [spectra[first + g, im] for g in range(taps_r - 1)]
            xs = [a + b for a, b in zip(xr, xi)]
            for k in range(count):
                xr.append(spectra[first + k + taps_r - 1, re])
                xi.append(spectra[first + k + taps_r - 1, im])
                xs.append(xr[-1] + xi[-1])
                both, up, down = xs[0] * fr[0], xr[0] * fd[0], xi[0] * fs[0]
                for r in range(1, taps_r):
                    both, up, down = both + xs[r] * fr[r], up + xr[r] * fd[r], down + xi[r] * fs[r]
                here = slice(h * lanes, (h + 1) * lanes)
                product[re, here] = both - down
                product[im, here] = both + up
                for window in (xr, xi, xs):
                    window.pop(0)
                h += 1
        return carry

    lax.fori_loop(0, freqs // SUBLANES, block, 0, unroll=4)
    own = [row_refs[first + taps_r // 2 + k][1] for first, count in windows for k in range(count)]
    for h in range(0, len(own), 2):
        two = slice(h * lanes, (h + 2) * lanes)
        conv = jnp.dot(inverse[...], product[:, two].astype(jnp.bfloat16), preferred_element_type=jnp.float32)
        for j in range(2):
            source, at, _ = own[h + j][1]
            value = sources[source][at].astype(jnp.float32)
            out[h + j] = (value + gelu(conv[:, j * lanes : (j + 1) * lanes])).astype(out.dtype)


def convolve(quad, tables, factors, sources, rows, windows, part):
    forward, inverse = tables
    taps_r, length, _ = factors.shape
    start, blocks = part
    out_rows = sum(count for _, count in windows)
    width = inverse.shape[0]
    lanes = blocks * LANES

    def block(array):
        offset = 0 if array.shape[2] == lanes else start
        return pl.BlockSpec((array.shape[0], array.shape[1], LANES), lambda i: (0, 0, i + offset))

    def whole(array):
        return pl.BlockSpec(array.shape, lambda i: (0,) * array.ndim)

    out = jax.ShapeDtypeStruct((out_rows, width, lanes), jnp.bfloat16)
    kernel = functools.partial(conv_kernel, windows=windows, row_refs=rows, counts=len(sources))
    return pl.pallas_call(
        kernel,
        grid=(blocks,),
        out_shape=out,
        in_specs=[pl.BlockSpec(memory_space=pltpu.SMEM), whole(forward), whole(inverse), block(factors)]
        + [block(a) for a in sources],
        out_specs=block(out),
        scratch_shapes=[
            pltpu.VMEM((len(rows), length, LANES), jnp.float32),
            pltpu.VMEM((length, out_rows * LANES), jnp.float32),
        ],
        compiler_params=pltpu.CompilerParams(vmem_limit_bytes=48 << 20),
        cost_estimate=pl.CostEstimate(
            flops=2 * lanes * length * (len(rows) * forward.shape[1] + out_rows * width),
            bytes_accessed=2 * lanes * (len(rows) * forward.shape[1] + 2 * taps_r * length),
            transcendentals=out_rows * lanes * width,
        ),
        name="zonal_conv",
    )(quad, forward, inverse, factors, *sources)


def mlp_kernel(gain, w_in, w_out, *refs, half, kept, parts, together):
    mixed = refs[: parts * together]
    refs = refs[parts * together + kept :]
    count, width, _ = mixed[0].shape
    channels, hidden_units = w_in.shape
    totals, normed = [], []
    for t in range(together):
        pieces = mixed[t * parts : (t + 1) * parts]
        values = [m[...].reshape(count * width, m.shape[2]).astype(jnp.float32) for m in pieces]
        values = values[0] if parts == 1 else jnp.concatenate(values, axis=1)
        average = jnp.mean(values, axis=1, keepdims=True)
        centred = values - average
        variance = jnp.mean(jnp.square(centred), axis=1, keepdims=True)
        normed.append((centred * lax.rsqrt(variance + 1e-05) * gain[...]).astype(jnp.bfloat16))
        totals.append(values)
    normed = jnp.concatenate(normed, axis=0)
    total = jnp.concatenate(totals, axis=0)
    step = hidden_units
    for f in range(0, hidden_units, step):
        hidden = jnp.dot(normed, w_in[:, f : f + step], preferred_element_type=jnp.float32)
        hidden = gelu(hidden).astype(jnp.bfloat16)
        total = total + jnp.dot(hidden, w_out[f : f + step], preferred_element_type=jnp.float32)
    result = total.astype(jnp.bfloat16).reshape(together * count, width, channels)
    refs[0][...] = result
    start = 0
    for first, last in zip(refs[1::2], refs[2::2]):
        here = slice(start, start + first.shape[2])
        first[...] = result[:, :half, here]
        last[...] = result[:, width - half :, here]
        start += first.shape[2]


def mlp(gain, w_in, w_out, mixed, steps, out_rows, edge, cuts=(), kept=None):
    width = mixed[0].shape[1]
    channels, hidden_units = w_in.shape
    together = len(steps[0][0])

    def chosen(values):
        def index(i):
            at = values[0]
            for k in range(1, len(values)):
                at = at + (values[k] - values[k - 1]) * (i >= k).astype(jnp.int32)
            return (at, 0, 0)

        return index

    def whole(array):
        return pl.BlockSpec(array.shape, lambda i: (0,) * array.ndim)

    def given(lon, lanes):
        sizes = (pl.Element(2 * together), pl.Element(lon), pl.Element(lanes))
        return pl.BlockSpec(sizes, chosen([row for _, row in steps]))

    lasts = [(width, channels)] + [(edge, cut) for cut in cuts for _ in range(2)]
    extra = [] if kept is None else [kept]
    return pl.pallas_call(
        functools.partial(mlp_kernel, half=edge, kept=len(extra), parts=len(mixed), together=together),
        grid=(len(steps),),
        out_shape=[jax.ShapeDtypeStruct((out_rows, *last), jnp.bfloat16) for last in lasts],
        in_specs=[whole(gain), whole(w_in), whole(w_out)]
        + [
            pl.BlockSpec((2, *m.shape[1:]), chosen([pairs[t] for pairs, _ in steps]))
            for t in range(together)
            for m in mixed
        ]
        + [pl.BlockSpec(memory_space=pl.ANY) for _ in extra],
        out_specs=[given(*last) for last in lasts],
        input_output_aliases={3 + together * len(mixed): 0} if extra else {},
        compiler_params=pltpu.CompilerParams(vmem_limit_bytes=48 << 20),
        cost_estimate=pl.CostEstimate(
            flops=8 * len(steps) * together * width * channels * hidden_units,
            bytes_accessed=8 * len(steps) * together * width * channels + 4 * channels * hidden_units,
            transcendentals=2 * len(steps) * together * width * hidden_units,
        ),
        name="channel_mlp",
    )(gain, w_in, w_out, *(list(mixed) * together), *extra)


def rotate(block, axis, hops):
    count = lax.axis_size(axis)
    return lax.ppermute(block, axis, [(i, (i + hops) % count) for i in range(count)])


def zonal_halos(first, last, half):
    width = first.shape[1]
    lefts, rights, hops, missing = [], [], 1, half
    while missing > 0:
        take = min(width, missing)
        lefts.insert(0, rotate(last[:, width - take :], "lon", hops))
        rights.append(rotate(first[:, :take], "lon", -hops))
        missing -= take
        hops += 1
    if len(lefts) == 1:
        return lefts[0], rights[0]
    return jnp.concatenate(lefts, axis=1), jnp.concatenate(rights, axis=1)


def step_rows(block, hops):
    count = lax.axis_size("lat")
    pairs = [(i, i + hops) for i in range(count) if 0 <= i + hops < count]
    return lax.ppermute(block, "lat", pairs)


def lane_parts(channels):
    units = channels // LANES
    least = max(1, units // 5)
    sizes = [(units - least + 1) // 2, (units - least) // 2, least]
    return [(sum(sizes[:k]), size) for k, size in enumerate(sizes) if size]


def body(ocean_state, zonal_kernel, norm_gain, input_weight, output_weight):
    blocks, kernel_rows, taps, channels = zonal_kernel.shape
    _, rows, _, width = ocean_state.shape
    rim = kernel_rows // 2
    half = taps // 2
    edge = min(half, width)
    forward, inverse, tap_basis = bases(width, taps)
    total_rows = rows * lax.axis_size("lat")
    index = lax.axis_index("lat") * rows - rim + jnp.arange(rows + 2 * rim, dtype=jnp.int32)
    quad = jnp.sin(jnp.pi * (index.astype(jnp.float32) + 0.5) / total_rows)
    quad = jnp.where((index >= 0) & (index < total_rows), quad, 0.0)
    factors = [
        jnp.einsum("kt,rtc->rkc", tap_basis, zonal_kernel[layer], preferred_element_type=jnp.float32)
        for layer in range(blocks)
    ]
    gains = norm_gain.astype(jnp.float32)[:, None, :]

    groups = [
        list(range(rim)) + list(range(rows - rim, rows)),
        list(range(rim, 2 * rim)) + list(range(rows - 2 * rim, rows - rim)),
        list(range(2 * rim, rows - 2 * rim)),
    ]
    group_of = {row: (k, at) for k, members in enumerate(groups) for at, row in enumerate(members)}
    state = jnp.swapaxes(ocean_state[0], 1, 2)
    mids = [state]
    mid_of = {row: (0, row) for row in range(rows)}

    def pick(members):
        low = members[: len(members) // 2]
        high = members[len(members) // 2 :]
        return jnp.concatenate([state[low[0] : low[-1] + 1], state[high[0] : high[-1] + 1]], axis=0)

    parts = lane_parts(channels)
    pieces = [slice(start * LANES, (start + count) * LANES) for start, count in parts]
    cuts = [count * LANES for _, count in parts]
    lanes = [slice(None), slice(None)] + pieces
    groups_of = [groups[0], groups[1]] + [groups[2]] * len(parts)
    firsts = [pick(members)[:, :edge, cut] for members, cut in zip(groups_of, lanes)]
    lasts = [pick(members)[:, width - edge :, cut] for members, cut in zip(groups_of, lanes)]
    tables = (forward, inverse)
    out = None
    for layer in range(blocks):
        final = layer + 1 == blocks
        halos = [zonal_halos(f, b, half) for f, b in zip(firsts, lasts)]

        def near(start):
            source, row = mid_of[start]
            return mids[source][row : row + rim]

        def far(start):
            at = group_of[start][1]
            return jnp.concatenate([halo[at : at + rim] for halo in halos[0]], axis=1)

        low = [step_rows(near(rows - rim), 1), step_rows(far(rows - rim), 1)]
        high = [step_rows(near(0), -1), step_rows(far(0), -1)]

        def own(row, used_mids, used):
            k, at = group_of[row]
            source, mid_row = mid_of[row]
            n = len(used_mids)
            j = used.index(k)
            every = slice(None)
            middle = (used_mids.index(source), mid_row, every)
            return (row + rim, [(n + j, at, every), middle, (n + len(used) + j, at, every)])

        def lat(number, at, place):
            return (
                place,
                [
                    (number + 1, at, slice(0, half)),
                    (number, at, slice(None)),
                    (number + 1, at, slice(half, 2 * half)),
                ],
            )

        used = [0, 1]
        used_mids = sorted({mid_of[row][0] for k in used for row in groups[k]})
        sources = [mids[s] for s in used_mids] + [halos[k][side] for side in (0, 1) for k in used]
        sources = sources + low + high
        n = len(sources)
        outer = (
            [lat(n - 4, r, r) for r in range(rim)]
            + [own(row, used_mids, used) for row in range(2 * rim)]
            + [own(row, used_mids, used) for row in range(rows - 2 * rim, rows)]
            + [lat(n - 2, r, rows + rim + r) for r in range(rim)]
        )
        windows = [(0, rim), (3 * rim, rim)]
        mixed_outer = [
            convolve(quad, tables, factors[layer], sources, outer, windows, (0, channels // LANES))
        ]
        used = [0, 1, 2]
        used_mids = sorted({source for source, _ in mid_of.values()})
        inner = [own(row, used_mids, used) for row in range(rows)]
        mixed_inner = []
        for k, part in enumerate(parts):
            chosen = [halos[0], halos[1], halos[2 + k]]
            sources = [mids[s] for s in used_mids] + [pair[side] for side in (0, 1) for pair in chosen]
            mixed_inner.append(
                convolve(quad, tables, factors[layer], sources, inner, [(0, rows - 2 * rim)], part)
            )
        weights = (gains[layer], input_weight[layer], output_weight[layer])
        pairs = rows // 2
        if final:
            (out,) = mlp(*weights, mixed_outer, [([0], 0), ([1], rows - 2)], rows, 0)
            steps = [([p], 2 * p + rim) for p in range(pairs - 2)]
            (out,) = mlp(*weights, mixed_inner, steps, rows, 0, kept=out)
        else:
            outs = [mlp(*weights, mixed_outer, [([0], 0), ([1], 2)], 2 * rim, edge, [channels])]
            outs.append(mlp(*weights, mixed_inner, [([0], 0), ([pairs - 3], 2)], 2 * rim, edge, [channels]))
            steps = [([p + 1], 2 * p) for p in range(pairs - 4)]
            outs.append(mlp(*weights, mixed_inner, steps, rows - 4 * rim, edge, cuts))
            mids = [o[0] for o in outs]
            mid_of = group_of
            firsts = [f for o in outs for f in o[1::2]]
            lasts = [b for o in outs for b in o[2::2]]
    return jnp.swapaxes(out, 1, 2)[None]


def solution(mesh):
    in_specs = (P(None, "lat", None, "lon"), P(), P(), P(), P())
    out_specs = P(None, "lat", None, "lon")
    return jax.shard_map(body, mesh=mesh, in_specs=in_specs, out_specs=out_specs, check_vma=False)
```

```python
import functools
import math

import jax
import jax.numpy as jnp
import numpy as np
from jax import lax
from jax.experimental import pallas as pl
from jax.experimental.pallas import tpu as pltpu
from jax.sharding import PartitionSpec as P


LANES = 128
PACK = 16
SUBLANES = 8


def bases(width, taps):
    length = -(-(width + taps) // (2 * PACK)) * 2 * PACK
    odd = 2 * np.arange(length // 2) + 1

    def wave(points):
        angle = np.pi / length * (points[:, None] * odd[None, :] % (2 * length))
        return np.concatenate([np.cos(angle), -np.sin(angle)], axis=1)

    forward = wave(np.arange(width + taps)).T
    inverse = 2.0 / length * wave(taps + np.arange(width))
    tap_basis = wave(np.arange(taps)).T
    return tuple(jnp.asarray(a, jnp.bfloat16) for a in (forward, inverse, tap_basis))


def gelu(values):
    return 0.5 * values * (1.0 + lax.erf(values * math.sqrt(0.5)))


def conv_kernel(*refs, windows, row_refs, counts):
    quad, forward, inverse, factors = refs[:4]
    sources = refs[4 : 4 + counts]
    out, spectra, product = refs[4 + counts :]
    lanes = out.shape[2]
    freqs = forward.shape[0] // 2
    every = len(row_refs)
    taps_r = factors.shape[0]

    def row(g):
        return jnp.concatenate([sources[source][at, lon] for source, at, lon in row_refs[g][1]], axis=0)

    for g in range(0, every, 2):
        two = jnp.concatenate([row(g), row(g + 1)], axis=1)
        result = jnp.dot(forward[...], two, preferred_element_type=jnp.float32)
        for j in range(2):
            spectra[g + j] = result[:, j * lanes : (j + 1) * lanes] * quad[row_refs[g + j][0]]

    def block(f, carry):
        start = pl.multiple_of(f * SUBLANES, SUBLANES)
        re = pl.ds(start, SUBLANES)
        im = pl.ds(pl.multiple_of(freqs + start, SUBLANES), SUBLANES)
        fr = [factors[r, re] for r in range(taps_r)]
        fi = [factors[r, im] for r in range(taps_r)]
        fd = [b - a for a, b in zip(fr, fi)]
        fs = [b + a for a, b in zip(fr, fi)]
        h = 0
        for first, count in windows:
            xr = [spectra[first + g, re] for g in range(taps_r - 1)]
            xi = [spectra[first + g, im] for g in range(taps_r - 1)]
            xs = [a + b for a, b in zip(xr, xi)]
            for k in range(count):
                xr.append(spectra[first + k + taps_r - 1, re])
                xi.append(spectra[first + k + taps_r - 1, im])
                xs.append(xr[-1] + xi[-1])
                both, up, down = xs[0] * fr[0], xr[0] * fd[0], xi[0] * fs[0]
                for r in range(1, taps_r):
                    both, up, down = both + xs[r] * fr[r], up + xr[r] * fd[r], down + xi[r] * fs[r]
                here = slice(h * lanes, (h + 1) * lanes)
                product[re, here] = both - down
                product[im, here] = both + up
                for window in (xr, xi, xs):
                    window.pop(0)
                h += 1
        return carry

    lax.fori_loop(0, freqs // SUBLANES, block, 0, unroll=4)
    own = [row_refs[first + taps_r // 2 + k][1] for first, count in windows for k in range(count)]
    for h in range(0, len(own), 2):
        two = slice(h * lanes, (h + 2) * lanes)
        conv = jnp.dot(inverse[...], product[:, two].astype(jnp.bfloat16), preferred_element_type=jnp.float32)
        for j in range(2):
            source, at, _ = own[h + j][1]
            value = sources[source][at].astype(jnp.float32)
            out[h + j] = (value + gelu(conv[:, j * lanes : (j + 1) * lanes])).astype(out.dtype)


def convolve(quad, tables, factors, sources, rows, windows, part):
    forward, inverse = tables
    taps_r, length, _ = factors.shape
    start, blocks = part
    out_rows = sum(count for _, count in windows)
    width = inverse.shape[0]
    lanes = blocks * LANES

    def block(array):
        offset = 0 if array.shape[2] == lanes else start
        return pl.BlockSpec((array.shape[0], array.shape[1], LANES), lambda i: (0, 0, i + offset))

    def whole(array):
        return pl.BlockSpec(array.shape, lambda i: (0,) * array.ndim)

    out = jax.ShapeDtypeStruct((out_rows, width, lanes), jnp.bfloat16)
    kernel = functools.partial(conv_kernel, windows=windows, row_refs=rows, counts=len(sources))
    return pl.pallas_call(
        kernel,
        grid=(blocks,),
        out_shape=out,
        in_specs=[pl.BlockSpec(memory_space=pltpu.SMEM), whole(forward), whole(inverse), block(factors)]
        + [block(a) for a in sources],
        out_specs=block(out),
        scratch_shapes=[
            pltpu.VMEM((len(rows), length, LANES), jnp.float32),
            pltpu.VMEM((length, out_rows * LANES), jnp.float32),
        ],
        compiler_params=pltpu.CompilerParams(vmem_limit_bytes=20 << 20),
        cost_estimate=pl.CostEstimate(
            flops=2 * lanes * length * (len(rows) * forward.shape[1] + out_rows * width),
            bytes_accessed=2 * lanes * (len(rows) * forward.shape[1] + 2 * taps_r * length),
            transcendentals=out_rows * lanes * width,
        ),
        name="zonal_conv",
    )(quad, forward, inverse, factors, *sources)


def mlp_kernel(gain, w_in, w_out, *refs, half, kept, parts, together):
    mixed = refs[: parts * together]
    refs = refs[parts * together + kept :]
    count, width, _ = mixed[0].shape
    channels, hidden_units = w_in.shape
    totals, normed = [], []
    for t in range(together):
        pieces = mixed[t * parts : (t + 1) * parts]
        values = [m[...].reshape(count * width, m.shape[2]).astype(jnp.float32) for m in pieces]
        values = values[0] if parts == 1 else jnp.concatenate(values, axis=1)
        average = jnp.mean(values, axis=1, keepdims=True)
        centred = values - average
        variance = jnp.mean(jnp.square(centred), axis=1, keepdims=True)
        normed.append((centred * lax.rsqrt(variance + 1e-05) * gain[...]).astype(jnp.bfloat16))
        totals.append(values)
    normed = jnp.concatenate(normed, axis=0)
    total = jnp.concatenate(totals, axis=0)
    step = hidden_units
    for f in range(0, hidden_units, step):
        hidden = jnp.dot(normed, w_in[:, f : f + step], preferred_element_type=jnp.float32)
        hidden = gelu(hidden).astype(jnp.bfloat16)
        total = total + jnp.dot(hidden, w_out[f : f + step], preferred_element_type=jnp.float32)
    result = total.astype(jnp.bfloat16).reshape(together * count, width, channels)
    refs[0][...] = result
    start = 0
    for first, last in zip(refs[1::2], refs[2::2]):
        here = slice(start, start + first.shape[2])
        first[...] = result[:, :half, here]
        last[...] = result[:, width - half :, here]
        start += first.shape[2]


def mlp(gain, w_in, w_out, mixed, steps, out_rows, edge, cuts=(), kept=None):
    width = mixed[0].shape[1]
    channels, hidden_units = w_in.shape
    together = len(steps[0][0])

    def chosen(values):
        def index(i):
            at = values[0]
            for k in range(1, len(values)):
                at = at + (values[k] - values[k - 1]) * (i >= k).astype(jnp.int32)
            return (at, 0, 0)

        return index

    def whole(array):
        return pl.BlockSpec(array.shape, lambda i: (0,) * array.ndim)

    def given(lon, lanes):
        sizes = (pl.Element(2 * together), pl.Element(lon), pl.Element(lanes))
        return pl.BlockSpec(sizes, chosen([row for _, row in steps]))

    lasts = [(width, channels)] + [(edge, cut) for cut in cuts for _ in range(2)]
    extra = [] if kept is None else [kept]
    return pl.pallas_call(
        functools.partial(mlp_kernel, half=edge, kept=len(extra), parts=len(mixed), together=together),
        grid=(len(steps),),
        out_shape=[jax.ShapeDtypeStruct((out_rows, *last), jnp.bfloat16) for last in lasts],
        in_specs=[whole(gain), whole(w_in), whole(w_out)]
        + [
            pl.BlockSpec((2, *m.shape[1:]), chosen([pairs[t] for pairs, _ in steps]))
            for t in range(together)
            for m in mixed
        ]
        + [pl.BlockSpec(memory_space=pl.ANY) for _ in extra],
        out_specs=[given(*last) for last in lasts],
        input_output_aliases={3 + together * len(mixed): 0} if extra else {},
        compiler_params=pltpu.CompilerParams(vmem_limit_bytes=20 << 20),
        cost_estimate=pl.CostEstimate(
            flops=8 * len(steps) * together * width * channels * hidden_units,
            bytes_accessed=8 * len(steps) * together * width * channels + 4 * channels * hidden_units,
            transcendentals=2 * len(steps) * together * width * hidden_units,
        ),
        name="channel_mlp",
    )(gain, w_in, w_out, *(list(mixed) * together), *extra)


def rotate(block, axis, hops):
    count = lax.axis_size(axis)
    return lax.ppermute(block, axis, [(i, (i + hops) % count) for i in range(count)])


def zonal_halos(first, last, half):
    width = first.shape[1]
    lefts, rights, hops, missing = [], [], 1, half
    while missing > 0:
        take = min(width, missing)
        lefts.insert(0, rotate(last[:, width - take :], "lon", hops))
        rights.append(rotate(first[:, :take], "lon", -hops))
        missing -= take
        hops += 1
    if len(lefts) == 1:
        return lefts[0], rights[0]
    return jnp.concatenate(lefts, axis=1), jnp.concatenate(rights, axis=1)


def step_rows(block, hops):
    count = lax.axis_size("lat")
    pairs = [(i, i + hops) for i in range(count) if 0 <= i + hops < count]
    return lax.ppermute(block, "lat", pairs)


def lane_parts(channels):
    units = channels // LANES
    least = max(1, units // 5)
    sizes = [(units - least + 1) // 2, (units - least) // 2, least]
    return [(sum(sizes[:k]), size) for k, size in enumerate(sizes) if size]


def body(ocean_state, zonal_kernel, norm_gain, input_weight, output_weight):
    blocks, kernel_rows, taps, channels = zonal_kernel.shape
    _, rows, _, width = ocean_state.shape
    rim = kernel_rows // 2
    half = taps // 2
    edge = min(half, width)
    forward, inverse, tap_basis = bases(width, taps)
    total_rows = rows * lax.axis_size("lat")
    index = lax.axis_index("lat") * rows - rim + jnp.arange(rows + 2 * rim, dtype=jnp.int32)
    quad = jnp.sin(jnp.pi * (index.astype(jnp.float32) + 0.5) / total_rows)
    quad = jnp.where((index >= 0) & (index < total_rows), quad, 0.0)
    factors = []
    for layer in range(blocks):
        taps_of = zonal_kernel[layer]
        factors.append(jnp.einsum("kt,rtc->rkc", tap_basis, taps_of, preferred_element_type=jnp.float32))
    gains = norm_gain.astype(jnp.float32)[:, None, :]

    groups = [
        list(range(rim)) + list(range(rows - rim, rows)),
        list(range(rim, 2 * rim)) + list(range(rows - 2 * rim, rows - rim)),
        list(range(2 * rim, rows - 2 * rim)),
    ]
    group_of = {row: (k, at) for k, members in enumerate(groups) for at, row in enumerate(members)}
    state = jnp.swapaxes(ocean_state[0], 1, 2)
    mids = [state]
    mid_of = {row: (0, row) for row in range(rows)}

    pairs = state.reshape(rows // rim, rim, width, channels)

    def pick(members, lon, cut):
        first, last = members[0] // rim, members[-1] // rim
        chosen = pairs[first : last + 1 : max(1, (last - first) // (len(members) // rim - 1))]
        return chosen[:, :, lon, cut].reshape(len(members), -1, chosen[..., cut].shape[-1])

    parts = lane_parts(channels)
    pieces = [slice(start * LANES, (start + count) * LANES) for start, count in parts]
    cuts = [count * LANES for _, count in parts]
    lanes = [slice(0, channels)] * 2 + pieces
    groups_of = [groups[0], groups[1]] + [groups[2]] * len(parts)
    firsts = [pick(members, slice(0, edge), cut) for members, cut in zip(groups_of, lanes)]
    lasts = [pick(members, slice(width - edge, width), cut) for members, cut in zip(groups_of, lanes)]
    tables = (forward, inverse)
    out = None
    for layer in range(blocks):
        final = layer + 1 == blocks
        halos = [zonal_halos(f, b, half) for f, b in zip(firsts, lasts)]

        def near(start):
            source, row = mid_of[start]
            return mids[source][row : row + rim]

        def far(start):
            at = group_of[start][1]
            return jnp.concatenate([halo[at : at + rim] for halo in halos[0]], axis=1)

        low = [step_rows(near(rows - rim), 1), step_rows(far(rows - rim), 1)]
        high = [step_rows(near(0), -1), step_rows(far(0), -1)]

        def own(row, used_mids, used):
            k, at = group_of[row]
            source, mid_row = mid_of[row]
            n = len(used_mids)
            j = used.index(k)
            every = slice(None)
            middle = (used_mids.index(source), mid_row, every)
            return (row + rim, [(n + j, at, every), middle, (n + len(used) + j, at, every)])

        def lat(number, at, place):
            return (
                place,
                [
                    (number + 1, at, slice(0, half)),
                    (number, at, slice(None)),
                    (number + 1, at, slice(half, 2 * half)),
                ],
            )

        used = [0, 1]
        used_mids = sorted({mid_of[row][0] for k in used for row in groups[k]})
        sources = [mids[s] for s in used_mids] + [halos[k][side] for side in (0, 1) for k in used]
        sources = sources + low + high
        n = len(sources)
        outer = (
            [lat(n - 4, r, r) for r in range(rim)]
            + [own(row, used_mids, used) for row in range(2 * rim)]
            + [own(row, used_mids, used) for row in range(rows - 2 * rim, rows)]
            + [lat(n - 2, r, rows + rim + r) for r in range(rim)]
        )
        windows = [(0, rim), (3 * rim, rim)]
        mixed_outer = [
            convolve(quad, tables, factors[layer], sources, outer, windows, (0, channels // LANES))
        ]
        used = [0, 1, 2]
        used_mids = sorted({source for source, _ in mid_of.values()})
        inner = [own(row, used_mids, used) for row in range(rows)]
        mixed_inner = []
        for k, part in enumerate(parts):
            chosen = [halos[0], halos[1], halos[2 + k]]
            sources = [mids[s] for s in used_mids] + [pair[side] for side in (0, 1) for pair in chosen]
            mixed_inner.append(
                convolve(quad, tables, factors[layer], sources, inner, [(0, rows - 2 * rim)], part)
            )
        weights = (gains[layer], input_weight[layer], output_weight[layer])
        count = rows // 2
        if final:
            (out,) = mlp(*weights, mixed_outer, [([0], 0), ([1], rows - 2)], rows, 0)
            steps = [([p], 2 * p + rim) for p in range(count - 2)]
            (out,) = mlp(*weights, mixed_inner, steps, rows, 0, kept=out)
        else:
            outs = [mlp(*weights, mixed_outer, [([0], 0), ([1], 2)], 2 * rim, edge, [channels])]
            outs.append(mlp(*weights, mixed_inner, [([0], 0), ([count - 3], 2)], 2 * rim, edge, [channels]))
            steps = [([p + 1], 2 * p) for p in range(count - 4)]
            outs.append(mlp(*weights, mixed_inner, steps, rows - 4 * rim, edge, cuts))
            mids = [o[0] for o in outs]
            mid_of = group_of
            firsts = [f for o in outs for f in o[1::2]]
            lasts = [b for o in outs for b in o[2::2]]
    return jnp.swapaxes(out, 1, 2)[None]


def solution(mesh):
    in_specs = (P(None, "lat", None, "lon"), P(), P(), P(), P())
    out_specs = P(None, "lat", None, "lon")
    return jax.shard_map(body, mesh=mesh, in_specs=in_specs, out_specs=out_specs, check_vma=False)
```

```python
import functools
import math

import jax
import jax.numpy as jnp
import numpy as np
from jax import lax
from jax.experimental import pallas as pl
from jax.experimental.pallas import tpu as pltpu
from jax.sharding import PartitionSpec as P


LANES = 128
PACK = 16
SUBLANES = 8


def bases(width, taps):
    length = -(-(width + taps) // (2 * PACK)) * 2 * PACK
    odd = 2 * np.arange(length // 2) + 1

    def wave(points):
        angle = np.pi / length * (points[:, None] * odd[None, :] % (2 * length))
        return np.concatenate([np.cos(angle), -np.sin(angle)], axis=1)

    forward = wave(np.arange(width + taps)).T
    inverse = 2.0 / length * wave(taps + np.arange(width))
    tap_basis = wave(np.arange(taps)).T
    return tuple(jnp.asarray(a, jnp.bfloat16) for a in (forward, inverse, tap_basis))


def gelu(values):
    return 0.5 * values * (1.0 + lax.erf(values * math.sqrt(0.5)))


def conv_kernel(*refs, windows, row_refs, counts):
    quad, forward, inverse, factors = refs[:4]
    sources = refs[4 : 4 + counts]
    out, spectra, product = refs[4 + counts :]
    lanes = out.shape[2]
    freqs = forward.shape[0] // 2
    every = len(row_refs)
    taps_r = factors.shape[0]

    def row(g):
        return jnp.concatenate([sources[source][at, lon] for source, at, lon in row_refs[g][1]], axis=0)

    for g in range(0, every, 2):
        two = jnp.concatenate([row(g), row(g + 1)], axis=1)
        result = jnp.dot(forward[...], two, preferred_element_type=jnp.float32)
        for j in range(2):
            spectra[g + j] = result[:, j * lanes : (j + 1) * lanes] * quad[row_refs[g + j][0]]

    def block(f, carry):
        start = pl.multiple_of(f * SUBLANES, SUBLANES)
        re = pl.ds(start, SUBLANES)
        im = pl.ds(pl.multiple_of(freqs + start, SUBLANES), SUBLANES)
        fr = [factors[r, re] for r in range(taps_r)]
        fi = [factors[r, im] for r in range(taps_r)]
        fd = [b - a for a, b in zip(fr, fi)]
        fs = [b + a for a, b in zip(fr, fi)]
        h = 0
        for first, count in windows:
            xr = [spectra[first + g, re] for g in range(taps_r - 1)]
            xi = [spectra[first + g, im] for g in range(taps_r - 1)]
            xs = [a + b for a, b in zip(xr, xi)]
            for k in range(count):
                xr.append(spectra[first + k + taps_r - 1, re])
                xi.append(spectra[first + k + taps_r - 1, im])
                xs.append(xr[-1] + xi[-1])
                both, up, down = xs[0] * fr[0], xr[0] * fd[0], xi[0] * fs[0]
                for r in range(1, taps_r):
                    both, up, down = both + xs[r] * fr[r], up + xr[r] * fd[r], down + xi[r] * fs[r]
                here = slice(h * lanes, (h + 1) * lanes)
                product[re, here] = both - down
                product[im, here] = both + up
                for window in (xr, xi, xs):
                    window.pop(0)
                h += 1
        return carry

    lax.fori_loop(0, freqs // SUBLANES, block, 0, unroll=4)
    own = [row_refs[first + taps_r // 2 + k][1] for first, count in windows for k in range(count)]
    for h in range(0, len(own), 2):
        two = slice(h * lanes, (h + 2) * lanes)
        conv = jnp.dot(inverse[...], product[:, two].astype(jnp.bfloat16), preferred_element_type=jnp.float32)
        for j in range(2):
            source, at, _ = own[h + j][1]
            value = sources[source][at].astype(jnp.float32)
            out[h + j] = (value + gelu(conv[:, j * lanes : (j + 1) * lanes])).astype(out.dtype)


def convolve(quad, tables, factors, sources, rows, windows, part):
    forward, inverse = tables
    taps_r, length, _ = factors.shape
    start, blocks = part
    out_rows = sum(count for _, count in windows)
    width = inverse.shape[0]
    lanes = blocks * LANES

    def block(array):
        offset = 0 if array.shape[2] == lanes else start
        return pl.BlockSpec((array.shape[0], array.shape[1], LANES), lambda i: (0, 0, i + offset))

    def whole(array):
        return pl.BlockSpec(array.shape, lambda i: (0,) * array.ndim)

    out = jax.ShapeDtypeStruct((out_rows, width, lanes), jnp.bfloat16)
    kernel = functools.partial(conv_kernel, windows=windows, row_refs=rows, counts=len(sources))
    return pl.pallas_call(
        kernel,
        grid=(blocks,),
        out_shape=out,
        in_specs=[pl.BlockSpec(memory_space=pltpu.SMEM), whole(forward), whole(inverse), block(factors)]
        + [block(a) for a in sources],
        out_specs=block(out),
        scratch_shapes=[
            pltpu.VMEM((len(rows), length, LANES), jnp.float32),
            pltpu.VMEM((length, out_rows * LANES), jnp.float32),
        ],
        compiler_params=pltpu.CompilerParams(vmem_limit_bytes=20 << 20),
        cost_estimate=pl.CostEstimate(
            flops=2 * lanes * length * (len(rows) * forward.shape[1] + out_rows * width),
            bytes_accessed=2 * lanes * (len(rows) * forward.shape[1] + 2 * taps_r * length),
            transcendentals=out_rows * lanes * width,
        ),
        name="zonal_conv",
    )(quad, forward, inverse, factors, *sources)


def mlp_kernel(gain, w_in, w_out, *refs, half, kept, parts, together):
    mixed = refs[: parts * together]
    refs = refs[parts * together + kept :]
    count, width, _ = mixed[0].shape
    channels, hidden_units = w_in.shape
    totals, normed = [], []
    for t in range(together):
        pieces = mixed[t * parts : (t + 1) * parts]
        values = [m[...].reshape(count * width, m.shape[2]).astype(jnp.float32) for m in pieces]
        values = values[0] if parts == 1 else jnp.concatenate(values, axis=1)
        average = jnp.mean(values, axis=1, keepdims=True)
        centred = values - average
        variance = jnp.mean(jnp.square(centred), axis=1, keepdims=True)
        normed.append((centred * lax.rsqrt(variance + 1e-05) * gain[...]).astype(jnp.bfloat16))
        totals.append(values)
    normed = jnp.concatenate(normed, axis=0)
    total = jnp.concatenate(totals, axis=0)
    step = hidden_units
    for f in range(0, hidden_units, step):
        hidden = jnp.dot(normed, w_in[:, f : f + step], preferred_element_type=jnp.float32)
        hidden = gelu(hidden).astype(jnp.bfloat16)
        total = total + jnp.dot(hidden, w_out[f : f + step], preferred_element_type=jnp.float32)
    result = total.astype(jnp.bfloat16).reshape(together * count, width, channels)
    refs[0][...] = result
    start = 0
    for first, last in zip(refs[1::2], refs[2::2]):
        here = slice(start, start + first.shape[2])
        first[...] = result[:, :half, here]
        last[...] = result[:, width - half :, here]
        start += first.shape[2]


def mlp(gain, w_in, w_out, mixed, steps, out_rows, edge, cuts=(), kept=None):
    width = mixed[0].shape[1]
    channels, hidden_units = w_in.shape
    together = len(steps[0][0])

    def chosen(values):
        def index(i):
            at = values[0]
            for k in range(1, len(values)):
                at = at + (values[k] - values[k - 1]) * (i >= k).astype(jnp.int32)
            return (at, 0, 0)

        return index

    def whole(array):
        return pl.BlockSpec(array.shape, lambda i: (0,) * array.ndim)

    def given(lon, lanes):
        sizes = (pl.Element(2 * together), pl.Element(lon), pl.Element(lanes))
        return pl.BlockSpec(sizes, chosen([row for _, row in steps]))

    lasts = [(width, channels)] + [(edge, cut) for cut in cuts for _ in range(2)]
    extra = [] if kept is None else [kept]
    return pl.pallas_call(
        functools.partial(mlp_kernel, half=edge, kept=len(extra), parts=len(mixed), together=together),
        grid=(len(steps),),
        out_shape=[jax.ShapeDtypeStruct((out_rows, *last), jnp.bfloat16) for last in lasts],
        in_specs=[whole(gain), whole(w_in), whole(w_out)]
        + [
            pl.BlockSpec((2, *m.shape[1:]), chosen([pairs[t] for pairs, _ in steps]))
            for t in range(together)
            for m in mixed
        ]
        + [pl.BlockSpec(memory_space=pl.ANY) for _ in extra],
        out_specs=[given(*last) for last in lasts],
        input_output_aliases={3 + together * len(mixed): 0} if extra else {},
        compiler_params=pltpu.CompilerParams(vmem_limit_bytes=20 << 20),
        cost_estimate=pl.CostEstimate(
            flops=8 * len(steps) * together * width * channels * hidden_units,
            bytes_accessed=8 * len(steps) * together * width * channels + 4 * channels * hidden_units,
            transcendentals=2 * len(steps) * together * width * hidden_units,
        ),
        name="channel_mlp",
    )(gain, w_in, w_out, *(list(mixed) * together), *extra)


def rotate(block, axis, hops):
    count = lax.axis_size(axis)
    return lax.ppermute(block, axis, [(i, (i + hops) % count) for i in range(count)])


def zonal_halos(first, last, half):
    width = first.shape[1]
    lefts, rights, hops, missing = [], [], 1, half
    while missing > 0:
        take = min(width, missing)
        lefts.insert(0, rotate(last[:, width - take :], "lon", hops))
        rights.append(rotate(first[:, :take], "lon", -hops))
        missing -= take
        hops += 1
    if len(lefts) == 1:
        return lefts[0], rights[0]
    return jnp.concatenate(lefts, axis=1), jnp.concatenate(rights, axis=1)


def step_rows(block, hops):
    count = lax.axis_size("lat")
    pairs = [(i, i + hops) for i in range(count) if 0 <= i + hops < count]
    return lax.ppermute(block, "lat", pairs)


def lane_parts(channels):
    units = channels // LANES
    least = max(1, units // 5)
    sizes = [(units - least + 1) // 2, (units - least) // 2, least]
    return [(sum(sizes[:k]), size) for k, size in enumerate(sizes) if size]


def body(ocean_state, zonal_kernel, norm_gain, input_weight, output_weight):
    blocks, kernel_rows, taps, channels = zonal_kernel.shape
    _, rows, _, width = ocean_state.shape
    rim = kernel_rows // 2
    half = taps // 2
    edge = min(half, width)
    forward, inverse, tap_basis = bases(width, taps)
    total_rows = rows * lax.axis_size("lat")
    index = lax.axis_index("lat") * rows - rim + jnp.arange(rows + 2 * rim, dtype=jnp.int32)
    quad = jnp.sin(jnp.pi * (index.astype(jnp.float32) + 0.5) / total_rows)
    quad = jnp.where((index >= 0) & (index < total_rows), quad, 0.0)
    factors = []
    for layer in range(blocks):
        taps_of = zonal_kernel[layer]
        factors.append(jnp.einsum("kt,rtc->rkc", tap_basis, taps_of, preferred_element_type=jnp.float32))
    gains = norm_gain.astype(jnp.float32)[:, None, :]

    groups = [
        list(range(rim)) + list(range(rows - rim, rows)),
        list(range(rim, 2 * rim)) + list(range(rows - 2 * rim, rows - rim)),
        list(range(2 * rim, rows - 2 * rim)),
    ]
    group_of = {row: (k, at) for k, members in enumerate(groups) for at, row in enumerate(members)}
    state = jnp.swapaxes(ocean_state[0], 1, 2)
    mids = [state]
    mid_of = {row: (0, row) for row in range(rows)}

    pairs = state.reshape(rows // rim, rim, width, channels)

    def pick(pairs, members, lon, cut):
        first, last = members[0] // rim, members[-1] // rim
        chosen = pairs[first : last + 1 : max(1, (last - first) // (len(members) // rim - 1))]
        return chosen[:, :, lon, cut].reshape(len(members), -1, chosen[..., cut].shape[-1])

    parts = lane_parts(channels)
    pieces = [slice(start * LANES, (start + count) * LANES) for start, count in parts]
    cuts = [count * LANES for _, count in parts]
    lanes = [slice(0, channels)] * 2 + pieces
    groups_of = [groups[0], groups[1]] + [groups[2]] * len(parts)
    head, tail = slice(0, edge), slice(width - edge, width)
    firsts = [pick(pairs, groups[0], head, lanes[0])]
    lasts = [pick(pairs, groups[0], tail, lanes[0])]
    pairs, _, _ = lax.optimization_barrier((pairs, firsts[0], lasts[0]))
    firsts += [pick(pairs, members, head, cut) for members, cut in zip(groups_of[1:], lanes[1:])]
    lasts += [pick(pairs, members, tail, cut) for members, cut in zip(groups_of[1:], lanes[1:])]
    tables = (forward, inverse)
    out = None
    for layer in range(blocks):
        final = layer + 1 == blocks
        halos = [zonal_halos(f, b, half) for f, b in zip(firsts, lasts)]

        def near(start):
            source, row = mid_of[start]
            return mids[source][row : row + rim]

        def far(start):
            at = group_of[start][1]
            return jnp.concatenate([halo[at : at + rim] for halo in halos[0]], axis=1)

        low = [step_rows(near(rows - rim), 1), step_rows(far(rows - rim), 1)]
        high = [step_rows(near(0), -1), step_rows(far(0), -1)]

        def own(row, used_mids, used):
            k, at = group_of[row]
            source, mid_row = mid_of[row]
            n = len(used_mids)
            j = used.index(k)
            every = slice(None)
            middle = (used_mids.index(source), mid_row, every)
            return (row + rim, [(n + j, at, every), middle, (n + len(used) + j, at, every)])

        def lat(number, at, place):
            return (
                place,
                [
                    (number + 1, at, slice(0, half)),
                    (number, at, slice(None)),
                    (number + 1, at, slice(half, 2 * half)),
                ],
            )

        used = [0, 1]
        used_mids = sorted({mid_of[row][0] for k in used for row in groups[k]})
        sources = [mids[s] for s in used_mids] + [halos[k][side] for side in (0, 1) for k in used]
        sources = sources + low + high
        n = len(sources)
        outer = (
            [lat(n - 4, r, r) for r in range(rim)]
            + [own(row, used_mids, used) for row in range(2 * rim)]
            + [own(row, used_mids, used) for row in range(rows - 2 * rim, rows)]
            + [lat(n - 2, r, rows + rim + r) for r in range(rim)]
        )
        windows = [(0, rim), (3 * rim, rim)]
        mixed_outer = [
            convolve(quad, tables, factors[layer], sources, outer, windows, (0, channels // LANES))
        ]
        used = [0, 1, 2]
        used_mids = sorted({source for source, _ in mid_of.values()})
        inner = [own(row, used_mids, used) for row in range(rows)]
        mixed_inner = []
        for k, part in enumerate(parts):
            chosen = [halos[0], halos[1], halos[2 + k]]
            sources = [mids[s] for s in used_mids] + [pair[side] for side in (0, 1) for pair in chosen]
            mixed_inner.append(
                convolve(quad, tables, factors[layer], sources, inner, [(0, rows - 2 * rim)], part)
            )
        weights = (gains[layer], input_weight[layer], output_weight[layer])
        count = rows // 2
        if final:
            (out,) = mlp(*weights, mixed_outer, [([0], 0), ([1], rows - 2)], rows, 0)
            steps = [([p], 2 * p + rim) for p in range(count - 2)]
            (out,) = mlp(*weights, mixed_inner, steps, rows, 0, kept=out)
        else:
            outs = [mlp(*weights, mixed_outer, [([0], 0), ([1], 2)], 2 * rim, edge, [channels])]
            outs.append(mlp(*weights, mixed_inner, [([0], 0), ([count - 3], 2)], 2 * rim, edge, [channels]))
            steps = [([p + 1], 2 * p) for p in range(count - 4)]
            outs.append(mlp(*weights, mixed_inner, steps, rows - 4 * rim, edge, cuts))
            mids = [o[0] for o in outs]
            mid_of = group_of
            firsts = [f for o in outs for f in o[1::2]]
            lasts = [b for o in outs for b in o[2::2]]
    return jnp.swapaxes(out, 1, 2)[None]


def solution(mesh):
    in_specs = (P(None, "lat", None, "lon"), P(), P(), P(), P())
    out_specs = P(None, "lat", None, "lon")
    return jax.shard_map(body, mesh=mesh, in_specs=in_specs, out_specs=out_specs, check_vma=False)
```

```python
import functools
import math

import jax
import jax.numpy as jnp
import numpy as np
from jax import lax
from jax.experimental import pallas as pl
from jax.experimental.pallas import tpu as pltpu
from jax.sharding import PartitionSpec as P


LANES = 128
PACK = 16
SUBLANES = 8


def bases(width, taps):
    length = -(-(width + taps) // (2 * PACK)) * 2 * PACK
    odd = 2 * np.arange(length // 2) + 1

    def wave(points):
        angle = np.pi / length * (points[:, None] * odd[None, :] % (2 * length))
        return np.concatenate([np.cos(angle), -np.sin(angle)], axis=1)

    forward = wave(np.arange(width + taps)).T
    inverse = 2.0 / length * wave(taps + np.arange(width))
    tap_basis = wave(np.arange(taps)).T
    return tuple(jnp.asarray(a, jnp.bfloat16) for a in (forward, inverse, tap_basis))


def gelu(values):
    return 0.5 * values * (1.0 + lax.erf(values * math.sqrt(0.5)))


def conv_kernel(*refs, windows, row_refs, counts, begin, lanes):
    quad, forward, inverse, factors = refs[:4]
    sources = refs[4 : 4 + counts]
    out, spectra, product = refs[4 + counts :]
    step = pl.program_id(0)
    part = out.shape[2]

    def block_of(ref):
        offset = 0 if ref.shape[2] == part else begin
        return pl.ds(pl.multiple_of((step + offset) * lanes, lanes), lanes)

    ours = [block_of(ref) for ref in sources]
    freqs = forward.shape[0] // 2
    every = len(row_refs)
    taps_r = factors.shape[0]

    def row(g):
        return jnp.concatenate([sources[s][at, lon, ours[s]] for s, at, lon in row_refs[g][1]], axis=0)

    for g in range(0, every, 2):
        two = jnp.concatenate([row(g), row(g + 1)], axis=1)
        result = jnp.dot(forward[...], two, preferred_element_type=jnp.float32)
        for j in range(2):
            spectra[g + j] = result[:, j * lanes : (j + 1) * lanes] * quad[row_refs[g + j][0]]

    def block(f, carry):
        start = pl.multiple_of(f * SUBLANES, SUBLANES)
        re = pl.ds(start, SUBLANES)
        im = pl.ds(pl.multiple_of(freqs + start, SUBLANES), SUBLANES)
        fr = [factors[r, re] for r in range(taps_r)]
        fi = [factors[r, im] for r in range(taps_r)]
        fd = [b - a for a, b in zip(fr, fi)]
        fs = [b + a for a, b in zip(fr, fi)]
        h = 0
        for first, count in windows:
            xr = [spectra[first + g, re] for g in range(taps_r - 1)]
            xi = [spectra[first + g, im] for g in range(taps_r - 1)]
            xs = [a + b for a, b in zip(xr, xi)]
            for k in range(count):
                xr.append(spectra[first + k + taps_r - 1, re])
                xi.append(spectra[first + k + taps_r - 1, im])
                xs.append(xr[-1] + xi[-1])
                both, up, down = xs[0] * fr[0], xr[0] * fd[0], xi[0] * fs[0]
                for r in range(1, taps_r):
                    both, up, down = both + xs[r] * fr[r], up + xr[r] * fd[r], down + xi[r] * fs[r]
                here = slice(h * lanes, (h + 1) * lanes)
                product[re, here] = both - down
                product[im, here] = both + up
                for window in (xr, xi, xs):
                    window.pop(0)
                h += 1
        return carry

    lax.fori_loop(0, freqs // SUBLANES, block, 0, unroll=4)
    own = [row_refs[first + taps_r // 2 + k][1] for first, count in windows for k in range(count)]
    for h in range(0, len(own), 2):
        two = slice(h * lanes, (h + 2) * lanes)
        conv = jnp.dot(inverse[...], product[:, two].astype(jnp.bfloat16), preferred_element_type=jnp.float32)
        for j in range(2):
            source, at, _ = own[h + j][1]
            value = sources[source][at, :, ours[source]].astype(jnp.float32)
            out[h + j, :, block_of(out)] = (value + gelu(conv[:, j * lanes : (j + 1) * lanes])).astype(out.dtype)


def convolve(quad, tables, factors, sources, rows, windows, part):
    forward, inverse = tables
    taps_r, length, _ = factors.shape
    start, blocks = part
    out_rows = sum(count for _, count in windows)
    width = inverse.shape[0]
    lanes = blocks * LANES

    held = pl.BlockSpec(memory_space=pltpu.VMEM)
    out = jax.ShapeDtypeStruct((out_rows, width, lanes), jnp.bfloat16)
    kernel = functools.partial(
        conv_kernel, windows=windows, row_refs=rows, counts=len(sources), begin=start, lanes=LANES
    )
    return pl.pallas_call(
        kernel,
        grid=(blocks,),
        out_shape=out,
        in_specs=[
            pl.BlockSpec(memory_space=pltpu.SMEM),
            held,
            held,
            pl.BlockSpec((taps_r, length, LANES), lambda i: (0, 0, i + start)),
        ]
        + [held] * len(sources),
        out_specs=held,
        scratch_shapes=[
            pltpu.VMEM((len(rows), length, LANES), jnp.float32),
            pltpu.VMEM((length, out_rows * LANES), jnp.float32),
        ],
        compiler_params=pltpu.CompilerParams(vmem_limit_bytes=20 << 20),
        cost_estimate=pl.CostEstimate(
            flops=2 * lanes * length * (len(rows) * forward.shape[1] + out_rows * width),
            bytes_accessed=2 * lanes * (len(rows) * forward.shape[1] + 2 * taps_r * length),
            transcendentals=out_rows * lanes * width,
        ),
        name="zonal_conv",
    )(quad, forward, inverse, factors, *sources)


def mlp_kernel(gain, w_in, w_out, *refs, half, kept, parts, together):
    mixed = refs[: parts * together]
    refs = refs[parts * together + kept :]
    count, width, _ = mixed[0].shape
    channels, hidden_units = w_in.shape
    totals, normed = [], []
    for t in range(together):
        pieces = mixed[t * parts : (t + 1) * parts]
        values = [m[...].reshape(count * width, m.shape[2]).astype(jnp.float32) for m in pieces]
        values = values[0] if parts == 1 else jnp.concatenate(values, axis=1)
        average = jnp.mean(values, axis=1, keepdims=True)
        centred = values - average
        variance = jnp.mean(jnp.square(centred), axis=1, keepdims=True)
        normed.append((centred * lax.rsqrt(variance + 1e-05) * gain[...]).astype(jnp.bfloat16))
        totals.append(values)
    normed = jnp.concatenate(normed, axis=0)
    total = jnp.concatenate(totals, axis=0)
    step = hidden_units
    for f in range(0, hidden_units, step):
        hidden = jnp.dot(normed, w_in[:, f : f + step], preferred_element_type=jnp.float32)
        hidden = gelu(hidden).astype(jnp.bfloat16)
        total = total + jnp.dot(hidden, w_out[f : f + step], preferred_element_type=jnp.float32)
    result = total.astype(jnp.bfloat16).reshape(together * count, width, channels)
    refs[0][...] = result
    start = 0
    for first, last in zip(refs[1::2], refs[2::2]):
        here = slice(start, start + first.shape[2])
        first[...] = result[:, :half, here]
        last[...] = result[:, width - half :, here]
        start += first.shape[2]


def mlp(gain, w_in, w_out, mixed, steps, out_rows, edge, cuts=(), kept=None):
    width = mixed[0].shape[1]
    channels, hidden_units = w_in.shape
    together = len(steps[0][0])

    def chosen(values):
        def index(i):
            at = values[0]
            for k in range(1, len(values)):
                at = at + (values[k] - values[k - 1]) * (i >= k).astype(jnp.int32)
            return (at, 0, 0)

        return index

    def whole(array):
        return pl.BlockSpec(array.shape, lambda i: (0,) * array.ndim)

    def given(lon, lanes):
        sizes = (pl.Element(2 * together), pl.Element(lon), pl.Element(lanes))
        return pl.BlockSpec(sizes, chosen([row for _, row in steps]))

    lasts = [(width, channels)] + [(edge, cut) for cut in cuts for _ in range(2)]
    extra = [] if kept is None else [kept]
    return pl.pallas_call(
        functools.partial(mlp_kernel, half=edge, kept=len(extra), parts=len(mixed), together=together),
        grid=(len(steps),),
        out_shape=[jax.ShapeDtypeStruct((out_rows, *last), jnp.bfloat16) for last in lasts],
        in_specs=[whole(gain), whole(w_in), whole(w_out)]
        + [
            pl.BlockSpec((2, *m.shape[1:]), chosen([pairs[t] for pairs, _ in steps]))
            for t in range(together)
            for m in mixed
        ]
        + [pl.BlockSpec(memory_space=pl.ANY) for _ in extra],
        out_specs=[given(*last) for last in lasts],
        input_output_aliases={3 + together * len(mixed): 0} if extra else {},
        compiler_params=pltpu.CompilerParams(vmem_limit_bytes=20 << 20),
        cost_estimate=pl.CostEstimate(
            flops=8 * len(steps) * together * width * channels * hidden_units,
            bytes_accessed=8 * len(steps) * together * width * channels + 4 * channels * hidden_units,
            transcendentals=2 * len(steps) * together * width * hidden_units,
        ),
        name="channel_mlp",
    )(gain, w_in, w_out, *(list(mixed) * together), *extra)


def rotate(block, axis, hops):
    count = lax.axis_size(axis)
    return lax.ppermute(block, axis, [(i, (i + hops) % count) for i in range(count)])


def zonal_halos(first, last, half):
    width = first.shape[1]
    lefts, rights, hops, missing = [], [], 1, half
    while missing > 0:
        take = min(width, missing)
        lefts.insert(0, rotate(last[:, width - take :], "lon", hops))
        rights.append(rotate(first[:, :take], "lon", -hops))
        missing -= take
        hops += 1
    if len(lefts) == 1:
        return lefts[0], rights[0]
    return jnp.concatenate(lefts, axis=1), jnp.concatenate(rights, axis=1)


def step_rows(block, hops):
    count = lax.axis_size("lat")
    pairs = [(i, i + hops) for i in range(count) if 0 <= i + hops < count]
    return lax.ppermute(block, "lat", pairs)


def lane_parts(channels):
    units = channels // LANES
    least = max(1, units // 5)
    sizes = [(units - least + 1) // 2, (units - least) // 2, least]
    return [(sum(sizes[:k]), size) for k, size in enumerate(sizes) if size]


def body(ocean_state, zonal_kernel, norm_gain, input_weight, output_weight):
    blocks, kernel_rows, taps, channels = zonal_kernel.shape
    _, rows, _, width = ocean_state.shape
    rim = kernel_rows // 2
    half = taps // 2
    edge = min(half, width)
    forward, inverse, tap_basis = bases(width, taps)
    total_rows = rows * lax.axis_size("lat")
    index = lax.axis_index("lat") * rows - rim + jnp.arange(rows + 2 * rim, dtype=jnp.int32)
    quad = jnp.sin(jnp.pi * (index.astype(jnp.float32) + 0.5) / total_rows)
    quad = jnp.where((index >= 0) & (index < total_rows), quad, 0.0)
    factors = []
    for layer in range(blocks):
        taps_of = zonal_kernel[layer]
        factors.append(jnp.einsum("kt,rtc->rkc", tap_basis, taps_of, preferred_element_type=jnp.float32))
    gains = norm_gain.astype(jnp.float32)[:, None, :]

    groups = [
        list(range(rim)) + list(range(rows - rim, rows)),
        list(range(rim, 2 * rim)) + list(range(rows - 2 * rim, rows - rim)),
        list(range(2 * rim, rows - 2 * rim)),
    ]
    group_of = {row: (k, at) for k, members in enumerate(groups) for at, row in enumerate(members)}
    state = jnp.swapaxes(ocean_state[0], 1, 2)
    mids = [state]
    mid_of = {row: (0, row) for row in range(rows)}

    pairs = state.reshape(rows // rim, rim, width, channels)

    def pick(pairs, members, lon, cut):
        first, last = members[0] // rim, members[-1] // rim
        chosen = pairs[first : last + 1 : max(1, (last - first) // (len(members) // rim - 1))]
        return chosen[:, :, lon, cut].reshape(len(members), -1, chosen[..., cut].shape[-1])

    parts = lane_parts(channels)
    pieces = [slice(start * LANES, (start + count) * LANES) for start, count in parts]
    cuts = [count * LANES for _, count in parts]
    lanes = [slice(0, channels)] * 2 + pieces
    groups_of = [groups[0], groups[1]] + [groups[2]] * len(parts)
    head, tail = slice(0, edge), slice(width - edge, width)
    firsts = [pick(pairs, groups[0], head, lanes[0])]
    lasts = [pick(pairs, groups[0], tail, lanes[0])]
    pairs, _, _ = lax.optimization_barrier((pairs, firsts[0], lasts[0]))
    firsts += [pick(pairs, members, head, cut) for members, cut in zip(groups_of[1:], lanes[1:])]
    lasts += [pick(pairs, members, tail, cut) for members, cut in zip(groups_of[1:], lanes[1:])]
    tables = (forward, inverse)
    out = None
    for layer in range(blocks):
        final = layer + 1 == blocks
        halos = [zonal_halos(f, b, half) for f, b in zip(firsts, lasts)]

        def near(start):
            source, row = mid_of[start]
            return mids[source][row : row + rim]

        def far(start):
            at = group_of[start][1]
            return jnp.concatenate([halo[at : at + rim] for halo in halos[0]], axis=1)

        low = [step_rows(near(rows - rim), 1), step_rows(far(rows - rim), 1)]
        high = [step_rows(near(0), -1), step_rows(far(0), -1)]

        def own(row, used_mids, used):
            k, at = group_of[row]
            source, mid_row = mid_of[row]
            n = len(used_mids)
            j = used.index(k)
            every = slice(None)
            middle = (used_mids.index(source), mid_row, every)
            return (row + rim, [(n + j, at, every), middle, (n + len(used) + j, at, every)])

        def lat(number, at, place):
            return (
                place,
                [
                    (number + 1, at, slice(0, half)),
                    (number, at, slice(None)),
                    (number + 1, at, slice(half, 2 * half)),
                ],
            )

        used = [0, 1]
        used_mids = sorted({mid_of[row][0] for k in used for row in groups[k]})
        sources = [mids[s] for s in used_mids] + [halos[k][side] for side in (0, 1) for k in used]
        sources = sources + low + high
        n = len(sources)
        outer = (
            [lat(n - 4, r, r) for r in range(rim)]
            + [own(row, used_mids, used) for row in range(2 * rim)]
            + [own(row, used_mids, used) for row in range(rows - 2 * rim, rows)]
            + [lat(n - 2, r, rows + rim + r) for r in range(rim)]
        )
        windows = [(0, rim), (3 * rim, rim)]
        mixed_outer = [
            convolve(quad, tables, factors[layer], sources, outer, windows, (0, channels // LANES))
        ]
        used = [0, 1, 2]
        used_mids = sorted({source for source, _ in mid_of.values()})
        inner = [own(row, used_mids, used) for row in range(rows)]
        mixed_inner = []
        for k, part in enumerate(parts):
            chosen = [halos[0], halos[1], halos[2 + k]]
            sources = [mids[s] for s in used_mids] + [pair[side] for side in (0, 1) for pair in chosen]
            mixed_inner.append(
                convolve(quad, tables, factors[layer], sources, inner, [(0, rows - 2 * rim)], part)
            )
        weights = (gains[layer], input_weight[layer], output_weight[layer])
        count = rows // 2
        if final:
            (out,) = mlp(*weights, mixed_outer, [([0], 0), ([1], rows - 2)], rows, 0)
            steps = [([p], 2 * p + rim) for p in range(count - 2)]
            (out,) = mlp(*weights, mixed_inner, steps, rows, 0, kept=out)
        else:
            outs = [mlp(*weights, mixed_outer, [([0], 0), ([1], 2)], 2 * rim, edge, [channels])]
            outs.append(mlp(*weights, mixed_inner, [([0], 0), ([count - 3], 2)], 2 * rim, edge, [channels]))
            steps = [([p + 1], 2 * p) for p in range(count - 4)]
            outs.append(mlp(*weights, mixed_inner, steps, rows - 4 * rim, edge, cuts))
            mids = [o[0] for o in outs]
            mid_of = group_of
            firsts = [f for o in outs for f in o[1::2]]
            lasts = [b for o in outs for b in o[2::2]]
    return jnp.swapaxes(out, 1, 2)[None]


def solution(mesh):
    in_specs = (P(None, "lat", None, "lon"), P(), P(), P(), P())
    out_specs = P(None, "lat", None, "lon")
    return jax.shard_map(body, mesh=mesh, in_specs=in_specs, out_specs=out_specs, check_vma=False)
```

```python
import functools
import math

import jax
import jax.numpy as jnp
import numpy as np
from jax import lax
from jax.experimental import pallas as pl
from jax.experimental.pallas import tpu as pltpu
from jax.sharding import PartitionSpec as P


LANES = 128
PACK = 16
SUBLANES = 8


def bases(width, taps):
    length = -(-(width + taps) // (2 * PACK)) * 2 * PACK
    odd = 2 * np.arange(length // 2) + 1

    def wave(points):
        angle = np.pi / length * (points[:, None] * odd[None, :] % (2 * length))
        return np.concatenate([np.cos(angle), -np.sin(angle)], axis=1)

    forward = wave(np.arange(width + taps)).T
    inverse = 2.0 / length * wave(taps + np.arange(width))
    tap_basis = wave(np.arange(taps)).T
    return tuple(jnp.asarray(a, jnp.bfloat16) for a in (forward, inverse, tap_basis))


def gelu(values):
    return 0.5 * values * (1.0 + lax.erf(values * math.sqrt(0.5)))


def conv_kernel(*refs, windows, row_refs, counts, begin, lanes):
    quad, forward, inverse, factors = refs[:4]
    sources = refs[4 : 4 + counts]
    out, spectra, product = refs[4 + counts :]
    step = pl.program_id(0)
    part = out.shape[2]

    def block_of(ref):
        offset = 0 if ref.shape[2] == part else begin
        return pl.ds(pl.multiple_of((step + offset) * lanes, lanes), lanes)

    ours = [block_of(ref) for ref in sources]
    freqs = forward.shape[0] // 2
    every = len(row_refs)
    taps_r = factors.shape[0]

    def row(g):
        return jnp.concatenate([sources[s][at, lon, ours[s]] for s, at, lon in row_refs[g][1]], axis=0)

    for g in range(0, every, 2):
        two = jnp.concatenate([row(g), row(g + 1)], axis=1)
        result = jnp.dot(forward[...], two, preferred_element_type=jnp.float32)
        for j in range(2):
            spectra[g + j] = result[:, j * lanes : (j + 1) * lanes] * quad[row_refs[g + j][0]]

    def block(f, carry):
        start = pl.multiple_of(f * SUBLANES, SUBLANES)
        re = pl.ds(start, SUBLANES)
        im = pl.ds(pl.multiple_of(freqs + start, SUBLANES), SUBLANES)
        fr = [factors[r, re] for r in range(taps_r)]
        fi = [factors[r, im] for r in range(taps_r)]
        fd = [b - a for a, b in zip(fr, fi)]
        fs = [b + a for a, b in zip(fr, fi)]
        h = 0
        for first, count in windows:
            xr = [spectra[first + g, re] for g in range(taps_r - 1)]
            xi = [spectra[first + g, im] for g in range(taps_r - 1)]
            xs = [a + b for a, b in zip(xr, xi)]
            for k in range(count):
                xr.append(spectra[first + k + taps_r - 1, re])
                xi.append(spectra[first + k + taps_r - 1, im])
                xs.append(xr[-1] + xi[-1])
                both, up, down = xs[0] * fr[0], xr[0] * fd[0], xi[0] * fs[0]
                for r in range(1, taps_r):
                    both, up, down = both + xs[r] * fr[r], up + xr[r] * fd[r], down + xi[r] * fs[r]
                here = slice(h * lanes, (h + 1) * lanes)
                product[re, here] = both - down
                product[im, here] = both + up
                for window in (xr, xi, xs):
                    window.pop(0)
                h += 1
        return carry

    lax.fori_loop(0, freqs // SUBLANES, block, 0, unroll=4)
    own = [row_refs[first + taps_r // 2 + k][1] for first, count in windows for k in range(count)]
    for h in range(0, len(own), 2):
        two = slice(h * lanes, (h + 2) * lanes)
        conv = jnp.dot(inverse[...], product[:, two].astype(jnp.bfloat16), preferred_element_type=jnp.float32)
        for j in range(2):
            source, at, _ = own[h + j][1]
            value = sources[source][at, :, ours[source]].astype(jnp.float32)
            out[h + j, :, block_of(out)] = (value + gelu(conv[:, j * lanes : (j + 1) * lanes])).astype(out.dtype)


def convolve(quad, tables, factors, sources, rows, windows, part):
    forward, inverse = tables
    taps_r, length, _ = factors.shape
    start, blocks = part
    out_rows = sum(count for _, count in windows)
    width = inverse.shape[0]
    lanes = blocks * LANES

    held = pl.BlockSpec(memory_space=pltpu.VMEM)
    out = jax.ShapeDtypeStruct((out_rows, width, lanes), jnp.bfloat16)
    kernel = functools.partial(
        conv_kernel, windows=windows, row_refs=rows, counts=len(sources), begin=start, lanes=LANES
    )
    return pl.pallas_call(
        kernel,
        grid=(blocks,),
        out_shape=out,
        in_specs=[
            pl.BlockSpec(memory_space=pltpu.SMEM),
            held,
            held,
            pl.BlockSpec((taps_r, length, LANES), lambda i: (0, 0, i + start)),
        ]
        + [held] * len(sources),
        out_specs=held,
        scratch_shapes=[
            pltpu.VMEM((len(rows), length, LANES), jnp.float32),
            pltpu.VMEM((length, out_rows * LANES), jnp.float32),
        ],
        compiler_params=pltpu.CompilerParams(vmem_limit_bytes=20 << 20),
        cost_estimate=pl.CostEstimate(
            flops=2 * lanes * length * (len(rows) * forward.shape[1] + out_rows * width),
            bytes_accessed=2 * lanes * (len(rows) * forward.shape[1] + 2 * taps_r * length),
            transcendentals=out_rows * lanes * width,
        ),
        name="zonal_conv",
    )(quad, forward, inverse, factors, *sources)


def mlp_kernel(gain, w_in, w_out, *refs, half, kept, parts, together):
    mixed = refs[: parts * together]
    refs = refs[parts * together + kept :]
    count, width, _ = mixed[0].shape
    channels, hidden_units = w_in.shape
    totals, normed = [], []
    for t in range(together):
        pieces = mixed[t * parts : (t + 1) * parts]
        values = [m[...].reshape(count * width, m.shape[2]).astype(jnp.float32) for m in pieces]
        values = values[0] if parts == 1 else jnp.concatenate(values, axis=1)
        average = jnp.mean(values, axis=1, keepdims=True)
        centred = values - average
        variance = jnp.mean(jnp.square(centred), axis=1, keepdims=True)
        normed.append((centred * lax.rsqrt(variance + 1e-05) * gain[...]).astype(jnp.bfloat16))
        totals.append(values)
    normed = jnp.concatenate(normed, axis=0)
    total = jnp.concatenate(totals, axis=0)
    step = hidden_units
    for f in range(0, hidden_units, step):
        hidden = jnp.dot(normed, w_in[:, f : f + step], preferred_element_type=jnp.float32)
        hidden = gelu(hidden).astype(jnp.bfloat16)
        total = total + jnp.dot(hidden, w_out[f : f + step], preferred_element_type=jnp.float32)
    result = total.astype(jnp.bfloat16).reshape(together * count, width, channels)
    refs[0][...] = result
    start = 0
    for first, last in zip(refs[1::2], refs[2::2]):
        here = slice(start, start + first.shape[2])
        first[...] = result[:, :half, here]
        last[...] = result[:, width - half :, here]
        start += first.shape[2]


def mlp(gain, w_in, w_out, mixed, steps, out_rows, edge, cuts=(), kept=None):
    width = mixed[0].shape[1]
    channels, hidden_units = w_in.shape
    together = len(steps[0][0])

    def chosen(values):
        def index(i):
            at = values[0]
            for k in range(1, len(values)):
                at = at + (values[k] - values[k - 1]) * (i >= k).astype(jnp.int32)
            return (at, 0, 0)

        return index

    def whole(array):
        return pl.BlockSpec(array.shape, lambda i: (0,) * array.ndim)

    def given(lon, lanes):
        sizes = (pl.Element(2 * together), pl.Element(lon), pl.Element(lanes))
        return pl.BlockSpec(sizes, chosen([row for _, row in steps]))

    lasts = [(width, channels)] + [(edge, cut) for cut in cuts for _ in range(2)]
    extra = [] if kept is None else [kept]
    return pl.pallas_call(
        functools.partial(mlp_kernel, half=edge, kept=len(extra), parts=len(mixed), together=together),
        grid=(len(steps),),
        out_shape=[jax.ShapeDtypeStruct((out_rows, *last), jnp.bfloat16) for last in lasts],
        in_specs=[whole(gain), whole(w_in), whole(w_out)]
        + [
            pl.BlockSpec((2, *m.shape[1:]), chosen([pairs[t] for pairs, _ in steps]))
            for t in range(together)
            for m in mixed
        ]
        + [pl.BlockSpec(memory_space=pl.ANY) for _ in extra],
        out_specs=[given(*last) for last in lasts],
        input_output_aliases={3 + together * len(mixed): 0} if extra else {},
        compiler_params=pltpu.CompilerParams(vmem_limit_bytes=20 << 20),
        cost_estimate=pl.CostEstimate(
            flops=8 * len(steps) * together * width * channels * hidden_units,
            bytes_accessed=8 * len(steps) * together * width * channels + 4 * channels * hidden_units,
            transcendentals=2 * len(steps) * together * width * hidden_units,
        ),
        name="channel_mlp",
    )(gain, w_in, w_out, *(list(mixed) * together), *extra)


def rotate(block, axis, hops):
    count = lax.axis_size(axis)
    return lax.ppermute(block, axis, [(i, (i + hops) % count) for i in range(count)])


def zonal_halos(first, last, half):
    width = first.shape[1]
    lefts, rights, hops, missing = [], [], 1, half
    while missing > 0:
        take = min(width, missing)
        lefts.insert(0, rotate(last[:, width - take :], "lon", hops))
        rights.append(rotate(first[:, :take], "lon", -hops))
        missing -= take
        hops += 1
    if len(lefts) == 1:
        return lefts[0], rights[0]
    return jnp.concatenate(lefts, axis=1), jnp.concatenate(rights, axis=1)


def step_rows(block, hops):
    count = lax.axis_size("lat")
    pairs = [(i, i + hops) for i in range(count) if 0 <= i + hops < count]
    return lax.ppermute(block, "lat", pairs)


def lane_parts(channels):
    units = channels // LANES
    least = max(1, units // 5)
    sizes = [(units - least + 1) // 2, (units - least) // 2, least]
    return [(sum(sizes[:k]), size) for k, size in enumerate(sizes) if size]


def body(ocean_state, zonal_kernel, norm_gain, input_weight, output_weight):
    blocks, kernel_rows, taps, channels = zonal_kernel.shape
    _, rows, _, width = ocean_state.shape
    rim = kernel_rows // 2
    half = taps // 2
    edge = min(half, width)
    forward, inverse, tap_basis = bases(width, taps)
    total_rows = rows * lax.axis_size("lat")
    index = lax.axis_index("lat") * rows - rim + jnp.arange(rows + 2 * rim, dtype=jnp.int32)
    quad = jnp.sin(jnp.pi * (index.astype(jnp.float32) + 0.5) / total_rows)
    quad = jnp.where((index >= 0) & (index < total_rows), quad, 0.0)
    factors = []
    for layer in range(blocks):
        taps_of = zonal_kernel[layer]
        factors.append(jnp.einsum("kt,rtc->rkc", tap_basis, taps_of, preferred_element_type=jnp.float32))
    gains = norm_gain.astype(jnp.float32)[:, None, :]

    groups = [
        list(range(rim)) + list(range(rows - rim, rows)),
        list(range(rim, 2 * rim)) + list(range(rows - 2 * rim, rows - rim)),
        list(range(2 * rim, rows - 2 * rim)),
    ]
    group_of = {row: (k, at) for k, members in enumerate(groups) for at, row in enumerate(members)}
    state = jnp.swapaxes(ocean_state[0], 1, 2)
    mids = [state]
    mid_of = {row: (0, row) for row in range(rows)}

    pairs = state.reshape(rows // rim, rim, width, channels)

    def pick(pairs, members, lon, cut):
        first, last = members[0] // rim, members[-1] // rim
        stride = max(1, (last - first) // (len(members) // rim - 1))
        low, high = (first, 0, lon.start, cut.start), (last + 1, rim, lon.stop, cut.stop)
        chosen = lax.slice(pairs, low, high, (stride, 1, 1, 1))
        return chosen.reshape(len(members), *chosen.shape[2:])

    parts = lane_parts(channels)
    pieces = [slice(start * LANES, (start + count) * LANES) for start, count in parts]
    cuts = [count * LANES for _, count in parts]
    lanes = [slice(0, channels)] * 2 + pieces
    groups_of = [groups[0], groups[1]] + [groups[2]] * len(parts)
    head, tail = slice(0, edge), slice(width - edge, width)
    lasts = [pick(pairs, groups[0], tail, lanes[0])]
    pairs, _ = lax.optimization_barrier((pairs, lasts[0]))
    firsts = [pick(pairs, groups[0], head, lanes[0])]
    pairs, _ = lax.optimization_barrier((pairs, firsts[0]))
    firsts += [pick(pairs, members, head, cut) for members, cut in zip(groups_of[1:], lanes[1:])]
    lasts += [pick(pairs, members, tail, cut) for members, cut in zip(groups_of[1:], lanes[1:])]
    tables = (forward, inverse)
    out = None
    for layer in range(blocks):
        final = layer + 1 == blocks
        halos = [zonal_halos(f, b, half) for f, b in zip(firsts, lasts)]

        def near(start):
            source, row = mid_of[start]
            return mids[source][row : row + rim]

        def far(start):
            at = group_of[start][1]
            return jnp.concatenate([halo[at : at + rim] for halo in halos[0]], axis=1)

        low = [step_rows(near(rows - rim), 1), step_rows(far(rows - rim), 1)]
        high = [step_rows(near(0), -1), step_rows(far(0), -1)]

        def own(row, used_mids, used):
            k, at = group_of[row]
            source, mid_row = mid_of[row]
            n = len(used_mids)
            j = used.index(k)
            every = slice(None)
            middle = (used_mids.index(source), mid_row, every)
            return (row + rim, [(n + j, at, every), middle, (n + len(used) + j, at, every)])

        def lat(number, at, place):
            return (
                place,
                [
                    (number + 1, at, slice(0, half)),
                    (number, at, slice(None)),
                    (number + 1, at, slice(half, 2 * half)),
                ],
            )

        used = [0, 1]
        used_mids = sorted({mid_of[row][0] for k in used for row in groups[k]})
        sources = [mids[s] for s in used_mids] + [halos[k][side] for side in (0, 1) for k in used]
        sources = sources + low + high
        n = len(sources)
        outer = (
            [lat(n - 4, r, r) for r in range(rim)]
            + [own(row, used_mids, used) for row in range(2 * rim)]
            + [own(row, used_mids, used) for row in range(rows - 2 * rim, rows)]
            + [lat(n - 2, r, rows + rim + r) for r in range(rim)]
        )
        windows = [(0, rim), (3 * rim, rim)]
        mixed_outer = [
            convolve(quad, tables, factors[layer], sources, outer, windows, (0, channels // LANES))
        ]
        used = [0, 1, 2]
        used_mids = sorted({source for source, _ in mid_of.values()})
        inner = [own(row, used_mids, used) for row in range(rows)]
        mixed_inner = []
        for k, part in enumerate(parts):
            chosen = [halos[0], halos[1], halos[2 + k]]
            sources = [mids[s] for s in used_mids] + [pair[side] for side in (0, 1) for pair in chosen]
            mixed_inner.append(
                convolve(quad, tables, factors[layer], sources, inner, [(0, rows - 2 * rim)], part)
            )
        weights = (gains[layer], input_weight[layer], output_weight[layer])
        count = rows // 2
        if final:
            (out,) = mlp(*weights, mixed_outer, [([0], 0), ([1], rows - 2)], rows, 0)
            steps = [([p], 2 * p + rim) for p in range(count - 2)]
            (out,) = mlp(*weights, mixed_inner, steps, rows, 0, kept=out)
        else:
            outs = [mlp(*weights, mixed_outer, [([0], 0), ([1], 2)], 2 * rim, edge, [channels])]
            outs.append(mlp(*weights, mixed_inner, [([0], 0), ([count - 3], 2)], 2 * rim, edge, [channels]))
            steps = [([p + 1], 2 * p) for p in range(count - 4)]
            outs.append(mlp(*weights, mixed_inner, steps, rows - 4 * rim, edge, cuts))
            mids = [o[0] for o in outs]
            mid_of = group_of
            firsts = [f for o in outs for f in o[1::2]]
            lasts = [b for o in outs for b in o[2::2]]
    return jnp.swapaxes(out, 1, 2)[None]


def solution(mesh):
    in_specs = (P(None, "lat", None, "lon"), P(), P(), P(), P())
    out_specs = P(None, "lat", None, "lon")
    return jax.shard_map(body, mesh=mesh, in_specs=in_specs, out_specs=out_specs, check_vma=False)
```

```python
import functools
import math

import jax
import jax.numpy as jnp
import numpy as np
from jax import lax
from jax.experimental import pallas as pl
from jax.experimental.pallas import tpu as pltpu
from jax.sharding import PartitionSpec as P


LANES = 128
PACK = 16
SUBLANES = 8


def bases(width, taps):
    length = -(-(width + taps) // (2 * PACK)) * 2 * PACK
    odd = 2 * np.arange(length // 2) + 1

    def wave(points):
        angle = np.pi / length * (points[:, None] * odd[None, :] % (2 * length))
        return np.concatenate([np.cos(angle), -np.sin(angle)], axis=1)

    forward = wave(np.arange(width + taps)).T
    inverse = 2.0 / length * wave(taps + np.arange(width))
    tap_basis = wave(np.arange(taps)).T
    return tuple(jnp.asarray(a, jnp.bfloat16) for a in (forward, inverse, tap_basis))


def gelu(values):
    return 0.5 * values * (1.0 + lax.erf(values * math.sqrt(0.5)))


def conv_kernel(*refs, windows, row_refs, counts, begin, lanes):
    quad, forward, inverse, factors = refs[:4]
    sources = refs[4 : 4 + counts]
    out, spectra, product = refs[4 + counts :]
    step = pl.program_id(0)
    part = out.shape[2]

    def block_of(ref):
        offset = 0 if ref.shape[2] == part else begin
        return pl.ds(pl.multiple_of((step + offset) * lanes, lanes), lanes)

    ours = [block_of(ref) for ref in sources]
    freqs = forward.shape[0] // 2
    every = len(row_refs)
    taps_r = factors.shape[0]

    def row(g):
        return jnp.concatenate([sources[s][at, lon, ours[s]] for s, at, lon in row_refs[g][1]], axis=0)

    for g in range(0, every, 2):
        two = jnp.concatenate([row(g), row(g + 1)], axis=1)
        result = jnp.dot(forward[...], two, preferred_element_type=jnp.float32)
        for j in range(2):
            spectra[g + j] = result[:, j * lanes : (j + 1) * lanes] * quad[row_refs[g + j][0]]

    def block(f, carry):
        start = pl.multiple_of(f * SUBLANES, SUBLANES)
        re = pl.ds(start, SUBLANES)
        im = pl.ds(pl.multiple_of(freqs + start, SUBLANES), SUBLANES)
        fr = [factors[r, re] for r in range(taps_r)]
        fi = [factors[r, im] for r in range(taps_r)]
        fd = [b - a for a, b in zip(fr, fi)]
        fs = [b + a for a, b in zip(fr, fi)]
        h = 0
        for first, count in windows:
            xr = [spectra[first + g, re] for g in range(taps_r - 1)]
            xi = [spectra[first + g, im] for g in range(taps_r - 1)]
            xs = [a + b for a, b in zip(xr, xi)]
            for k in range(count):
                xr.append(spectra[first + k + taps_r - 1, re])
                xi.append(spectra[first + k + taps_r - 1, im])
                xs.append(xr[-1] + xi[-1])
                both, up, down = xs[0] * fr[0], xr[0] * fd[0], xi[0] * fs[0]
                for r in range(1, taps_r):
                    both, up, down = both + xs[r] * fr[r], up + xr[r] * fd[r], down + xi[r] * fs[r]
                here = slice(h * lanes, (h + 1) * lanes)
                product[re, here] = both - down
                product[im, here] = both + up
                for window in (xr, xi, xs):
                    window.pop(0)
                h += 1
        return carry

    lax.fori_loop(0, freqs // SUBLANES, block, 0, unroll=4)
    own = [row_refs[first + taps_r // 2 + k][1] for first, count in windows for k in range(count)]
    for h in range(0, len(own), 2):
        two = slice(h * lanes, (h + 2) * lanes)
        conv = jnp.dot(inverse[...], product[:, two].astype(jnp.bfloat16), preferred_element_type=jnp.float32)
        for j in range(2):
            source, at, _ = own[h + j][1]
            value = sources[source][at, :, ours[source]].astype(jnp.float32)
            out[h + j, :, block_of(out)] = (value + gelu(conv[:, j * lanes : (j + 1) * lanes])).astype(out.dtype)


def convolve(quad, tables, factors, sources, rows, windows, part):
    forward, inverse = tables
    taps_r, length, _ = factors.shape
    start, blocks = part
    out_rows = sum(count for _, count in windows)
    width = inverse.shape[0]
    lanes = blocks * LANES

    held = pl.BlockSpec(memory_space=pltpu.VMEM)
    out = jax.ShapeDtypeStruct((out_rows, width, lanes), jnp.bfloat16)
    kernel = functools.partial(
        conv_kernel, windows=windows, row_refs=rows, counts=len(sources), begin=start, lanes=LANES
    )
    return pl.pallas_call(
        kernel,
        grid=(blocks,),
        out_shape=out,
        in_specs=[
            pl.BlockSpec(memory_space=pltpu.SMEM),
            held,
            held,
            pl.BlockSpec((taps_r, length, LANES), lambda i: (0, 0, i + start)),
        ]
        + [held] * len(sources),
        out_specs=held,
        scratch_shapes=[
            pltpu.VMEM((len(rows), length, LANES), jnp.float32),
            pltpu.VMEM((length, out_rows * LANES), jnp.float32),
        ],
        compiler_params=pltpu.CompilerParams(vmem_limit_bytes=20 << 20),
        cost_estimate=pl.CostEstimate(
            flops=2 * lanes * length * (len(rows) * forward.shape[1] + out_rows * width),
            bytes_accessed=2 * lanes * (len(rows) * forward.shape[1] + 2 * taps_r * length),
            transcendentals=out_rows * lanes * width,
        ),
        name="zonal_conv",
    )(quad, forward, inverse, factors, *sources)


def mlp_kernel(gain, w_in, w_out, *refs, half, kept, parts, together):
    mixed = refs[: parts * together]
    given = refs[parts * together + kept :]
    count, width, _ = mixed[0].shape
    channels = w_in.shape[0]

    def load(t):
        pieces = mixed[t * parts : (t + 1) * parts]
        values = [m[...].reshape(count * width, m.shape[2]).astype(jnp.float32) for m in pieces]
        values = values[0] if parts == 1 else jnp.concatenate(values, axis=1)
        average = jnp.mean(values, axis=1, keepdims=True)
        centred = values - average
        variance = jnp.mean(jnp.square(centred), axis=1, keepdims=True)
        return values, (centred * lax.rsqrt(variance + 1e-05) * gain[...]).astype(jnp.bfloat16)

    following = load(0)
    for t in range(together):
        values, normed = following
        hidden = jnp.dot(normed, w_in[...], preferred_element_type=jnp.float32)
        hidden = gelu(hidden).astype(jnp.bfloat16)
        if t + 1 < together:
            following = load(t + 1)
        result = values + jnp.dot(hidden, w_out[...], preferred_element_type=jnp.float32)
        result = result.astype(jnp.bfloat16).reshape(count, width, channels)
        here = slice(t * count, (t + 1) * count)
        given[0][here] = result
        start = 0
        for first, last in zip(given[1::2], given[2::2]):
            cut = slice(start, start + first.shape[2])
            first[here] = result[:, :half, cut]
            last[here] = result[:, width - half :, cut]
            start += first.shape[2]


def mlp(gain, w_in, w_out, mixed, steps, out_rows, edge, cuts=(), kept=None):
    width = mixed[0].shape[1]
    channels, hidden_units = w_in.shape
    together = len(steps[0][0])

    def chosen(values):
        def index(i):
            at = values[0]
            for k in range(1, len(values)):
                at = at + (values[k] - values[k - 1]) * (i >= k).astype(jnp.int32)
            return (at, 0, 0)

        return index

    def whole(array):
        return pl.BlockSpec(array.shape, lambda i: (0,) * array.ndim)

    def given(lon, lanes):
        sizes = (pl.Element(2 * together), pl.Element(lon), pl.Element(lanes))
        return pl.BlockSpec(sizes, chosen([row for _, row in steps]))

    lasts = [(width, channels)] + [(edge, cut) for cut in cuts for _ in range(2)]
    extra = [] if kept is None else [kept]
    return pl.pallas_call(
        functools.partial(mlp_kernel, half=edge, kept=len(extra), parts=len(mixed), together=together),
        grid=(len(steps),),
        out_shape=[jax.ShapeDtypeStruct((out_rows, *last), jnp.bfloat16) for last in lasts],
        in_specs=[whole(gain), whole(w_in), whole(w_out)]
        + [
            pl.BlockSpec((2, *m.shape[1:]), chosen([pairs[t] for pairs, _ in steps]))
            for t in range(together)
            for m in mixed
        ]
        + [pl.BlockSpec(memory_space=pl.ANY) for _ in extra],
        out_specs=[given(*last) for last in lasts],
        input_output_aliases={3 + together * len(mixed): 0} if extra else {},
        compiler_params=pltpu.CompilerParams(vmem_limit_bytes=20 << 20),
        cost_estimate=pl.CostEstimate(
            flops=8 * len(steps) * together * width * channels * hidden_units,
            bytes_accessed=8 * len(steps) * together * width * channels + 4 * channels * hidden_units,
            transcendentals=2 * len(steps) * together * width * hidden_units,
        ),
        name="channel_mlp",
    )(gain, w_in, w_out, *(list(mixed) * together), *extra)


def edge_kernel(state, first, last, sems, *, spans):
    edge, width = first.shape[1], state.shape[1]
    copies = []
    for k, (row, at, count) in enumerate(spans):
        for side, (target, lon) in enumerate([(last, width - edge), (first, 0)]):
            source = state.at[pl.ds(row, count), pl.ds(lon, edge)]
            copy = pltpu.make_async_copy(source, target.at[pl.ds(at, count)], sems.at[2 * k + side])
            copy.start()
            copies.append(copy)
    for copy in copies:
        copy.wait()


def edges(state, spans, edge):
    rows = sum(count for _, _, count in spans)
    out = jax.ShapeDtypeStruct((rows, edge, state.shape[2]), state.dtype)
    return pl.pallas_call(
        functools.partial(edge_kernel, spans=spans),
        out_shape=[out, out],
        in_specs=[pl.BlockSpec(memory_space=pltpu.HBM)],
        out_specs=[pl.BlockSpec(memory_space=pltpu.VMEM)] * 2,
        scratch_shapes=[pltpu.SemaphoreType.DMA((2 * len(spans),))],
        compiler_params=pltpu.CompilerParams(vmem_limit_bytes=60 << 20),
        name="edges",
    )(state)


def rotate(block, axis, hops):
    count = lax.axis_size(axis)
    return lax.ppermute(block, axis, [(i, (i + hops) % count) for i in range(count)])


def zonal_halos(first, last, half):
    width = first.shape[1]
    lefts, rights, hops, missing = [], [], 1, half
    while missing > 0:
        take = min(width, missing)
        lefts.insert(0, rotate(last[:, width - take :], "lon", hops))
        rights.append(rotate(first[:, :take], "lon", -hops))
        missing -= take
        hops += 1
    if len(lefts) == 1:
        return lefts[0], rights[0]
    return jnp.concatenate(lefts, axis=1), jnp.concatenate(rights, axis=1)


def step_rows(block, hops):
    count = lax.axis_size("lat")
    pairs = [(i, i + hops) for i in range(count) if 0 <= i + hops < count]
    return lax.ppermute(block, "lat", pairs)


def lane_parts(channels):
    units = channels // LANES
    least = max(1, units // 5)
    sizes = [(units - least + 1) // 2, (units - least) // 2, least]
    return [(sum(sizes[:k]), size) for k, size in enumerate(sizes) if size]


def body(ocean_state, zonal_kernel, norm_gain, input_weight, output_weight):
    blocks, kernel_rows, taps, channels = zonal_kernel.shape
    _, rows, _, width = ocean_state.shape
    rim = kernel_rows // 2
    half = taps // 2
    edge = min(half, width)
    forward, inverse, tap_basis = bases(width, taps)
    total_rows = rows * lax.axis_size("lat")
    index = lax.axis_index("lat") * rows - rim + jnp.arange(rows + 2 * rim, dtype=jnp.int32)
    quad = jnp.sin(jnp.pi * (index.astype(jnp.float32) + 0.5) / total_rows)
    quad = jnp.where((index >= 0) & (index < total_rows), quad, 0.0)
    factors = []
    for layer in range(blocks):
        taps_of = zonal_kernel[layer]
        factors.append(jnp.einsum("kt,rtc->rkc", tap_basis, taps_of, preferred_element_type=jnp.float32))
    gains = norm_gain.astype(jnp.float32)[:, None, :]

    groups = [
        list(range(rim)) + list(range(rows - rim, rows)),
        list(range(rim, 2 * rim)) + list(range(rows - 2 * rim, rows - rim)),
        list(range(2 * rim, rows - 2 * rim)),
    ]
    group_of = {row: (k, at) for k, members in enumerate(groups) for at, row in enumerate(members)}
    state = jnp.swapaxes(ocean_state[0], 1, 2)
    mids = [state]
    mid_of = {row: (0, row) for row in range(rows)}

    pairs = state.reshape(rows // rim, rim, width, channels)

    def pick(pairs, members, lon, cut):
        first, last = members[0] // rim, members[-1] // rim
        stride = max(1, (last - first) // (len(members) // rim - 1))
        low, high = (first, 0, lon.start, cut.start), (last + 1, rim, lon.stop, cut.stop)
        chosen = lax.slice(pairs, low, high, (stride, 1, 1, 1))
        return chosen.reshape(len(members), *chosen.shape[2:])

    parts = lane_parts(channels)
    pieces = [slice(start * LANES, (start + count) * LANES) for start, count in parts]
    cuts = [count * LANES for _, count in parts]
    lanes = [slice(0, channels)] * 2 + pieces
    groups_of = [groups[0], groups[1]] + [groups[2]] * len(parts)
    head, tail = slice(0, edge), slice(width - edge, width)
    first, last = edges(state, [(0, 0, rim), (rows - rim, rim, rim)], edge)
    firsts, lasts = [first], [last]
    pairs, _ = lax.optimization_barrier((pairs, first[:1, :1, :1]))
    firsts += [pick(pairs, members, head, cut) for members, cut in zip(groups_of[1:], lanes[1:])]
    lasts += [pick(pairs, members, tail, cut) for members, cut in zip(groups_of[1:], lanes[1:])]
    tables = (forward, inverse)
    out = None
    for layer in range(blocks):
        final = layer + 1 == blocks
        halos = [zonal_halos(f, b, half) for f, b in zip(firsts, lasts)]

        def near(start):
            source, row = mid_of[start]
            return mids[source][row : row + rim]

        def far(start):
            at = group_of[start][1]
            return jnp.concatenate([halo[at : at + rim] for halo in halos[0]], axis=1)

        low = [step_rows(near(rows - rim), 1), step_rows(far(rows - rim), 1)]
        high = [step_rows(near(0), -1), step_rows(far(0), -1)]

        def own(row, used_mids, used):
            k, at = group_of[row]
            source, mid_row = mid_of[row]
            n = len(used_mids)
            j = used.index(k)
            every = slice(None)
            middle = (used_mids.index(source), mid_row, every)
            return (row + rim, [(n + j, at, every), middle, (n + len(used) + j, at, every)])

        def lat(number, at, place):
            return (
                place,
                [
                    (number + 1, at, slice(0, half)),
                    (number, at, slice(None)),
                    (number + 1, at, slice(half, 2 * half)),
                ],
            )

        used = [0, 1]
        used_mids = sorted({mid_of[row][0] for k in used for row in groups[k]})
        sources = [mids[s] for s in used_mids] + [halos[k][side] for side in (0, 1) for k in used]
        sources = sources + low + high
        n = len(sources)
        outer = (
            [lat(n - 4, r, r) for r in range(rim)]
            + [own(row, used_mids, used) for row in range(2 * rim)]
            + [own(row, used_mids, used) for row in range(rows - 2 * rim, rows)]
            + [lat(n - 2, r, rows + rim + r) for r in range(rim)]
        )
        windows = [(0, rim), (3 * rim, rim)]
        mixed_outer = [
            convolve(quad, tables, factors[layer], sources, outer, windows, (0, channels // LANES))
        ]
        used = [0, 1, 2]
        used_mids = sorted({source for source, _ in mid_of.values()})
        inner = [own(row, used_mids, used) for row in range(rows)]
        mixed_inner = []
        for k, part in enumerate(parts):
            chosen = [halos[0], halos[1], halos[2 + k]]
            sources = [mids[s] for s in used_mids] + [pair[side] for side in (0, 1) for pair in chosen]
            mixed_inner.append(
                convolve(quad, tables, factors[layer], sources, inner, [(0, rows - 2 * rim)], part)
            )
        weights = (gains[layer], input_weight[layer], output_weight[layer])
        count = rows // 2
        if final:
            (out,) = mlp(*weights, mixed_outer, [([0], 0), ([1], rows - 2)], rows, 0)
            steps = [([p, p + 1], 2 * p + rim) for p in range(0, count - 2, 2)]
            (out,) = mlp(*weights, mixed_inner, steps, rows, 0, kept=out)
        else:
            outs = [mlp(*weights, mixed_outer, [([0], 0), ([1], 2)], 2 * rim, edge, [channels])]
            outs.append(mlp(*weights, mixed_inner, [([0], 0), ([count - 3], 2)], 2 * rim, edge, [channels]))
            steps = [([p + 1], 2 * p) for p in range(count - 4)]
            outs.append(mlp(*weights, mixed_inner, steps, rows - 4 * rim, edge, cuts))
            mids = [o[0] for o in outs]
            mid_of = group_of
            firsts = [f for o in outs for f in o[1::2]]
            lasts = [b for o in outs for b in o[2::2]]
    return jnp.swapaxes(out, 1, 2)[None]


def solution(mesh):
    in_specs = (P(None, "lat", None, "lon"), P(), P(), P(), P())
    out_specs = P(None, "lat", None, "lon")
    return jax.shard_map(body, mesh=mesh, in_specs=in_specs, out_specs=out_specs, check_vma=False)
```

```python
import functools
import math

import jax
import jax.numpy as jnp
import numpy as np
from jax import lax
from jax.experimental import pallas as pl
from jax.experimental.pallas import tpu as pltpu
from jax.sharding import PartitionSpec as P


LANES = 128
PACK = 16
SUBLANES = 8


def bases(width, taps):
    length = -(-(width + taps) // (2 * PACK)) * 2 * PACK
    odd = 2 * np.arange(length // 2) + 1

    def wave(points):
        angle = np.pi / length * (points[:, None] * odd[None, :] % (2 * length))
        return np.concatenate([np.cos(angle), -np.sin(angle)], axis=1)

    forward = wave(np.arange(width + taps)).T
    inverse = 2.0 / length * wave(taps + np.arange(width))
    tap_basis = wave(np.arange(taps)).T
    return tuple(jnp.asarray(a, jnp.bfloat16) for a in (forward, inverse, tap_basis))


def gelu(values):
    return 0.5 * values * (1.0 + lax.erf(values * math.sqrt(0.5)))


def conv_kernel(*refs, windows, row_refs, counts, begin, lanes):
    quad, forward, inverse, factors = refs[:4]
    sources = refs[4 : 4 + counts]
    out, spectra, product = refs[4 + counts :]
    step = pl.program_id(0)
    part = out.shape[2]

    def block_of(ref):
        offset = 0 if ref.shape[2] == part else begin
        return pl.ds(pl.multiple_of((step + offset) * lanes, lanes), lanes)

    ours = [block_of(ref) for ref in sources]
    freqs = forward.shape[0] // 2
    every = len(row_refs)
    taps_r = factors.shape[0]

    def row(g):
        return jnp.concatenate([sources[s][at, lon, ours[s]] for s, at, lon in row_refs[g][1]], axis=0)

    for g in range(0, every, 2):
        two = jnp.concatenate([row(g), row(g + 1)], axis=1)
        result = jnp.dot(forward[...], two, preferred_element_type=jnp.float32)
        for j in range(2):
            spectra[g + j] = result[:, j * lanes : (j + 1) * lanes] * quad[row_refs[g + j][0]]

    def block(f, carry):
        start = pl.multiple_of(f * SUBLANES, SUBLANES)
        re = pl.ds(start, SUBLANES)
        im = pl.ds(pl.multiple_of(freqs + start, SUBLANES), SUBLANES)
        fr = [factors[r, re] for r in range(taps_r)]
        fi = [factors[r, im] for r in range(taps_r)]
        fd = [b - a for a, b in zip(fr, fi)]
        fs = [b + a for a, b in zip(fr, fi)]
        h = 0
        for first, count in windows:
            xr = [spectra[first + g, re] for g in range(taps_r - 1)]
            xi = [spectra[first + g, im] for g in range(taps_r - 1)]
            xs = [a + b for a, b in zip(xr, xi)]
            for k in range(count):
                xr.append(spectra[first + k + taps_r - 1, re])
                xi.append(spectra[first + k + taps_r - 1, im])
                xs.append(xr[-1] + xi[-1])
                both, up, down = xs[0] * fr[0], xr[0] * fd[0], xi[0] * fs[0]
                for r in range(1, taps_r):
                    both, up, down = both + xs[r] * fr[r], up + xr[r] * fd[r], down + xi[r] * fs[r]
                here = slice(h * lanes, (h + 1) * lanes)
                product[re, here] = both - down
                product[im, here] = both + up
                for window in (xr, xi, xs):
                    window.pop(0)
                h += 1
        return carry

    lax.fori_loop(0, freqs // SUBLANES, block, 0, unroll=4)
    own = [row_refs[first + taps_r // 2 + k][1] for first, count in windows for k in range(count)]
    for h in range(0, len(own), 2):
        two = slice(h * lanes, (h + 2) * lanes)
        conv = jnp.dot(inverse[...], product[:, two].astype(jnp.bfloat16), preferred_element_type=jnp.float32)
        for j in range(2):
            source, at, _ = own[h + j][1]
            value = sources[source][at, :, ours[source]].astype(jnp.float32)
            out[h + j, :, block_of(out)] = (value + gelu(conv[:, j * lanes : (j + 1) * lanes])).astype(out.dtype)


def convolve(quad, tables, factors, sources, rows, windows, part):
    forward, inverse = tables
    taps_r, length, _ = factors.shape
    start, blocks = part
    out_rows = sum(count for _, count in windows)
    width = inverse.shape[0]
    lanes = blocks * LANES

    held = pl.BlockSpec(memory_space=pltpu.VMEM)
    out = jax.ShapeDtypeStruct((out_rows, width, lanes), jnp.bfloat16)
    kernel = functools.partial(
        conv_kernel, windows=windows, row_refs=rows, counts=len(sources), begin=start, lanes=LANES
    )
    return pl.pallas_call(
        kernel,
        grid=(blocks,),
        out_shape=out,
        in_specs=[
            pl.BlockSpec(memory_space=pltpu.SMEM),
            held,
            held,
            pl.BlockSpec((taps_r, length, LANES), lambda i: (0, 0, i + start)),
        ]
        + [held] * len(sources),
        out_specs=held,
        scratch_shapes=[
            pltpu.VMEM((len(rows), length, LANES), jnp.float32),
            pltpu.VMEM((length, out_rows * LANES), jnp.float32),
        ],
        compiler_params=pltpu.CompilerParams(vmem_limit_bytes=20 << 20),
        cost_estimate=pl.CostEstimate(
            flops=2 * lanes * length * (len(rows) * forward.shape[1] + out_rows * width),
            bytes_accessed=2 * lanes * (len(rows) * forward.shape[1] + 2 * taps_r * length),
            transcendentals=out_rows * lanes * width,
        ),
        name="zonal_conv",
    )(quad, forward, inverse, factors, *sources)


def mlp_kernel(gain, w_in, w_out, *refs, half, kept, parts, together):
    mixed = refs[: parts * together]
    given = refs[parts * together + kept :]
    count, width, _ = mixed[0].shape
    channels = w_in.shape[0]

    def load(t):
        pieces = mixed[t * parts : (t + 1) * parts]
        values = [m[...].reshape(count * width, m.shape[2]).astype(jnp.float32) for m in pieces]
        values = values[0] if parts == 1 else jnp.concatenate(values, axis=1)
        average = jnp.mean(values, axis=1, keepdims=True)
        centred = values - average
        variance = jnp.mean(jnp.square(centred), axis=1, keepdims=True)
        return values, (centred * lax.rsqrt(variance + 1e-05) * gain[...]).astype(jnp.bfloat16)

    following = load(0)
    for t in range(together):
        values, normed = following
        hidden = jnp.dot(normed, w_in[...], preferred_element_type=jnp.float32)
        hidden = gelu(hidden).astype(jnp.bfloat16)
        if t + 1 < together:
            following = load(t + 1)
        result = values + jnp.dot(hidden, w_out[...], preferred_element_type=jnp.float32)
        result = result.astype(jnp.bfloat16).reshape(count, width, channels)
        here = slice(t * count, (t + 1) * count)
        given[0][here] = result
        start = 0
        for first, last in zip(given[1::2], given[2::2]):
            cut = slice(start, start + first.shape[2])
            first[here] = result[:, :half, cut]
            last[here] = result[:, width - half :, cut]
            start += first.shape[2]


def mlp(gain, w_in, w_out, mixed, steps, out_rows, edge, cuts=(), kept=None):
    width = mixed[0].shape[1]
    channels, hidden_units = w_in.shape
    together = len(steps[0][0])

    def chosen(values):
        def index(i):
            at = values[0]
            for k in range(1, len(values)):
                at = at + (values[k] - values[k - 1]) * (i >= k).astype(jnp.int32)
            return (at, 0, 0)

        return index

    def whole(array):
        return pl.BlockSpec(array.shape, lambda i: (0,) * array.ndim)

    def given(lon, lanes):
        sizes = (pl.Element(2 * together), pl.Element(lon), pl.Element(lanes))
        return pl.BlockSpec(sizes, chosen([row for _, row in steps]))

    lasts = [(width, channels)] + [(edge, cut) for cut in cuts for _ in range(2)]
    extra = [] if kept is None else [kept]
    return pl.pallas_call(
        functools.partial(mlp_kernel, half=edge, kept=len(extra), parts=len(mixed), together=together),
        grid=(len(steps),),
        out_shape=[jax.ShapeDtypeStruct((out_rows, *last), jnp.bfloat16) for last in lasts],
        in_specs=[whole(gain), whole(w_in), whole(w_out)]
        + [
            pl.BlockSpec((2, *m.shape[1:]), chosen([pairs[t] for pairs, _ in steps]))
            for t in range(together)
            for m in mixed
        ]
        + [pl.BlockSpec(memory_space=pl.ANY) for _ in extra],
        out_specs=[given(*last) for last in lasts],
        input_output_aliases={3 + together * len(mixed): 0} if extra else {},
        compiler_params=pltpu.CompilerParams(vmem_limit_bytes=20 << 20),
        cost_estimate=pl.CostEstimate(
            flops=8 * len(steps) * together * width * channels * hidden_units,
            bytes_accessed=8 * len(steps) * together * width * channels + 4 * channels * hidden_units,
            transcendentals=2 * len(steps) * together * width * hidden_units,
        ),
        name="channel_mlp",
    )(gain, w_in, w_out, *(list(mixed) * together), *extra)


def rotate(block, axis, hops):
    count = lax.axis_size(axis)
    return lax.ppermute(block, axis, [(i, (i + hops) % count) for i in range(count)])


def zonal_halos(first, last, half):
    width = first.shape[1]
    lefts, rights, hops, missing = [], [], 1, half
    while missing > 0:
        take = min(width, missing)
        lefts.insert(0, rotate(last[:, width - take :], "lon", hops))
        rights.append(rotate(first[:, :take], "lon", -hops))
        missing -= take
        hops += 1
    if len(lefts) == 1:
        return lefts[0], rights[0]
    return jnp.concatenate(lefts, axis=1), jnp.concatenate(rights, axis=1)


def step_rows(block, hops):
    count = lax.axis_size("lat")
    pairs = [(i, i + hops) for i in range(count) if 0 <= i + hops < count]
    return lax.ppermute(block, "lat", pairs)


def lane_parts(channels):
    units = channels // LANES
    least = max(1, units // 5)
    sizes = [(units - least + 1) // 2, (units - least) // 2, least]
    return [(sum(sizes[:k]), size) for k, size in enumerate(sizes) if size]


def body(ocean_state, zonal_kernel, norm_gain, input_weight, output_weight):
    blocks, kernel_rows, taps, channels = zonal_kernel.shape
    _, rows, _, width = ocean_state.shape
    rim = kernel_rows // 2
    half = taps // 2
    edge = min(half, width)
    forward, inverse, tap_basis = bases(width, taps)
    total_rows = rows * lax.axis_size("lat")
    index = lax.axis_index("lat") * rows - rim + jnp.arange(rows + 2 * rim, dtype=jnp.int32)
    quad = jnp.sin(jnp.pi * (index.astype(jnp.float32) + 0.5) / total_rows)
    quad = jnp.where((index >= 0) & (index < total_rows), quad, 0.0)
    factors = []
    for layer in range(blocks):
        taps_of = zonal_kernel[layer]
        factors.append(jnp.einsum("kt,rtc->rkc", tap_basis, taps_of, preferred_element_type=jnp.float32))
    gains = norm_gain.astype(jnp.float32)[:, None, :]

    groups = [
        list(range(rim)) + list(range(rows - rim, rows)),
        list(range(rim, 2 * rim)) + list(range(rows - 2 * rim, rows - rim)),
        list(range(2 * rim, rows - 2 * rim)),
    ]
    group_of = {row: (k, at) for k, members in enumerate(groups) for at, row in enumerate(members)}
    state = jnp.swapaxes(ocean_state[0], 1, 2)
    mids = [state]
    mid_of = {row: (0, row) for row in range(rows)}

    pairs = state.reshape(rows // rim, rim, width, channels)

    def pick(pairs, members, lon, cut):
        first, last = members[0] // rim, members[-1] // rim
        stride = max(1, (last - first) // (len(members) // rim - 1))
        low, high = (first, 0, lon.start, cut.start), (last + 1, rim, lon.stop, cut.stop)
        chosen = lax.slice(pairs, low, high, (stride, 1, 1, 1))
        return chosen.reshape(len(members), *chosen.shape[2:])

    parts = lane_parts(channels)
    pieces = [slice(start * LANES, (start + count) * LANES) for start, count in parts]
    cuts = [count * LANES for _, count in parts]
    lanes = [slice(0, channels)] * 2 + pieces
    groups_of = [groups[0], groups[1]] + [groups[2]] * len(parts)
    head, tail = slice(0, edge), slice(width - edge, width)
    lasts = [pick(pairs, groups[0], tail, lanes[0])]
    pairs, _ = lax.optimization_barrier((pairs, lasts[0]))
    firsts = [pick(pairs, groups[0], head, lanes[0])]
    pairs, _ = lax.optimization_barrier((pairs, firsts[0]))
    firsts += [pick(pairs, members, head, cut) for members, cut in zip(groups_of[1:], lanes[1:])]
    lasts += [pick(pairs, members, tail, cut) for members, cut in zip(groups_of[1:], lanes[1:])]
    tables = (forward, inverse)
    out = None
    for layer in range(blocks):
        final = layer + 1 == blocks
        halos = [zonal_halos(f, b, half) for f, b in zip(firsts, lasts)]

        def near(start):
            source, row = mid_of[start]
            return mids[source][row : row + rim]

        def far(start):
            at = group_of[start][1]
            return jnp.concatenate([halo[at : at + rim] for halo in halos[0]], axis=1)

        low = [step_rows(near(rows - rim), 1), step_rows(far(rows - rim), 1)]
        high = [step_rows(near(0), -1), step_rows(far(0), -1)]

        def own(row, used_mids, used):
            k, at = group_of[row]
            source, mid_row = mid_of[row]
            n = len(used_mids)
            j = used.index(k)
            every = slice(None)
            middle = (used_mids.index(source), mid_row, every)
            return (row + rim, [(n + j, at, every), middle, (n + len(used) + j, at, every)])

        def lat(number, at, place):
            return (
                place,
                [
                    (number + 1, at, slice(0, half)),
                    (number, at, slice(None)),
                    (number + 1, at, slice(half, 2 * half)),
                ],
            )

        used = [0, 1]
        used_mids = sorted({mid_of[row][0] for k in used for row in groups[k]})
        sources = [mids[s] for s in used_mids] + [halos[k][side] for side in (0, 1) for k in used]
        sources = sources + low + high
        n = len(sources)
        outer = (
            [lat(n - 4, r, r) for r in range(rim)]
            + [own(row, used_mids, used) for row in range(2 * rim)]
            + [own(row, used_mids, used) for row in range(rows - 2 * rim, rows)]
            + [lat(n - 2, r, rows + rim + r) for r in range(rim)]
        )
        windows = [(0, rim), (3 * rim, rim)]
        mixed_outer = [
            convolve(quad, tables, factors[layer], sources, outer, windows, (0, channels // LANES))
        ]
        used = [0, 1, 2]
        used_mids = sorted({source for source, _ in mid_of.values()})
        inner = [own(row, used_mids, used) for row in range(rows)]
        mixed_inner = []
        for k, part in enumerate(parts):
            chosen = [halos[0], halos[1], halos[2 + k]]
            sources = [mids[s] for s in used_mids] + [pair[side] for side in (0, 1) for pair in chosen]
            mixed_inner.append(
                convolve(quad, tables, factors[layer], sources, inner, [(0, rows - 2 * rim)], part)
            )
        weights = (gains[layer], input_weight[layer], output_weight[layer])
        count = rows // 2
        if final:
            (out,) = mlp(*weights, mixed_outer, [([0], 0), ([1], rows - 2)], rows, 0)
            steps = [([p, p + 1], 2 * p + rim) for p in range(0, count - 2, 2)]
            (out,) = mlp(*weights, mixed_inner, steps, rows, 0, kept=out)
        else:
            outs = [mlp(*weights, mixed_outer, [([0], 0), ([1], 2)], 2 * rim, edge, [channels])]
            outs.append(mlp(*weights, mixed_inner, [([0], 0), ([count - 3], 2)], 2 * rim, edge, [channels]))
            steps = [([p + 1], 2 * p) for p in range(count - 4)]
            outs.append(mlp(*weights, mixed_inner, steps, rows - 4 * rim, edge, cuts))
            mids = [o[0] for o in outs]
            mid_of = group_of
            firsts = [f for o in outs for f in o[1::2]]
            lasts = [b for o in outs for b in o[2::2]]
    return jnp.swapaxes(out, 1, 2)[None]


def solution(mesh):
    in_specs = (P(None, "lat", None, "lon"), P(), P(), P(), P())
    out_specs = P(None, "lat", None, "lon")
    return jax.shard_map(body, mesh=mesh, in_specs=in_specs, out_specs=out_specs, check_vma=False)
```

```python
import functools
import math

import jax
import jax.numpy as jnp
import numpy as np
from jax import lax
from jax.experimental import pallas as pl
from jax.experimental.pallas import tpu as pltpu
from jax.sharding import PartitionSpec as P


LANES = 128
PACK = 16
SUBLANES = 8


def bases(width, taps):
    length = -(-(width + taps) // (2 * PACK)) * 2 * PACK
    odd = 2 * np.arange(length // 2) + 1

    def wave(points):
        angle = np.pi / length * (points[:, None] * odd[None, :] % (2 * length))
        return np.concatenate([np.cos(angle), -np.sin(angle)], axis=1)

    forward = wave(np.arange(width + taps)).T
    inverse = 2.0 / length * wave(taps + np.arange(width))
    tap_basis = wave(np.arange(taps)).T
    return tuple(jnp.asarray(a, jnp.bfloat16) for a in (forward, inverse, tap_basis))


def gelu(values):
    return 0.5 * values * (1.0 + lax.erf(values * math.sqrt(0.5)))


def conv_kernel(*refs, windows, row_refs, counts, begin, lanes):
    quad, forward, inverse, factors = refs[:4]
    sources = refs[4 : 4 + counts]
    out, spectra, product = refs[4 + counts :]
    step = pl.program_id(0)
    part = out.shape[2]

    def block_of(ref):
        offset = 0 if ref.shape[2] == part else begin
        return pl.ds(pl.multiple_of((step + offset) * lanes, lanes), lanes)

    ours = [block_of(ref) for ref in sources]
    freqs = forward.shape[0] // 2
    every = len(row_refs)
    taps_r = factors.shape[0]

    def row(g):
        return jnp.concatenate([sources[s][at, lon, ours[s]] for s, at, lon in row_refs[g][1]], axis=0)

    for g in range(0, every, 2):
        two = jnp.concatenate([row(g), row(g + 1)], axis=1)
        result = jnp.dot(forward[...], two, preferred_element_type=jnp.float32)
        for j in range(2):
            spectra[g + j] = result[:, j * lanes : (j + 1) * lanes] * quad[row_refs[g + j][0]]

    def block(f, carry):
        start = pl.multiple_of(f * SUBLANES, SUBLANES)
        re = pl.ds(start, SUBLANES)
        im = pl.ds(pl.multiple_of(freqs + start, SUBLANES), SUBLANES)
        fr = [factors[r, re] for r in range(taps_r)]
        fi = [factors[r, im] for r in range(taps_r)]
        fd = [b - a for a, b in zip(fr, fi)]
        fs = [b + a for a, b in zip(fr, fi)]
        h = 0
        for first, count in windows:
            xr = [spectra[first + g, re] for g in range(taps_r - 1)]
            xi = [spectra[first + g, im] for g in range(taps_r - 1)]
            xs = [a + b for a, b in zip(xr, xi)]
            for k in range(count):
                xr.append(spectra[first + k + taps_r - 1, re])
                xi.append(spectra[first + k + taps_r - 1, im])
                xs.append(xr[-1] + xi[-1])
                both, up, down = xs[0] * fr[0], xr[0] * fd[0], xi[0] * fs[0]
                for r in range(1, taps_r):
                    both, up, down = both + xs[r] * fr[r], up + xr[r] * fd[r], down + xi[r] * fs[r]
                here = slice(h * lanes, (h + 1) * lanes)
                product[re, here] = both - down
                product[im, here] = both + up
                for window in (xr, xi, xs):
                    window.pop(0)
                h += 1
        return carry

    lax.fori_loop(0, freqs // SUBLANES, block, 0, unroll=4)
    own = [row_refs[first + taps_r // 2 + k][1] for first, count in windows for k in range(count)]
    for h in range(0, len(own), 2):
        two = slice(h * lanes, (h + 2) * lanes)
        conv = jnp.dot(inverse[...], product[:, two].astype(jnp.bfloat16), preferred_element_type=jnp.float32)
        for j in range(2):
            source, at, _ = own[h + j][1]
            value = sources[source][at, :, ours[source]].astype(jnp.float32)
            out[h + j, :, block_of(out)] = (value + gelu(conv[:, j * lanes : (j + 1) * lanes])).astype(out.dtype)


def convolve(quad, tables, factors, sources, rows, windows, part):
    forward, inverse = tables
    taps_r, length, _ = factors.shape
    start, blocks = part
    out_rows = sum(count for _, count in windows)
    width = inverse.shape[0]
    lanes = blocks * LANES

    held = pl.BlockSpec(memory_space=pltpu.VMEM)
    out = jax.ShapeDtypeStruct((out_rows, width, lanes), jnp.bfloat16)
    kernel = functools.partial(
        conv_kernel, windows=windows, row_refs=rows, counts=len(sources), begin=start, lanes=LANES
    )
    return pl.pallas_call(
        kernel,
        grid=(blocks,),
        out_shape=out,
        in_specs=[
            pl.BlockSpec(memory_space=pltpu.SMEM),
            held,
            held,
            pl.BlockSpec((taps_r, length, LANES), lambda i: (0, 0, i + start)),
        ]
        + [held] * len(sources),
        out_specs=held,
        scratch_shapes=[
            pltpu.VMEM((len(rows), length, LANES), jnp.float32),
            pltpu.VMEM((length, out_rows * LANES), jnp.float32),
        ],
        compiler_params=pltpu.CompilerParams(vmem_limit_bytes=20 << 20),
        cost_estimate=pl.CostEstimate(
            flops=2 * lanes * length * (len(rows) * forward.shape[1] + out_rows * width),
            bytes_accessed=2 * lanes * (len(rows) * forward.shape[1] + 2 * taps_r * length),
            transcendentals=out_rows * lanes * width,
        ),
        name="zonal_conv",
    )(quad, forward, inverse, factors, *sources)


def mlp_kernel(gain, w_in, w_out, *refs, half, kept, parts, together):
    mixed = refs[: parts * together]
    given = refs[parts * together + kept :]
    count, width, _ = mixed[0].shape
    channels = w_in.shape[0]

    def load(t):
        pieces = mixed[t * parts : (t + 1) * parts]
        values = [m[...].reshape(count * width, m.shape[2]).astype(jnp.float32) for m in pieces]
        values = values[0] if parts == 1 else jnp.concatenate(values, axis=1)
        average = jnp.mean(values, axis=1, keepdims=True)
        centred = values - average
        variance = jnp.mean(jnp.square(centred), axis=1, keepdims=True)
        return values, (centred * lax.rsqrt(variance + 1e-05) * gain[...]).astype(jnp.bfloat16)

    following = load(0)
    for t in range(together):
        values, normed = following
        hidden = jnp.dot(normed, w_in[...], preferred_element_type=jnp.float32)
        hidden = gelu(hidden).astype(jnp.bfloat16)
        if t + 1 < together:
            following = load(t + 1)
        result = values + jnp.dot(hidden, w_out[...], preferred_element_type=jnp.float32)
        result = result.astype(jnp.bfloat16).reshape(count, width, channels)
        here = slice(t * count, (t + 1) * count)
        given[0][here] = result
        start = 0
        for first, last in zip(given[1::2], given[2::2]):
            cut = slice(start, start + first.shape[2])
            first[here] = result[:, :half, cut]
            last[here] = result[:, width - half :, cut]
            start += first.shape[2]


def mlp(gain, w_in, w_out, mixed, steps, out_rows, edge, cuts=(), kept=None):
    width = mixed[0].shape[1]
    channels, hidden_units = w_in.shape
    together = len(steps[0][0])

    def chosen(values):
        def index(i):
            at = values[0]
            for k in range(1, len(values)):
                at = at + (values[k] - values[k - 1]) * (i >= k).astype(jnp.int32)
            return (at, 0, 0)

        return index

    def whole(array):
        return pl.BlockSpec(array.shape, lambda i: (0,) * array.ndim)

    def given(lon, lanes):
        sizes = (pl.Element(2 * together), pl.Element(lon), pl.Element(lanes))
        return pl.BlockSpec(sizes, chosen([row for _, row in steps]))

    lasts = [(width, channels)] + [(edge, cut) for cut in cuts for _ in range(2)]
    extra = [] if kept is None else [kept]
    return pl.pallas_call(
        functools.partial(mlp_kernel, half=edge, kept=len(extra), parts=len(mixed), together=together),
        grid=(len(steps),),
        out_shape=[jax.ShapeDtypeStruct((out_rows, *last), jnp.bfloat16) for last in lasts],
        in_specs=[whole(gain), whole(w_in), whole(w_out)]
        + [
            pl.BlockSpec((2, *m.shape[1:]), chosen([pairs[t] for pairs, _ in steps]))
            for t in range(together)
            for m in mixed
        ]
        + [pl.BlockSpec(memory_space=pl.ANY) for _ in extra],
        out_specs=[given(*last) for last in lasts],
        input_output_aliases={3 + together * len(mixed): 0} if extra else {},
        compiler_params=pltpu.CompilerParams(vmem_limit_bytes=20 << 20),
        cost_estimate=pl.CostEstimate(
            flops=8 * len(steps) * together * width * channels * hidden_units,
            bytes_accessed=8 * len(steps) * together * width * channels + 4 * channels * hidden_units,
            transcendentals=2 * len(steps) * together * width * hidden_units,
        ),
        name="channel_mlp",
    )(gain, w_in, w_out, *(list(mixed) * together), *extra)


def rotate(block, axis, hops):
    count = lax.axis_size(axis)
    return lax.ppermute(block, axis, [(i, (i + hops) % count) for i in range(count)])


def zonal_halos(first, last, half):
    width = first.shape[1]
    lefts, rights, hops, missing = [], [], 1, half
    while missing > 0:
        take = min(width, missing)
        lefts.insert(0, rotate(last[:, width - take :], "lon", hops))
        rights.append(rotate(first[:, :take], "lon", -hops))
        missing -= take
        hops += 1
    if len(lefts) == 1:
        return lefts[0], rights[0]
    return jnp.concatenate(lefts, axis=1), jnp.concatenate(rights, axis=1)


def step_rows(block, hops):
    count = lax.axis_size("lat")
    pairs = [(i, i + hops) for i in range(count) if 0 <= i + hops < count]
    return lax.ppermute(block, "lat", pairs)


def lane_parts(channels):
    units = channels // LANES
    least = max(1, units // 5)
    sizes = [(units - least + 1) // 2, (units - least) // 2, least]
    return [(sum(sizes[:k]), size) for k, size in enumerate(sizes) if size]


def body(ocean_state, zonal_kernel, norm_gain, input_weight, output_weight):
    blocks, kernel_rows, taps, channels = zonal_kernel.shape
    _, rows, _, width = ocean_state.shape
    rim = kernel_rows // 2
    half = taps // 2
    edge = min(half, width)
    forward, inverse, tap_basis = bases(width, taps)
    total_rows = rows * lax.axis_size("lat")
    index = lax.axis_index("lat") * rows - rim + jnp.arange(rows + 2 * rim, dtype=jnp.int32)
    quad = jnp.sin(jnp.pi * (index.astype(jnp.float32) + 0.5) / total_rows)
    quad = jnp.where((index >= 0) & (index < total_rows), quad, 0.0)
    factors = []
    for layer in range(blocks):
        taps_of = zonal_kernel[layer]
        factors.append(jnp.einsum("kt,rtc->rkc", tap_basis, taps_of, preferred_element_type=jnp.float32))
    gains = norm_gain.astype(jnp.float32)[:, None, :]

    groups = [
        list(range(rim)) + list(range(rows - rim, rows)),
        list(range(rim, 2 * rim)) + list(range(rows - 2 * rim, rows - rim)),
        list(range(2 * rim, rows - 2 * rim)),
    ]
    group_of = {row: (k, at) for k, members in enumerate(groups) for at, row in enumerate(members)}
    state = jnp.swapaxes(ocean_state[0], 1, 2)
    mids = [state]
    mid_of = {row: (0, row) for row in range(rows)}

    pairs = state.reshape(rows // rim, rim, width, channels)

    def pick(pairs, members, lon, cut):
        first, last = members[0] // rim, members[-1] // rim
        stride = max(1, (last - first) // (len(members) // rim - 1))
        low, high = (first, 0, lon.start, cut.start), (last + 1, rim, lon.stop, cut.stop)
        chosen = lax.slice(pairs, low, high, (stride, 1, 1, 1))
        return chosen.reshape(len(members), *chosen.shape[2:])

    parts = lane_parts(channels)
    pieces = [slice(start * LANES, (start + count) * LANES) for start, count in parts]
    cuts = [count * LANES for _, count in parts]
    lanes = [slice(0, channels)] * 2 + pieces
    groups_of = [groups[0], groups[1]] + [groups[2]] * len(parts)
    head, tail = slice(0, edge), slice(width - edge, width)
    firsts, lasts = [None] * len(lanes), [None] * len(lanes)
    for k in [len(lanes) - 1] + list(range(len(lanes) - 1)):
        for edges, lon in ((lasts, tail), (firsts, head)):
            edges[k] = pick(pairs, groups_of[k], lon, lanes[k])
            if k in (0, len(lanes) - 1):
                pairs, _ = lax.optimization_barrier((pairs, edges[k]))
    tables = (forward, inverse)
    out = None
    for layer in range(blocks):
        final = layer + 1 == blocks
        halos = [zonal_halos(f, b, half) for f, b in zip(firsts, lasts)]

        def near(start):
            source, row = mid_of[start]
            return mids[source][row : row + rim]

        def far(start):
            at = group_of[start][1]
            return jnp.concatenate([halo[at : at + rim] for halo in halos[0]], axis=1)

        low = [step_rows(near(rows - rim), 1), step_rows(far(rows - rim), 1)]
        high = [step_rows(near(0), -1), step_rows(far(0), -1)]

        def own(row, used_mids, used):
            k, at = group_of[row]
            source, mid_row = mid_of[row]
            n = len(used_mids)
            j = used.index(k)
            every = slice(None)
            middle = (used_mids.index(source), mid_row, every)
            return (row + rim, [(n + j, at, every), middle, (n + len(used) + j, at, every)])

        def lat(number, at, place):
            return (
                place,
                [
                    (number + 1, at, slice(0, half)),
                    (number, at, slice(None)),
                    (number + 1, at, slice(half, 2 * half)),
                ],
            )

        used = [0, 1]
        used_mids = sorted({mid_of[row][0] for k in used for row in groups[k]})
        sources = [mids[s] for s in used_mids] + [halos[k][side] for side in (0, 1) for k in used]
        sources = sources + low + high
        n = len(sources)
        outer = (
            [lat(n - 4, r, r) for r in range(rim)]
            + [own(row, used_mids, used) for row in range(2 * rim)]
            + [own(row, used_mids, used) for row in range(rows - 2 * rim, rows)]
            + [lat(n - 2, r, rows + rim + r) for r in range(rim)]
        )
        windows = [(0, rim), (3 * rim, rim)]
        mixed_outer = [
            convolve(quad, tables, factors[layer], sources, outer, windows, (0, channels // LANES))
        ]
        used = [0, 1, 2]
        used_mids = sorted({source for source, _ in mid_of.values()})
        inner = [own(row, used_mids, used) for row in range(rows)]
        mixed_inner = []
        for k, part in enumerate(parts):
            chosen = [halos[0], halos[1], halos[2 + k]]
            sources = [mids[s] for s in used_mids] + [pair[side] for side in (0, 1) for pair in chosen]
            mixed_inner.append(
                convolve(quad, tables, factors[layer], sources, inner, [(0, rows - 2 * rim)], part)
            )
        weights = (gains[layer], input_weight[layer], output_weight[layer])
        count = rows // 2
        if final:
            (out,) = mlp(*weights, mixed_outer, [([0], 0), ([1], rows - 2)], rows, 0)
            steps = [([p, p + 1], 2 * p + rim) for p in range(0, count - 2, 2)]
            (out,) = mlp(*weights, mixed_inner, steps, rows, 0, kept=out)
        else:
            outs = [mlp(*weights, mixed_outer, [([0], 0), ([1], 2)], 2 * rim, edge, [channels])]
            outs.append(mlp(*weights, mixed_inner, [([0], 0), ([count - 3], 2)], 2 * rim, edge, [channels]))
            steps = [([p + 1], 2 * p) for p in range(count - 4)]
            outs.append(mlp(*weights, mixed_inner, steps, rows - 4 * rim, edge, cuts))
            mids = [o[0] for o in outs]
            mid_of = group_of
            firsts = [f for o in outs for f in o[1::2]]
            lasts = [b for o in outs for b in o[2::2]]
    return jnp.swapaxes(out, 1, 2)[None]


def solution(mesh):
    in_specs = (P(None, "lat", None, "lon"), P(), P(), P(), P())
    out_specs = P(None, "lat", None, "lon")
    return jax.shard_map(body, mesh=mesh, in_specs=in_specs, out_specs=out_specs, check_vma=False)
```

```python
import functools
import math

import jax
import jax.numpy as jnp
import numpy as np
from jax import lax
from jax.experimental import pallas as pl
from jax.experimental.pallas import tpu as pltpu
from jax.sharding import PartitionSpec as P


LANES = 128
PACK = 16
SUBLANES = 8


def bases(width, taps):
    length = -(-(width + taps) // (2 * PACK)) * 2 * PACK
    odd = 2 * np.arange(length // 2) + 1

    def wave(points):
        angle = np.pi / length * (points[:, None] * odd[None, :] % (2 * length))
        return np.concatenate([np.cos(angle), -np.sin(angle)], axis=1)

    forward = wave(np.arange(width + taps)).T
    inverse = 2.0 / length * wave(taps + np.arange(width))
    tap_basis = wave(np.arange(taps)).T
    return tuple(jnp.asarray(a, jnp.bfloat16) for a in (forward, inverse, tap_basis))


def gelu(values):
    return 0.5 * values * (1.0 + lax.erf(values * math.sqrt(0.5)))


def conv_kernel(*refs, windows, row_refs, counts, begin, lanes):
    quad, forward, inverse, factors = refs[:4]
    sources = refs[4 : 4 + counts]
    out, spectra, product = refs[4 + counts :]
    step = pl.program_id(0)
    part = out.shape[2]

    def block_of(ref):
        offset = 0 if ref.shape[2] == part else begin
        if part == lanes:
            return slice(offset * lanes, (offset + 1) * lanes)
        return pl.ds(pl.multiple_of((step + offset) * lanes, lanes), lanes)

    ours = [block_of(ref) for ref in sources]
    its = block_of(factors) if part == lanes else slice(None)
    freqs = forward.shape[0] // 2
    every = len(row_refs)
    taps_r = factors.shape[0]

    def row(g):
        return jnp.concatenate([sources[s][at, lon, ours[s]] for s, at, lon in row_refs[g][1]], axis=0)

    for g in range(0, every, 2):
        two = jnp.concatenate([row(g), row(g + 1)], axis=1)
        result = jnp.dot(forward[...], two, preferred_element_type=jnp.float32)
        for j in range(2):
            spectra[g + j] = result[:, j * lanes : (j + 1) * lanes] * quad[row_refs[g + j][0]]

    def block(f, carry):
        start = pl.multiple_of(f * SUBLANES, SUBLANES)
        re = pl.ds(start, SUBLANES)
        im = pl.ds(pl.multiple_of(freqs + start, SUBLANES), SUBLANES)
        fr = [factors[r, re, its] for r in range(taps_r)]
        fi = [factors[r, im, its] for r in range(taps_r)]
        fd = [b - a for a, b in zip(fr, fi)]
        fs = [b + a for a, b in zip(fr, fi)]
        h = 0
        for first, count in windows:
            xr = [spectra[first + g, re] for g in range(taps_r - 1)]
            xi = [spectra[first + g, im] for g in range(taps_r - 1)]
            xs = [a + b for a, b in zip(xr, xi)]
            for k in range(count):
                xr.append(spectra[first + k + taps_r - 1, re])
                xi.append(spectra[first + k + taps_r - 1, im])
                xs.append(xr[-1] + xi[-1])
                both, up, down = xs[0] * fr[0], xr[0] * fd[0], xi[0] * fs[0]
                for r in range(1, taps_r):
                    both, up, down = both + xs[r] * fr[r], up + xr[r] * fd[r], down + xi[r] * fs[r]
                here = slice(h * lanes, (h + 1) * lanes)
                product[re, here] = both - down
                product[im, here] = both + up
                for window in (xr, xi, xs):
                    window.pop(0)
                h += 1
        return carry

    lax.fori_loop(0, freqs // SUBLANES, block, 0, unroll=4)
    own = [row_refs[first + taps_r // 2 + k][1] for first, count in windows for k in range(count)]
    for h in range(0, len(own), 2):
        two = slice(h * lanes, (h + 2) * lanes)
        conv = jnp.dot(inverse[...], product[:, two].astype(jnp.bfloat16), preferred_element_type=jnp.float32)
        for j in range(2):
            source, at, _ = own[h + j][1]
            value = sources[source][at, :, ours[source]].astype(jnp.float32)
            out[h + j, :, block_of(out)] = (value + gelu(conv[:, j * lanes : (j + 1) * lanes])).astype(out.dtype)


def convolve(quad, tables, factors, sources, rows, windows, part):
    forward, inverse = tables
    taps_r, length, _ = factors.shape
    start, blocks = part
    out_rows = sum(count for _, count in windows)
    width = inverse.shape[0]
    lanes = blocks * LANES

    held = pl.BlockSpec(memory_space=pltpu.VMEM)
    out = jax.ShapeDtypeStruct((out_rows, width, lanes), jnp.bfloat16)
    kernel = functools.partial(
        conv_kernel, windows=windows, row_refs=rows, counts=len(sources), begin=start, lanes=LANES
    )
    return pl.pallas_call(
        kernel,
        grid=(blocks,),
        out_shape=out,
        in_specs=[
            pl.BlockSpec(memory_space=pltpu.SMEM),
            held,
            held,
            held if blocks == 1 else pl.BlockSpec((taps_r, length, LANES), lambda i: (0, 0, i + start)),
        ]
        + [held] * len(sources),
        out_specs=held,
        scratch_shapes=[
            pltpu.VMEM((len(rows), length, LANES), jnp.float32),
            pltpu.VMEM((length, out_rows * LANES), jnp.float32),
        ],
        compiler_params=pltpu.CompilerParams(vmem_limit_bytes=20 << 20),
        cost_estimate=pl.CostEstimate(
            flops=2 * lanes * length * (len(rows) * forward.shape[1] + out_rows * width),
            bytes_accessed=2 * lanes * (len(rows) * forward.shape[1] + 2 * taps_r * length),
            transcendentals=out_rows * lanes * width,
        ),
        name="zonal_conv",
    )(quad, forward, inverse, factors, *sources)


def mlp_kernel(gain, w_in, w_out, *refs, half, kept, parts, together):
    mixed = refs[: parts * together]
    given = refs[parts * together + kept :]
    count, width, _ = mixed[0].shape
    channels = w_in.shape[0]

    def load(t):
        pieces = mixed[t * parts : (t + 1) * parts]
        values = [m[...].reshape(count * width, m.shape[2]).astype(jnp.float32) for m in pieces]
        values = values[0] if parts == 1 else jnp.concatenate(values, axis=1)
        average = jnp.mean(values, axis=1, keepdims=True)
        centred = values - average
        variance = jnp.mean(jnp.square(centred), axis=1, keepdims=True)
        return values, (centred * lax.rsqrt(variance + 1e-05) * gain[...]).astype(jnp.bfloat16)

    following = load(0)
    for t in range(together):
        values, normed = following
        hidden = jnp.dot(normed, w_in[...], preferred_element_type=jnp.float32)
        hidden = gelu(hidden).astype(jnp.bfloat16)
        if t + 1 < together:
            following = load(t + 1)
        result = values + jnp.dot(hidden, w_out[...], preferred_element_type=jnp.float32)
        result = result.astype(jnp.bfloat16).reshape(count, width, channels)
        here = slice(t * count, (t + 1) * count)
        given[0][here] = result
        start = 0
        for first, last in zip(given[1::2], given[2::2]):
            cut = slice(start, start + first.shape[2])
            first[here] = result[:, :half, cut]
            last[here] = result[:, width - half :, cut]
            start += first.shape[2]


def mlp(gain, w_in, w_out, mixed, steps, out_rows, edge, cuts=(), kept=None):
    width = mixed[0].shape[1]
    channels, hidden_units = w_in.shape
    together = len(steps[0][0])

    def chosen(values):
        def index(i):
            at = values[0]
            for k in range(1, len(values)):
                at = at + (values[k] - values[k - 1]) * (i >= k).astype(jnp.int32)
            return (at, 0, 0)

        return index

    def whole(array):
        return pl.BlockSpec(array.shape, lambda i: (0,) * array.ndim)

    def given(lon, lanes):
        sizes = (pl.Element(2 * together), pl.Element(lon), pl.Element(lanes))
        return pl.BlockSpec(sizes, chosen([row for _, row in steps]))

    lasts = [(width, channels)] + [(edge, cut) for cut in cuts for _ in range(2)]
    extra = [] if kept is None else [kept]
    return pl.pallas_call(
        functools.partial(mlp_kernel, half=edge, kept=len(extra), parts=len(mixed), together=together),
        grid=(len(steps),),
        out_shape=[jax.ShapeDtypeStruct((out_rows, *last), jnp.bfloat16) for last in lasts],
        in_specs=[whole(gain), whole(w_in), whole(w_out)]
        + [
            pl.BlockSpec((2, *m.shape[1:]), chosen([pairs[t] for pairs, _ in steps]))
            for t in range(together)
            for m in mixed
        ]
        + [pl.BlockSpec(memory_space=pl.ANY) for _ in extra],
        out_specs=[given(*last) for last in lasts],
        input_output_aliases={3 + together * len(mixed): 0} if extra else {},
        compiler_params=pltpu.CompilerParams(vmem_limit_bytes=20 << 20),
        cost_estimate=pl.CostEstimate(
            flops=8 * len(steps) * together * width * channels * hidden_units,
            bytes_accessed=8 * len(steps) * together * width * channels + 4 * channels * hidden_units,
            transcendentals=2 * len(steps) * together * width * hidden_units,
        ),
        name="channel_mlp",
    )(gain, w_in, w_out, *(list(mixed) * together), *extra)


def rotate(block, axis, hops):
    count = lax.axis_size(axis)
    return lax.ppermute(block, axis, [(i, (i + hops) % count) for i in range(count)])


def zonal_halos(first, last, half):
    width = first.shape[1]
    lefts, rights, hops, missing = [], [], 1, half
    while missing > 0:
        take = min(width, missing)
        lefts.insert(0, rotate(last[:, width - take :], "lon", hops))
        rights.append(rotate(first[:, :take], "lon", -hops))
        missing -= take
        hops += 1
    if len(lefts) == 1:
        return lefts[0], rights[0]
    return jnp.concatenate(lefts, axis=1), jnp.concatenate(rights, axis=1)


def step_rows(block, hops):
    count = lax.axis_size("lat")
    pairs = [(i, i + hops) for i in range(count) if 0 <= i + hops < count]
    return lax.ppermute(block, "lat", pairs)


def lane_parts(channels):
    units = channels // LANES
    least = max(1, units // 5)
    sizes = [(units - least + 1) // 2, (units - least) // 2, least]
    return [(sum(sizes[:k]), size) for k, size in enumerate(sizes) if size]


def body(ocean_state, zonal_kernel, norm_gain, input_weight, output_weight):
    blocks, kernel_rows, taps, channels = zonal_kernel.shape
    _, rows, _, width = ocean_state.shape
    rim = kernel_rows // 2
    half = taps // 2
    edge = min(half, width)
    forward, inverse, tap_basis = bases(width, taps)
    total_rows = rows * lax.axis_size("lat")
    index = lax.axis_index("lat") * rows - rim + jnp.arange(rows + 2 * rim, dtype=jnp.int32)
    quad = jnp.sin(jnp.pi * (index.astype(jnp.float32) + 0.5) / total_rows)
    quad = jnp.where((index >= 0) & (index < total_rows), quad, 0.0)
    factors = []
    for layer in range(blocks):
        taps_of = zonal_kernel[layer]
        factors.append(jnp.einsum("kt,rtc->rkc", tap_basis, taps_of, preferred_element_type=jnp.float32))
    gains = norm_gain.astype(jnp.float32)[:, None, :]

    groups = [
        list(range(rim)) + list(range(rows - rim, rows)),
        list(range(rim, 2 * rim)) + list(range(rows - 2 * rim, rows - rim)),
        list(range(2 * rim, rows - 2 * rim)),
    ]
    group_of = {row: (k, at) for k, members in enumerate(groups) for at, row in enumerate(members)}
    state = jnp.swapaxes(ocean_state[0], 1, 2)
    mids = [state]
    mid_of = {row: (0, row) for row in range(rows)}

    pairs = state.reshape(rows // rim, rim, width, channels)

    def pick(pairs, members, lon, cut):
        first, last = members[0] // rim, members[-1] // rim
        stride = max(1, (last - first) // (len(members) // rim - 1))
        low, high = (first, 0, lon.start, cut.start), (last + 1, rim, lon.stop, cut.stop)
        chosen = lax.slice(pairs, low, high, (stride, 1, 1, 1))
        return chosen.reshape(len(members), *chosen.shape[2:])

    parts = lane_parts(channels)
    pieces = [slice(start * LANES, (start + count) * LANES) for start, count in parts]
    cuts = [count * LANES for _, count in parts]
    lanes = [slice(0, channels)] * 2 + pieces
    groups_of = [groups[0], groups[1]] + [groups[2]] * len(parts)
    head, tail = slice(0, edge), slice(width - edge, width)
    lasts = [pick(pairs, groups[0], tail, lanes[0])]
    pairs, _ = lax.optimization_barrier((pairs, lasts[0]))
    firsts = [pick(pairs, groups[0], head, lanes[0])]
    pairs, _ = lax.optimization_barrier((pairs, firsts[0]))
    firsts += [pick(pairs, members, head, cut) for members, cut in zip(groups_of[1:], lanes[1:])]
    lasts += [pick(pairs, members, tail, cut) for members, cut in zip(groups_of[1:], lanes[1:])]
    tables = (forward, inverse)
    out = None
    for layer in range(blocks):
        final = layer + 1 == blocks
        halos = [zonal_halos(f, b, half) for f, b in zip(firsts, lasts)]

        def near(start):
            source, row = mid_of[start]
            return mids[source][row : row + rim]

        def far(start):
            at = group_of[start][1]
            return jnp.concatenate([halo[at : at + rim] for halo in halos[0]], axis=1)

        low = [step_rows(near(rows - rim), 1), step_rows(far(rows - rim), 1)]
        high = [step_rows(near(0), -1), step_rows(far(0), -1)]

        def own(row, used_mids, used):
            k, at = group_of[row]
            source, mid_row = mid_of[row]
            n = len(used_mids)
            j = used.index(k)
            every = slice(None)
            middle = (used_mids.index(source), mid_row, every)
            return (row + rim, [(n + j, at, every), middle, (n + len(used) + j, at, every)])

        def lat(number, at, place):
            return (
                place,
                [
                    (number + 1, at, slice(0, half)),
                    (number, at, slice(None)),
                    (number + 1, at, slice(half, 2 * half)),
                ],
            )

        used = [0, 1]
        used_mids = sorted({mid_of[row][0] for k in used for row in groups[k]})
        sources = [mids[s] for s in used_mids] + [halos[k][side] for side in (0, 1) for k in used]
        sources = sources + low + high
        n = len(sources)
        outer = (
            [lat(n - 4, r, r) for r in range(rim)]
            + [own(row, used_mids, used) for row in range(2 * rim)]
            + [own(row, used_mids, used) for row in range(rows - 2 * rim, rows)]
            + [lat(n - 2, r, rows + rim + r) for r in range(rim)]
        )
        windows = [(0, rim), (3 * rim, rim)]
        mixed_outer = [
            convolve(quad, tables, factors[layer], sources, outer, windows, (0, channels // LANES))
        ]
        used = [0, 1, 2]
        used_mids = sorted({source for source, _ in mid_of.values()})
        inner = [own(row, used_mids, used) for row in range(rows)]
        mixed_inner = []
        for k, part in enumerate(parts):
            chosen = [halos[0], halos[1], halos[2 + k]]
            sources = [mids[s] for s in used_mids] + [pair[side] for side in (0, 1) for pair in chosen]
            mixed_inner.append(
                convolve(quad, tables, factors[layer], sources, inner, [(0, rows - 2 * rim)], part)
            )
        weights = (gains[layer], input_weight[layer], output_weight[layer])
        count = rows // 2
        if final:
            (out,) = mlp(*weights, mixed_outer, [([0], 0), ([1], rows - 2)], rows, 0)
            steps = [([p, p + 1], 2 * p + rim) for p in range(0, count - 2, 2)]
            (out,) = mlp(*weights, mixed_inner, steps, rows, 0, kept=out)
        else:
            outs = [mlp(*weights, mixed_outer, [([0], 0), ([1], 2)], 2 * rim, edge, [channels])]
            outs.append(mlp(*weights, mixed_inner, [([0], 0), ([count - 3], 2)], 2 * rim, edge, [channels]))
            steps = [([p + 1], 2 * p) for p in range(count - 4)]
            outs.append(mlp(*weights, mixed_inner, steps, rows - 4 * rim, edge, cuts))
            mids = [o[0] for o in outs]
            mid_of = group_of
            firsts = [f for o in outs for f in o[1::2]]
            lasts = [b for o in outs for b in o[2::2]]
    return jnp.swapaxes(out, 1, 2)[None]


def solution(mesh):
    in_specs = (P(None, "lat", None, "lon"), P(), P(), P(), P())
    out_specs = P(None, "lat", None, "lon")
    return jax.shard_map(body, mesh=mesh, in_specs=in_specs, out_specs=out_specs, check_vma=False)
```
